32 devices in a mesh: pix: 8 (over y, x, core), tm: 4 (over z).
Axes of the slice: x: 2, y: 2, z: 4, core: 2. Of those that a mesh axis runs over, the one named last changes fastest.
Arguments:
- raw_movie: float32 [64, 256, 2048], P('pix', None, 'tm'), may hold values from 0.05 to 2
- footprints: float32 [256, 16384], P('tm', 'pix'), may hold values from 0.05 to 1
- traces: float32 [256, 2048], P('pix', 'tm'), may hold values from 0.05 to 1
Outputs:
- denoised: float32 [64, 256, 2048], P('pix', None, 'tm')
- new_footprints: float32 [256, 16384], P('tm', 'pix')
- new_traces: float32 [256, 2048], P('pix', 'tm')
The draws below stay inside these ranges and needn't reach their ends.
All inputs are finite; a program needn't handle non-finite values.
Results may differ from the reference program's by a relative error of at most 0.00013.
Values sent between devices are 32-bit elements; how exact they have to be, the bound alone decides.
No kernel may reach another device: no remote copies, remote signals or barrier semaphores. Data moves between devices by JAX's collectives and lax.ppermute only.
A program may use at most 64 MiB of HBM per device.

```python
import math
import jax
import jax.numpy as jnp
from jax import lax

WID = 256
FR_DEV = 512
RANK = 256
HGT = 64
PIXELS = 16384
FRAMES = 2048
N_TM = 4


def block_scale(key, dims, cuts, least, largest):
    def one(position, shards_of):
        draws = jax.random.uniform(jax.random.fold_in(jax.random.fold_in(key, 6), position), (shards_of,), jnp.float32, least / len(cuts), largest / len(cuts))
        return jnp.repeat(jnp.exp(draws), dims[position] // shards_of).reshape((-1,) + (1,) * (len(dims) - position - 1))

    loudness = one(*cuts[0])
    for cut in cuts[1:]:
        loudness = loudness * one(*cut)
    return loudness


def setup_inputs(seed: int = 0) -> dict:
    keys = jax.random.split(jax.random.key(seed), 4)
    raw_movie = jnp.clip(jnp.exp(math.log(2.0) - 3.6888794 * jax.random.uniform(keys[0], (HGT, WID, FRAMES), jnp.float32) ** block_scale(keys[0], (HGT, WID, FRAMES), ((0, 8), (2, 4)), -0.2, 0.2)), 0.05, 2.0)
    footprints = jnp.clip(jnp.exp(math.log(1.0) - 2.9957323 * jax.random.uniform(keys[1], (RANK, PIXELS), jnp.float32) ** block_scale(keys[1], (RANK, PIXELS), ((0, 4), (1, 8)), -0.2, 0.2)), 0.05, 1.0)
    traces = jnp.clip(jnp.exp(math.log(1.0) - 2.9957323 * jax.random.uniform(keys[2], (RANK, FRAMES), jnp.float32) ** block_scale(keys[2], (RANK, FRAMES), ((0, 8), (1, 4)), -0.2, 0.2)), 0.05, 1.0)
    return {"raw_movie": raw_movie, "footprints": footprints, "traces": traces}


edge_scale = 0.5
step_size = 0.24


def flux_term(change):
    return change / (1.0 + (change / edge_scale) * (change / edge_scale))


def substep(extended):
    middle = extended[1:-1]
    padded = jnp.pad(middle, ((0, 0), (1, 1), (0, 0)))
    summed = flux_term(extended[:-2] - middle) + flux_term(extended[2:] - middle)
    summed = summed + flux_term(padded[:, :-2] - middle) + flux_term(padded[:, 2:] - middle)
    return middle + step_size * summed


def diffuse(frames_block):
    current = frames_block
    for repeat in range(4):
        current = substep(jnp.pad(current, ((1, 1), (0, 0), (0, 0))))
    return current


def matmul_hi(left, right):
    return jnp.dot(left, right, precision=lax.Precision.HIGHEST, preferred_element_type=jnp.float32)


def contract_last(left, right):
    return lax.dot_general(left, right, (((1,), (1,)), ((), ())), precision=lax.Precision.HIGHEST, preferred_element_type=jnp.float32)


def reference(raw_movie, footprints, traces):
    stacked = jnp.moveaxis(raw_movie.reshape(HGT, WID, N_TM, FR_DEV), 2, 0)
    denoised = jnp.moveaxis(lax.map(diffuse, stacked), 0, 2).reshape(HGT, WID, FRAMES)
    pixels = denoised.reshape(HGT * WID, FRAMES)
    numerator = matmul_hi(footprints, pixels)
    gram = contract_last(footprints, footprints)
    new_traces = traces * numerator / matmul_hi(gram, traces)
    foot_numerator = contract_last(new_traces, pixels)
    trace_gram = contract_last(new_traces, new_traces)
    new_footprints = footprints * foot_numerator / matmul_hi(trace_gram, footprints)
    return denoised, new_footprints, new_traces
```

```python
import jax
import jax.numpy as jnp
from jax import lax
from jax.experimental import pallas as pl
from jax.experimental.pallas import tpu as pltpu
from jax.sharding import PartitionSpec as P


edge_square = 0.25
step_scale = 0.06
SUBSTEPS = 4
LANES = 128
CHUNKS = 2


def flux_quarter(change):
    return change / (change * change + edge_square)


def split(value):
    high = value.astype(jnp.bfloat16)
    low = (value - high.astype(jnp.float32)).astype(jnp.bfloat16)
    return high, low


def dot3(left, right, dims):
    def one(a, b):
        return lax.dot_general(a, b, (dims, ((), ())), preferred_element_type=jnp.float32)

    return one(left[0], right[0]) + (one(left[0], right[1]) + one(left[1], right[0]))


NN = ((1,), (0,))
NT = ((1,), (1,))


def diffuse_call(flags, raw, halo_up, halo_down, detour, carried, offset, frames):
    rows, cols, total = raw.shape
    halo = halo_up.shape[0]
    width = 64
    pad = 8
    extended = rows + 2 * halo

    def kernel(flags, *refs):
        if detour is None:
            raw_ref, up_ref, down_ref = refs[:3]
            refs = refs[3:]
        else:
            raw_ref, up_ref, down_ref, detour_ref = refs[:4]
            refs = refs[4:]
        if carried is not None:
            refs = refs[1:]
        out_ref, high_ref, low_ref, first_buf, second_buf = refs
        zero = jnp.zeros((extended, pad, LANES), jnp.float32)
        for buf in (first_buf, second_buf):
            buf[:, 0:pad, :] = zero
            buf[:, pad + cols :, :] = zero
        inside = slice(pad, pad + cols)
        first_buf[0:halo, inside, :] = up_ref[...]
        first_buf[halo : halo + rows, inside, :] = raw_ref[...]
        first_buf[halo + rows :, inside, :] = down_ref[...]
        if detour is not None:

            @pl.when(flags[2] == 1)
            def _():
                first_buf[0:halo, inside, :] = detour_ref[...]

            @pl.when(flags[3] == 1)
            def _():
                first_buf[halo + rows :, inside, :] = detour_ref[...]

        scale_up = step_scale * flags[0].astype(jnp.float32)
        scale_down = step_scale * flags[1].astype(jnp.float32)
        head = lax.broadcasted_iota(jnp.int32, (width, LANES), 0) == 0
        bufs = (first_buf, second_buf)
        for step in range(SUBSTEPS):
            src, dst = bufs[step % 2], bufs[1 - step % 2]
            top = step
            middle = range(step + 1, extended - step - 1)

            def tile(j, left_flux):
                base = pl.multiple_of(pad + j * width, 8)
                col = pl.multiple_of(j * width, width)
                kept = []
                current = src[top + 1, pl.ds(base, width), :]
                flux_up = flux_quarter(current - src[top, pl.ds(base, width), :])
                for k, row in enumerate(middle):
                    below = src[row + 1, pl.ds(base, width), :]
                    flux_down = flux_quarter(below - current)
                    flux_right = flux_quarter(src[row, pl.ds(base + 1, width), :] - current)
                    rolled = pltpu.roll(flux_right, 1, 0)
                    flux_left = jnp.where(head, left_flux[k], rolled)
                    scale = step_scale
                    if row < halo:
                        scale = scale_up
                    if row >= halo + rows:
                        scale = scale_down
                    value = current + scale * ((flux_down - flux_up) + (flux_right - flux_left))
                    kept.append(rolled)
                    if step + 1 < SUBSTEPS:
                        dst[row, pl.ds(base, width), :] = value
                    else:
                        out_ref[row - halo, pl.ds(col, width), :] = value
                        high, low = split(value)
                        high_ref[row - halo, pl.ds(col, width), :] = high
                        low_ref[row - halo, pl.ds(col, width), :] = low
                    current, flux_up = below, flux_down
                return tuple(kept)

            edge = tuple(flux_quarter(src[row, pl.ds(pad, width), :]) for row in middle)
            lax.fori_loop(0, cols // width, tile, edge)

    base_block = offset // LANES

    def spec(count, shift):
        return pl.BlockSpec((count, cols, LANES), lambda i, flags: (0, 0, i + shift))

    operands = [flags, raw, halo_up, halo_down]
    in_specs = [spec(rows, base_block), spec(halo, 0), spec(halo, 0)]
    if detour is not None:
        operands.append(detour)
        in_specs.append(spec(halo, 0))
    aliases = {}
    if carried is not None:
        operands.append(carried)
        in_specs.append(pl.BlockSpec(memory_space=pl.ANY))
        aliases = {len(operands) - 1: 0}
    return pl.pallas_call(
        kernel,
        grid_spec=pltpu.PrefetchScalarGridSpec(
            num_scalar_prefetch=1,
            grid=(frames // LANES,),
            in_specs=in_specs,
            out_specs=[spec(rows, base_block), spec(rows, 0), spec(rows, 0)],
            scratch_shapes=[pltpu.VMEM((extended, cols + 2 * pad, LANES), jnp.float32)] * 2,
        ),
        out_shape=[
            jax.ShapeDtypeStruct((rows, cols, total), jnp.float32),
            jax.ShapeDtypeStruct((rows, cols, frames), jnp.bfloat16),
            jax.ShapeDtypeStruct((rows, cols, frames), jnp.bfloat16),
        ],
        input_output_aliases=aliases,
        cost_estimate=pl.CostEstimate(
            flops=rows * cols * frames * 100,
            bytes_accessed=rows * cols * frames * 16,
            transcendentals=rows * cols * frames * 10,
        ),
        name="diffuse",
    )(*operands)


def pick_slots(scalars, own, pairs, count):
    here = scalars[0]
    found = [own[...]]
    for s, (from_above, from_below) in enumerate(pairs, 1):
        found.append(jnp.where(here + s < count, from_above[...], from_below[...]))
    return jnp.concatenate(found, axis=0)


def numerator_call(scalars, own, pairs, high, low, with_gram):
    count = len(pairs) + 1
    rank = own.shape[0] * count
    pixel_count, frames = high.shape
    block = 512
    half = rank // 2
    steps = pixel_count // block
    columns = frames + (rank if with_gram else 0)

    def kernel(scalars, *refs):
        own_ref = refs[0]
        pair_refs = [(refs[1 + 2 * k], refs[2 + 2 * k]) for k in range(count - 1)]
        high_ref, low_ref, keep_ref, send_ref, total = refs[2 * count - 1 :]
        step = pl.program_id(0)

        @pl.when(step == 0)
        def _():
            total[...] = jnp.zeros_like(total)

        foot = split(pick_slots(scalars, own_ref, pair_refs, count))
        total[:, 0:frames] += dot3(foot, (high_ref[...], low_ref[...]), NN)
        if with_gram:
            total[:, frames:] += dot3(foot, foot, NT)

        @pl.when(step == steps - 1)
        def _():
            mine = pl.multiple_of(scalars[1] * half, half)
            other = pl.multiple_of((1 - scalars[1]) * half, half)
            keep_ref[...] = total[pl.ds(mine, half), :]
            send_ref[...] = total[pl.ds(other, half), :]

    foot_spec = pl.BlockSpec((own.shape[0], block), lambda k, s: (0, k))
    movie_spec = pl.BlockSpec((block, frames), lambda k, s: (k, 0))
    out_spec = pl.BlockSpec((half, columns), lambda k, s: (0, 0))
    out = jax.ShapeDtypeStruct((half, columns), jnp.float32)
    flat = [array for pair in pairs for array in pair]
    return pl.pallas_call(
        kernel,
        grid_spec=pltpu.PrefetchScalarGridSpec(
            num_scalar_prefetch=1,
            grid=(steps,),
            in_specs=[foot_spec] * (1 + len(flat)) + [movie_spec] * 2,
            out_specs=[out_spec, out_spec],
            scratch_shapes=[pltpu.VMEM((rank, columns), jnp.float32)],
        ),
        out_shape=[out, out],
        cost_estimate=pl.CostEstimate(
            flops=6 * rank * pixel_count * columns,
            bytes_accessed=4 * pixel_count * (rank + frames),
            transcendentals=0,
        ),
        name="numerator",
    )(scalars, own, *flat, high, low)


def traces_call(scalars, first, second, gram_first, gram_second, trace_full, chunk, count, frames):
    half = first.shape[0]
    rank = 2 * half
    share = rank // count
    whole = trace_full.shape

    def kernel(scalars, first_ref, second_ref, gram_a, gram_b, trace_ref, out_ref, rotated):
        here = scalars[0]
        for k in range(count):
            at = pl.multiple_of(lax.rem(here + k, count) * share, share)
            rotated[k * share : (k + 1) * share, :] = trace_ref[pl.ds(at, share), :]
        gram = gram_a[...] + gram_b[...]
        below = dot3(split(gram), split(rotated[...]), NN)
        mine = pl.multiple_of(scalars[1] * half, half)
        out_ref[...] = rotated[pl.ds(mine, half), :] * (first_ref[...] + second_ref[...]) / below

    sum_spec = pl.BlockSpec((half, frames), lambda k, s: (0, 0))
    gram_spec = pl.BlockSpec((half, rank), lambda k, s: (0, frames // rank))
    return pl.pallas_call(
        kernel,
        grid_spec=pltpu.PrefetchScalarGridSpec(
            num_scalar_prefetch=1,
            grid=(1,),
            in_specs=[sum_spec, sum_spec, gram_spec, gram_spec]
            + [pl.BlockSpec((rank, frames), lambda k, s: (0, chunk))],
            out_specs=pl.BlockSpec((half, frames), lambda k, s: (0, 0)),
            scratch_shapes=[pltpu.VMEM((rank, frames), jnp.float32)],
        ),
        out_shape=jax.ShapeDtypeStruct((half, frames), jnp.float32),
        cost_estimate=pl.CostEstimate(
            flops=6 * half * rank * frames, bytes_accessed=8 * rank * frames, transcendentals=0
        ),
        name="traces",
    )(scalars, first, second, gram_first, gram_second, trace_full)


def foot_call(scalars, mine, other, high, low, carried, slots, count, trace_rows):
    half, frames = mine.shape
    rank = 2 * half
    share = rank // count
    pixel_count = high.shape[0]
    block = rank
    steps = pixel_count // block

    def kernel(scalars, mine_ref, other_ref, high_ref, low_ref, *refs):
        carried_refs = refs[: len(carried)]
        refs = refs[len(carried) :]
        out_refs = refs[: len(slots)]
        traces_ref, full, full_high, full_low, ordered = refs[len(slots) :]
        step = pl.program_id(0)

        @pl.when(step == 0)
        def _():
            core = scalars[1]
            full[pl.ds(pl.multiple_of(core * half, half), half), :] = mine_ref[...]
            full[pl.ds(pl.multiple_of((1 - core) * half, half), half), :] = other_ref[...]
            full_high[...], full_low[...] = split(full[...])
            rows = traces_ref.shape[0]
            traces_ref[...] = full[pl.ds(pl.multiple_of(scalars[2], rows), rows), :]
            for k in range(count):
                at = pl.multiple_of(lax.rem(scalars[0] + k, count) * share, share)
                ordered[pl.ds(at, share), :] = full[k * share : (k + 1) * share, :]

        def emit(right):
            for k, slot in enumerate(slots):
                at = slot * share
                left = (full_high[at : at + share, :], full_low[at : at + share, :])
                value = dot3(left, right, NT)
                if carried:
                    value = value + carried_refs[k][...]
                out_refs[k][...] = value

        @pl.when(step < steps)
        def _():
            emit((high_ref[...], low_ref[...]))

        @pl.when(step == steps)
        def _():
            emit(split(ordered[...]))

    half_spec = pl.BlockSpec((half, frames), lambda j, s: (0, 0))
    movie_spec = pl.BlockSpec((block, frames), lambda j, s: (jnp.minimum(j, steps - 1), 0))
    block_spec = pl.BlockSpec((share, block), lambda j, s: (0, j))
    return pl.pallas_call(
        kernel,
        grid_spec=pltpu.PrefetchScalarGridSpec(
            num_scalar_prefetch=1,
            grid=(steps + 1,),
            in_specs=[half_spec] * 2 + [movie_spec] * 2 + [block_spec] * len(carried),
            out_specs=[block_spec] * len(slots) + [pl.BlockSpec((trace_rows, frames), lambda j, s: (0, 0))],
            scratch_shapes=[
                pltpu.VMEM((rank, frames), jnp.float32),
                pltpu.VMEM((rank, frames), jnp.bfloat16),
                pltpu.VMEM((rank, frames), jnp.bfloat16),
                pltpu.VMEM((rank, frames), jnp.float32),
            ],
        ),
        out_shape=[jax.ShapeDtypeStruct((share, pixel_count + rank), jnp.float32)] * len(slots)
        + [jax.ShapeDtypeStruct((trace_rows, frames), jnp.float32)],
        cost_estimate=pl.CostEstimate(
            flops=6 * share * len(slots) * pixel_count * frames,
            bytes_accessed=4 * pixel_count * (frames + share * len(slots)),
            transcendentals=0,
        ),
        name="foot",
    )(scalars, mine, other, high, low, *carried)


def final_call(scalars, own, pairs, parts):
    count = len(pairs) + 1
    share, pixel_count = own.shape
    rank = share * count
    block = 512
    steps = pixel_count // block

    def kernel(scalars, *refs):
        own_ref = refs[0]
        pair_refs = [(refs[1 + 2 * k], refs[2 + 2 * k]) for k in range(count - 1)]
        refs = refs[2 * count - 1 :]
        part_refs = refs[: len(parts)]
        gram_refs = refs[len(parts) : 2 * len(parts)]
        out_ref, ordered = refs[-2:]
        above = part_refs[0][...]
        gram = gram_refs[0][...]
        for part_ref, gram_ref in zip(part_refs[1:], gram_refs[1:]):
            above = above + part_ref[...]
            gram = gram + gram_ref[...]
        here = scalars[0]
        ordered[pl.ds(pl.multiple_of(here * share, share), share), :] = own_ref[...]
        for s, (from_above, from_below) in enumerate(pair_refs, 1):
            at = pl.multiple_of(lax.rem(here + s, count) * share, share)
            ordered[pl.ds(at, share), :] = jnp.where(here + s < count, from_above[...], from_below[...])
        below = dot3(split(gram), split(ordered[...]), NN)
        out_ref[...] = own_ref[...] * above / below

    foot_spec = pl.BlockSpec((share, block), lambda k, s: (0, k))
    gram_spec = pl.BlockSpec((share, rank), lambda k, s: (0, pixel_count // rank))
    flat = [array for pair in pairs for array in pair]
    return pl.pallas_call(
        kernel,
        grid_spec=pltpu.PrefetchScalarGridSpec(
            num_scalar_prefetch=1,
            grid=(steps,),
            in_specs=[foot_spec] * (1 + len(flat)) + [foot_spec] * len(parts) + [gram_spec] * len(parts),
            out_specs=foot_spec,
            scratch_shapes=[pltpu.VMEM((rank, block), jnp.float32)],
        ),
        out_shape=jax.ShapeDtypeStruct((share, pixel_count), jnp.float32),
        cost_estimate=pl.CostEstimate(
            flops=6 * share * rank * pixel_count, bytes_accessed=4 * pixel_count * (rank + 5 * share), transcendentals=0
        ),
        name="final",
    )(scalars, own, *flat, *parts, *parts)


def line_gather(block, axis, count, here):
    up, down = {}, {}
    last_up = last_down = block
    for r in range(1, count):
        up_pairs = [(k, k + 1) for k in range(r - 1, count - 1)]
        down_pairs = [(k + 1, k) for k in range(0, count - r)]
        if r == count - 1 and count != 3:
            merged = jnp.where(here == 1, last_down, last_up) if count > 2 else block
            last_up = last_down = lax.ppermute(merged, axis, up_pairs + down_pairs)
        else:
            last_up = lax.ppermute(last_up, axis, up_pairs)
            last_down = lax.ppermute(last_down, axis, down_pairs)
        up[r], down[r] = last_up, last_down
    return [(down[s], up[count - s]) for s in range(1, count)]


def body(raw_movie, footprints, traces):
    rows, cols, frame_count = raw_movie.shape
    pixel_count = rows * cols
    share = footprints.shape[0]
    pix_count = lax.axis_size("pix")
    count = lax.axis_size("tm")
    pix = lax.axis_index("pix")
    here = lax.axis_index("tm")
    core = lax.rem(pix, 2)
    rank = share * count
    trace_rows = traces.shape[0]
    start = lax.rem(pix * trace_rows - here * share + rank, rank)
    frames = frame_count // CHUNKS
    halo = SUBSTEPS

    pairs = line_gather(footprints, "tm", count, here)

    group = 4
    up_pairs = [(k, k + 1) for k in range(pix_count - 1)]
    bent = [k for k in range(pix_count - 1) if k % group == group - 1] if pix_count % group == 0 else []
    halos = []
    for c in range(CHUNKS):
        cut = slice(c * frames, (c + 1) * frames)
        send = [(k, k + 1) for k in range(pix_count - 1) if c == 0 or k not in bent]
        tail = raw_movie[rows - halo :, :, cut]
        head = raw_movie[:halo, :, cut]
        from_above = lax.ppermute(tail, "pix", send)
        from_below = lax.ppermute(head, "pix", [(b, a) for a, b in send])
        detour = None
        if c > 0 and bent:
            corner = lax.rem(pix, group) == group - 1
            edge = lax.dynamic_slice(
                raw_movie, (jnp.where(corner, rows - halo, 0), 0, c * frames), (halo, cols, frames)
            )
            first = [(k, k + group) for k in bent] + [(k + 1, k + 1 - group) for k in bent]
            second = [(k + group, k + 1) for k in bent] + [(k + 1 - group, k) for k in bent]
            detour = lax.ppermute(lax.ppermute(edge, "pix", first), "pix", second)
        halos.append((from_above, from_below, detour))

    trace_full = lax.all_gather(traces, "pix", axis=0, tiled=True)

    flags = jnp.stack(
        [
            (pix > 0).astype(jnp.int32),
            (pix < pix_count - 1).astype(jnp.int32),
            (lax.rem(pix, group) == 0).astype(jnp.int32) * (pix > 0),
            (lax.rem(pix, group) == group - 1).astype(jnp.int32) * (pix < pix_count - 1),
        ]
    )
    scalars = jnp.stack([here, core, start]).astype(jnp.int32)

    current = None
    gram_parts = None
    halves = []
    movies = []
    swap = [(k, k ^ 1) for k in range(pix_count)]
    for c in range(CHUNKS):
        from_above, from_below, detour = halos[c]
        current, high, low = diffuse_call(
            flags, raw_movie, from_above, from_below, detour, current, c * frames, frames
        )
        high = high.reshape(pixel_count, frames)
        low = low.reshape(pixel_count, frames)
        movies.append((high, low))
        total, given = numerator_call(scalars, footprints, pairs, high, low, c == 0)
        arrived = lax.ppermute(given, "pix", swap)
        bit = 2
        while bit < pix_count:
            total = total + arrived
            arrived = lax.ppermute(total, "pix", [(k, k ^ bit) for k in range(pix_count)])
            bit *= 2
        if c == 0:
            gram_parts = (total, arrived)
        mine = traces_call(scalars, total, arrived, *gram_parts, trace_full, c, count, frames)
        halves.append((mine, lax.ppermute(mine, "pix", swap)))

    slots = list(range(count))
    partial = []
    new_traces = []
    for c in range(CHUNKS - 1):
        mine, other = halves[c]
        result = foot_call(scalars, mine, other, *movies[c], partial, slots, count, trace_rows)
        partial = result[:count]
        new_traces.append(result[count])
    mine, other = halves[-1]
    result = foot_call(scalars, mine, other, *movies[-1], partial, slots, count, trace_rows)
    blocks = result[:count]
    new_traces.append(result[count])

    sent = jnp.where(here == 0, blocks[count - 1], blocks[1])
    up_last = down_last = None
    for r in range(1, count):
        up_pairs = [(k, k + 1) for k in range(r)]
        down_pairs = [(count - 1 - k, count - 2 - k) for k in range(r)]
        if r == 1 and count > 3:
            up_last = down_last = lax.ppermute(sent, "tm", up_pairs + down_pairs)
            continue
        up_block, down_block = blocks[count - r], blocks[r]
        if r > 1:
            up_block = up_block + up_last
            down_block = down_block + down_last
        up_last = lax.ppermute(up_block, "tm", up_pairs)
        down_last = lax.ppermute(down_block, "tm", down_pairs)
    new_footprints = final_call(scalars, footprints, pairs, [blocks[0], up_last, down_last])
    return current, new_footprints, jnp.concatenate(new_traces, axis=1)


def solution(mesh):
    placed = (P("pix", None, "tm"), P("tm", "pix"), P("pix", "tm"))
    return jax.shard_map(
        body,
        mesh=mesh,
        in_specs=placed,
        out_specs=(P("pix", None, "tm"), P("tm", "pix"), P("pix", "tm")),
        check_vma=False,
    )
```

```python
import jax
import jax.numpy as jnp
from jax import lax
from jax.experimental import pallas as pl
from jax.experimental.pallas import tpu as pltpu
from jax.sharding import PartitionSpec as P


edge_square = 0.25
step_scale = 0.06
SUBSTEPS = 4
LANES = 128
GROUP = 4
HALVES = 2
CHUNKS = 2

NN = ((1,), (0,))
NT = ((1,), (1,))


def flux_quarter(change):
    return change / (change * change + edge_square)


def split(value):
    high = value.astype(jnp.bfloat16)
    low = (value - high.astype(jnp.float32)).astype(jnp.bfloat16)
    return high, low


def stacked(value):
    return jnp.concatenate(split(value), axis=0)


def dot(left, right, dims):
    return lax.dot_general(left, right, (dims, ((), ())), preferred_element_type=jnp.float32)


def fold(value):
    half = value.shape[0] // 2
    return value[:half] + value[half:]


def cost(flops, moved):
    return pl.CostEstimate(flops=flops, bytes_accessed=moved, transcendentals=0)


def shaped(*shape, dtype=jnp.float32):
    return jax.ShapeDtypeStruct(shape, dtype)


def edges_call(flags, raw, halo, chunk, frames, with_corner):
    rows, cols, _ = raw.shape
    shift = rows - halo

    def kernel(flags, head_ref, tail_ref, head_out, tail_out, *corner_out):
        head_out[...] = head_ref[...]
        tail_out[...] = tail_ref[...]
        if with_corner:
            corner_out[0][...] = jnp.where(flags[4] == 1, tail_ref[...], head_ref[...])

    block = (1, cols, frames)
    outs = 3 if with_corner else 2
    return pl.pallas_call(
        kernel,
        grid_spec=pltpu.PrefetchScalarGridSpec(
            num_scalar_prefetch=1,
            grid=(halo,),
            in_specs=[
                pl.BlockSpec(block, lambda i, flags: (i, 0, chunk)),
                pl.BlockSpec(block, lambda i, flags: (shift + i, 0, chunk)),
            ],
            out_specs=[pl.BlockSpec(block, lambda i, flags: (i, 0, 0))] * outs,
        ),
        out_shape=[shaped(halo, cols, frames)] * outs,
        cost_estimate=cost(1, 4 * halo * cols * frames * 4),
        name="edges",
    )(flags, raw, raw)


def diffuse_call(flags, raw, halo_up, halo_down, detour, carried, chunk):
    rows, cols, total = raw.shape
    halo, _, frames = halo_up.shape
    groups = frames // LANES
    width = 64
    pad = 8
    extended = rows + 2 * halo

    def kernel(flags, *refs):
        if detour is None:
            raw_ref, up_ref, down_ref = refs[:3]
            refs = refs[3:]
        else:
            raw_ref, up_ref, down_ref, detour_ref = refs[:4]
            refs = refs[4:]
        if carried is not None:
            refs = refs[1:]
        out_ref, pair_ref, first_buf, second_buf = refs
        zero = jnp.zeros((extended, pad, LANES), jnp.float32)
        for buf in (first_buf, second_buf):
            buf[:, 0:pad, :] = zero
            buf[:, pad + cols :, :] = zero
        inside = slice(pad, pad + cols)
        first_buf[0:halo, inside, :] = up_ref[...]
        first_buf[halo : halo + rows, inside, :] = raw_ref[...]
        first_buf[halo + rows :, inside, :] = down_ref[...]
        if detour is not None:

            @pl.when(flags[2] == 1)
            def _():
                first_buf[0:halo, inside, :] = detour_ref[...]

            @pl.when(flags[3] == 1)
            def _():
                first_buf[halo + rows :, inside, :] = detour_ref[...]

        scale_up = step_scale * flags[0].astype(jnp.float32)
        scale_down = step_scale * flags[1].astype(jnp.float32)
        head = lax.broadcasted_iota(jnp.int32, (width, LANES), 0) == 0
        bufs = (first_buf, second_buf)
        for step in range(SUBSTEPS):
            src, dst = bufs[step % 2], bufs[1 - step % 2]
            top = step
            middle = range(step + 1, extended - step - 1)

            def tile(j, left_flux):
                base = pl.multiple_of(pad + j * width, 8)
                col = pl.multiple_of(j * width, width)
                kept = []
                current = src[top + 1, pl.ds(base, width), :]
                flux_up = flux_quarter(current - src[top, pl.ds(base, width), :])
                for k, row in enumerate(middle):
                    below = src[row + 1, pl.ds(base, width), :]
                    flux_down = flux_quarter(below - current)
                    flux_right = flux_quarter(src[row, pl.ds(base + 1, width), :] - current)
                    rolled = pltpu.roll(flux_right, 1, 0)
                    flux_left = jnp.where(head, left_flux[k], rolled)
                    scale = step_scale
                    if row < halo:
                        scale = scale_up
                    if row >= halo + rows:
                        scale = scale_down
                    value = current + scale * ((flux_down - flux_up) + (flux_right - flux_left))
                    kept.append(rolled)
                    if step + 1 < SUBSTEPS:
                        dst[row, pl.ds(base, width), :] = value
                    else:
                        out_ref[row - halo, pl.ds(col, width), :] = value
                        high, low = split(value)
                        pair_ref[row - halo, pl.ds(col, width), 0:LANES] = high
                        pair_ref[row - halo, pl.ds(col, width), LANES:] = low
                    current, flux_up = below, flux_down
                return tuple(kept)

            edge = tuple(flux_quarter(src[row, pl.ds(pad, width), :]) for row in middle)
            lax.fori_loop(0, cols // width, tile, edge)

    def spec(count, at):
        return pl.BlockSpec((count, cols, LANES), lambda i, flags: (0, 0, at + i))

    operands = [flags, raw, halo_up, halo_down]
    in_specs = [spec(rows, chunk * groups), spec(halo, 0), spec(halo, 0)]
    if detour is not None:
        operands.append(detour)
        in_specs.append(spec(halo, 0))
    aliases = {}
    if carried is not None:
        operands.append(carried)
        in_specs.append(pl.BlockSpec(memory_space=pl.ANY))
        aliases = {len(operands) - 1: 0}
    return pl.pallas_call(
        kernel,
        grid_spec=pltpu.PrefetchScalarGridSpec(
            num_scalar_prefetch=1,
            grid=(groups,),
            in_specs=in_specs,
            out_specs=[
                spec(rows, chunk * groups),
                pl.BlockSpec((rows, cols, 2 * LANES), lambda i, flags: (0, 0, i)),
            ],
            scratch_shapes=[pltpu.VMEM((extended, cols + 2 * pad, LANES), jnp.float32)] * 2,
        ),
        out_shape=[shaped(rows, cols, total), shaped(rows, cols, 2 * frames, dtype=jnp.bfloat16)],
        input_output_aliases=aliases,
        cost_estimate=cost(rows * cols * frames * 200, rows * cols * frames * 16),
        name="diffuse",
    )(*operands)


def footprints_call(scalars, own, pairs):
    count = len(pairs) + 1
    share, pixel_count = own.shape
    rank = share * count
    block = 512
    steps = pixel_count // block

    def kernel(scalars, *refs):
        own_ref = refs[0]
        pair_refs = [(refs[1 + 2 * k], refs[2 + 2 * k]) for k in range(count - 1)]
        out_ref, gram_ref, total = refs[2 * count - 1 :]
        here = scalars[0]
        step = pl.program_id(0)

        def put(slot, value):
            at = pl.multiple_of(lax.rem(here + slot, count) * share, share)
            high, low = split(value)
            out_ref[pl.ds(at, share), :] = high
            out_ref[pl.ds(rank + at, share), :] = low

        put(0, own_ref[...])
        for s, (from_above, from_below) in enumerate(pair_refs, 1):
            put(s, jnp.where(here + s < count, from_above[...], from_below[...]))

        @pl.when(step == 0)
        def _():
            total[...] = jnp.zeros_like(total)

        total[...] += dot(out_ref[...], out_ref[0:rank, :], NT)

        @pl.when(step == steps - 1)
        def _():
            cross = total[rank:, :]
            gram_ref[...] = total[0:rank, :] + (cross + cross.T)

    foot_spec = pl.BlockSpec((share, block), lambda k, s: (0, k))
    flat = [array for pair in pairs for array in pair]
    return pl.pallas_call(
        kernel,
        grid_spec=pltpu.PrefetchScalarGridSpec(
            num_scalar_prefetch=1,
            grid=(steps,),
            in_specs=[foot_spec] * (1 + len(flat)),
            out_specs=[
                pl.BlockSpec((2 * rank, block), lambda k, s: (0, k)),
                pl.BlockSpec((rank, rank), lambda k, s: (0, 0)),
            ],
            scratch_shapes=[pltpu.VMEM((2 * rank, rank), jnp.float32)],
        ),
        out_shape=[shaped(2 * rank, pixel_count, dtype=jnp.bfloat16), shaped(rank, rank)],
        cost_estimate=cost(4 * rank * rank * pixel_count, 8 * rank * pixel_count),
        name="footprints",
    )(scalars, own, *flat)


def numerator_call(scalars, foot, movies, gram, trace_rows):
    rank = foot.shape[0] // 2
    pixel_count, pair = movies[0].shape
    frames = pair // 2
    columns = frames * len(movies) + rank
    block = 512
    steps = pixel_count // block
    chips = rank // (2 * trace_rows)

    def kernel(scalars, foot_ref, gram_ref, *refs):
        movie_refs = refs[: len(movies)]
        keep_ref, send_ref, total = refs[len(movies) :]
        step = pl.program_id(0)

        @pl.when(step == 0)
        def _():
            total[...] = jnp.zeros_like(total)

        for k, movie_ref in enumerate(movie_refs):
            part = fold(dot(foot_ref[...], movie_ref[...], NN))
            for g in range(frames // LANES):
                at = k * frames + g * LANES
                both = part[:, 2 * g * LANES : 2 * (g + 1) * LANES]
                total[:, at : at + LANES] += both[:, 0:LANES] + both[:, LANES:]

        @pl.when(step == steps - 1)
        def _():
            total[:, frames * len(movies) :] = gram_ref[...]
            core = scalars[1]
            for k in range(chips):
                chip = scalars[2] ^ k
                mine = pl.multiple_of((2 * chip + core) * trace_rows, trace_rows)
                other = pl.multiple_of((2 * chip + 1 - core) * trace_rows, trace_rows)
                keep_ref[k] = total[pl.ds(mine, trace_rows), :]
                send_ref[k] = total[pl.ds(other, trace_rows), :]

    out_spec = pl.BlockSpec((chips, trace_rows, columns), lambda k, s: (0, 0, 0))
    return pl.pallas_call(
        kernel,
        grid_spec=pltpu.PrefetchScalarGridSpec(
            num_scalar_prefetch=1,
            grid=(steps,),
            in_specs=[
                pl.BlockSpec((2 * rank, block), lambda k, s: (0, k)),
                pl.BlockSpec((rank, rank), lambda k, s: (0, 0)),
            ]
            + [pl.BlockSpec((block, pair), lambda k, s: (k, 0))] * len(movies),
            out_specs=[out_spec, out_spec],
            scratch_shapes=[pltpu.VMEM((rank, columns), jnp.float32)],
        ),
        out_shape=[shaped(chips, trace_rows, columns)] * 2,
        cost_estimate=cost(8 * rank * pixel_count * columns, 4 * pixel_count * (rank + columns)),
        name="numerator",
    )(scalars, foot, gram, *movies)


def traces_call(scalars, keep, arrived, parts, near, far):
    _, trace_rows, columns = keep.shape
    frames = near.shape[2]
    rank = columns - frames
    chips = near.shape[0]

    def kernel(scalars, near_ref, far_ref, *refs):
        part_refs, (out_ref, full) = refs[:-2], refs[-2:]
        for k in range(chips):
            device = 2 * (scalars[2] ^ k) + scalars[1]
            full[pl.ds(pl.multiple_of(device * trace_rows, trace_rows), trace_rows), :] = near_ref[k]
            device = 2 * (scalars[2] ^ k) + 1 - scalars[1]
            full[pl.ds(pl.multiple_of(device * trace_rows, trace_rows), trace_rows), :] = far_ref[k]
        total = part_refs[0][0] + part_refs[1][0]
        for part_ref in part_refs[2:]:
            total = total + part_ref[...]
        gram = stacked(total[:, frames:])
        high, low = split(full[...])
        below = fold(dot(gram, high, NN)) + dot(gram[0:trace_rows], low, NN)
        out_ref[...] = near_ref[0] * total[:, 0:frames] / below

    whole = pl.BlockSpec(near.shape, lambda k, s: (0, 0, 0))
    return pl.pallas_call(
        kernel,
        grid_spec=pltpu.PrefetchScalarGridSpec(
            num_scalar_prefetch=1,
            grid=(1,),
            in_specs=[whole, whole]
            + [pl.BlockSpec((1, trace_rows, columns), lambda k, s: (0, 0, 0))] * 2
            + [pl.BlockSpec((trace_rows, columns), lambda k, s: (0, 0))] * len(parts),
            out_specs=pl.BlockSpec((trace_rows, frames), lambda k, s: (0, 0)),
            scratch_shapes=[pltpu.VMEM((rank, frames), jnp.float32)],
        ),
        out_shape=shaped(trace_rows, frames),
        cost_estimate=cost(6 * trace_rows * rank * frames, 8 * rank * frames),
        name="traces",
    )(scalars, near, far, keep, arrived, *parts)


def products_call(scalars, near, far, movies, half, count, with_gram):
    chips = len(near)
    trace_rows, frames = near[0].shape
    rank = 2 * chips * trace_rows
    share = rank // count
    pixel_count, pair = movies[0].shape
    part = pixel_count // HALVES
    block = rank
    steps = part // block
    columns = part + (rank if with_gram else 0)
    groups = frames // LANES
    outs = count + 1

    def kernel(scalars, *refs):
        near_refs, far_refs, refs = refs[:chips], refs[chips : 2 * chips], refs[2 * chips :]
        movie_refs = refs[: len(movies)]
        refs = refs[len(movies) :]
        out_refs = refs[:outs]
        full, left, result = refs[outs:]
        step = pl.program_id(0)
        here = scalars[0]

        @pl.when(step == 0)
        def _():
            for k in range(chips):
                device = 2 * (scalars[2] ^ k) + scalars[1]
                full[pl.ds(pl.multiple_of(device * trace_rows, trace_rows), trace_rows), :] = near_refs[k][...]
                device = 2 * (scalars[2] ^ k) + 1 - scalars[1]
                full[pl.ds(pl.multiple_of(device * trace_rows, trace_rows), trace_rows), :] = far_refs[k][...]
            high, low = split(full[...])
            for g in range(groups):
                cut = slice(g * LANES, (g + 1) * LANES)
                at = 2 * g * LANES
                left[0:rank, at : at + LANES] = high[:, cut]
                left[0:rank, at + LANES : at + 2 * LANES] = high[:, cut]
                left[rank:, at : at + LANES] = low[:, cut]
                left[rank:, at + LANES : at + 2 * LANES] = jnp.zeros_like(low[:, cut])

        def emit(total, at):
            result[...] = total
            for k, out_ref in enumerate(out_refs):
                slot = lax.rem(here + k, count) if k < count else scalars[3]
                row = pl.multiple_of(slot * share, share)
                out_ref[:, pl.ds(at, block)] = result[pl.ds(row, share), :]

        total = dot(left[:, 0:pair], movie_refs[0][...], NT)
        for k in range(1, len(movies)):
            total += dot(left[:, k * pair : (k + 1) * pair], movie_refs[k][...], NT)
        emit(fold(total), pl.multiple_of(step * block, block))
        if with_gram:

            @pl.when(step == steps - 1)
            def _():
                high, low = split(full[...])
                both = dot(jnp.concatenate([high, low], axis=0), high, NT)
                cross = both[rank:]
                emit(both[0:rank] + (cross + cross.T), part)

    piece = pl.BlockSpec((trace_rows, frames), lambda j, s: (0, 0))
    return pl.pallas_call(
        kernel,
        grid_spec=pltpu.PrefetchScalarGridSpec(
            num_scalar_prefetch=1,
            grid=(steps,),
            in_specs=[piece] * (2 * chips)
            + [pl.BlockSpec((block, pair), lambda j, s: (half * steps + j, 0))] * len(movies),
            out_specs=[pl.BlockSpec((share, columns), lambda j, s: (0, 0))] * outs,
            scratch_shapes=[
                pltpu.VMEM((rank, frames), jnp.float32),
                pltpu.VMEM((2 * rank, 2 * frames), jnp.bfloat16),
                pltpu.VMEM((rank, block), jnp.float32),
            ],
        ),
        out_shape=[shaped(share, columns)] * outs,
        cost_estimate=cost(8 * rank * part * frames, 4 * part * (frames + rank)),
        name="products",
    )(scalars, *near, *far, *movies)


def final_call(scalars, own, foot, parts, grams, carried, half):
    share, pixel_count = own.shape
    rank = foot.shape[0] // 2
    part = pixel_count // HALVES
    block = 512
    steps = part // block

    def kernel(scalars, own_ref, foot_ref, *refs):
        part_refs = refs[: len(parts)]
        gram_refs = refs[len(parts) : len(parts) + len(grams)]
        out_ref = refs[-1]
        above = part_refs[0][...]
        for part_ref in part_refs[1:]:
            above = above + part_ref[...]
        gram = gram_refs[0][...]
        for gram_ref in gram_refs[1:]:
            gram = gram + gram_ref[...]
        both = stacked(gram)
        below = fold(dot(both, foot_ref[0:rank, :], NN)) + dot(both[0:share], foot_ref[rank:, :], NN)
        out_ref[...] = own_ref[...] * above / below

    at = half * steps
    in_specs = [
        pl.BlockSpec((share, block), lambda k, s: (0, at + k)),
        pl.BlockSpec((2 * rank, block), lambda k, s: (0, at + k)),
    ]
    in_specs += [pl.BlockSpec((share, block), lambda k, s: (0, k))] * len(parts)
    in_specs += [pl.BlockSpec((share, rank), lambda k, s: (0, part // rank))] * len(grams)
    operands = [scalars, own, foot, *parts, *grams]
    aliases = {}
    if carried is not None:
        operands.append(carried)
        in_specs.append(pl.BlockSpec(memory_space=pl.ANY))
        aliases = {len(operands) - 1: 0}
    return pl.pallas_call(
        kernel,
        grid_spec=pltpu.PrefetchScalarGridSpec(
            num_scalar_prefetch=1,
            grid=(steps,),
            in_specs=in_specs,
            out_specs=pl.BlockSpec((share, block), lambda k, s: (0, at + k)),
        ),
        out_shape=shaped(share, pixel_count),
        input_output_aliases=aliases,
        cost_estimate=cost(6 * share * rank * part, 4 * part * (rank + 5 * share)),
        name="final",
    )(*operands)


def line_gather(block, axis, count, here):
    up, down = {}, {}
    last_up = last_down = block
    for r in range(1, count):
        up_pairs = [(k, k + 1) for k in range(r - 1, count - 1)]
        down_pairs = [(k + 1, k) for k in range(0, count - r)]
        if r == count - 1 and count != 3:
            merged = jnp.where(here == 1, last_down, last_up) if count > 2 else block
            last_up = last_down = lax.ppermute(merged, axis, up_pairs + down_pairs)
        else:
            last_up = lax.ppermute(last_up, axis, up_pairs)
            last_down = lax.ppermute(last_down, axis, down_pairs)
        up[r], down[r] = last_up, last_down
    return [(down[s], up[count - s]) for s in range(1, count)]


def line_scatter(blocks, axis, count):
    up_last = down_last = None
    for r in range(1, count):
        up_pairs = [(k, k + 1) for k in range(r)]
        down_pairs = [(count - 1 - k, count - 2 - k) for k in range(r)]
        if r == 1 and count > 3:
            up_last = down_last = lax.ppermute(blocks[count], axis, up_pairs + down_pairs)
            continue
        up_block, down_block = blocks[count - r], blocks[r]
        if r > 1:
            up_block = up_block + up_last
            down_block = down_block + down_last
        up_last = lax.ppermute(up_block, axis, up_pairs)
        down_last = lax.ppermute(down_block, axis, down_pairs)
    return [blocks[0], up_last, down_last]


def compute(raw_movie, footprints, traces):
    rows, cols, frame_count = raw_movie.shape
    pixel_count = rows * cols
    pix_count = lax.axis_size("pix")
    count = lax.axis_size("tm")
    pix = lax.axis_index("pix")
    here = lax.axis_index("tm")
    core = lax.rem(pix, 2)
    trace_rows = traces.shape[0]
    frames = frame_count // CHUNKS
    halo = SUBSTEPS

    def swap(mask):
        return [(k, k ^ mask) for k in range(pix_count)]

    inner = (pix > 0).astype(jnp.int32)
    outer = (pix < pix_count - 1).astype(jnp.int32)
    corner = (lax.rem(pix, GROUP) == GROUP - 1).astype(jnp.int32)
    flags = jnp.stack([inner, outer, (lax.rem(pix, GROUP) == 0) * inner, corner * outer, corner]).astype(jnp.int32)
    first_out = lax.rem(here + jnp.where(here == 0, count - 1, 1), count)
    scalars = jnp.stack([here, core, lax.div(pix, 2), first_out]).astype(jnp.int32)

    pairs = line_gather(footprints, "tm", count, here)

    bent = [k for k in range(pix_count - 1) if k % GROUP == GROUP - 1] if pix_count % GROUP == 0 else []
    halos = []
    for c in range(CHUNKS):
        last = c == CHUNKS - 1 and bool(bent)
        send = [(k, k + 1) for k in range(pix_count - 1) if not (last and k in bent)]
        edges = edges_call(flags, raw_movie, halo, c, frames, last)
        detour = None
        if last:
            first = [(k, k + GROUP) for k in bent] + [(k + 1, k + 1 - GROUP) for k in bent]
            second = [(k + GROUP, k + 1) for k in bent] + [(k + 1 - GROUP, k) for k in bent]
            detour = lax.ppermute(edges[2], "pix", first)
            detour = lax.ppermute(detour, "pix", second)
        from_above = lax.ppermute(edges[1], "pix", send)
        from_below = lax.ppermute(edges[0], "pix", [(b, a) for a, b in send])
        halos.append((from_above, from_below, detour))

    near = traces[None]
    mask = 2
    while mask < pix_count:
        near = jnp.concatenate([near, lax.ppermute(near, "pix", swap(mask))], axis=0)
        mask *= 2
    far = lax.ppermute(near, "pix", swap(1))

    current = None
    movies = []
    for c in range(CHUNKS):
        current, pair = diffuse_call(flags, raw_movie, *halos[c], current, c)
        movies.append(pair.reshape(pixel_count, 2 * frames))

    foot, gram = footprints_call(scalars, footprints, pairs)
    keep, send = numerator_call(scalars, foot, movies, gram, trace_rows)
    arrived = lax.ppermute(send, "pix", swap(1))
    parts = []
    for k in range(1, keep.shape[0]):
        parts.append(lax.ppermute(keep[k] + arrived[k], "pix", swap(2 * k)))
    new_traces = traces_call(scalars, keep, arrived, parts, near, far)
    near = [new_traces]
    for k in range(1, keep.shape[0]):
        near.append(lax.ppermute(new_traces, "pix", swap(2 * k)))
    far = []
    for piece in near:
        far.append(lax.ppermute(piece, "pix", swap(1)))

    products = []
    for h in range(HALVES):
        products.append(products_call(scalars, near, far, movies, h, count, h == 0))
    sums = [line_scatter(blocks, "tm", count) for blocks in products]
    new_footprints = None
    for h in range(HALVES):
        new_footprints = final_call(scalars, footprints, foot, sums[h], sums[0], new_footprints, h)
    return current, new_footprints, new_traces


def solution(mesh):
    placed = (P("pix", None, "tm"), P("tm", "pix"), P("pix", "tm"))
    return jax.shard_map(
        compute,
        mesh=mesh,
        in_specs=placed,
        out_specs=(P("pix", None, "tm"), P("tm", "pix"), P("pix", "tm")),
        check_vma=False,
    )
```

```python
import jax
import jax.numpy as jnp
from jax import lax
from jax.experimental import pallas as pl
from jax.experimental.pallas import tpu as pltpu
from jax.sharding import PartitionSpec as P


edge_square = 0.25
step_scale = 0.06
SUBSTEPS = 4
LANES = 128
GROUP = 4
HALVES = 2
CHUNKS = 2

HERE, CORE, CHIP, FIRST, TURNED, INSIDE, BENT, CORNER = 0, 1, 2, 3, 4, 5, 7, 9

NN = ((1,), (0,))
NT = ((1,), (1,))


def flux_quarter(change):
    return change / (change * change + edge_square)


def split(value):
    high = value.astype(jnp.bfloat16)
    low = (value - high.astype(jnp.float32)).astype(jnp.bfloat16)
    return high, low


def stacked(value):
    return jnp.concatenate(split(value), axis=0)


def dot(left, right, dims):
    return lax.dot_general(left, right, (dims, ((), ())), preferred_element_type=jnp.float32)


def fold(value):
    half = value.shape[0] // 2
    return value[:half] + value[half:]


def grant(mebibytes):
    return pltpu.CompilerParams(vmem_limit_bytes=mebibytes * 1024 * 1024)


def cost(flops, moved):
    return pl.CostEstimate(flops=flops, bytes_accessed=moved, transcendentals=0)


def shaped(*shape, dtype=jnp.float32):
    return jax.ShapeDtypeStruct(shape, dtype)


def edges_call(flags, raw, halo, chunk, frames, with_corner):
    rows, cols, _ = raw.shape
    shift = rows - halo
    outs = 3 if with_corner else 2

    def kernel(flags, raw_ref, *refs):
        out_refs, sems = refs[:outs], refs[outs]
        starts = [0, shift, flags[CORNER] * shift]
        copies = [
            pltpu.make_async_copy(
                raw_ref.at[pl.ds(starts[k], halo), :, pl.ds(chunk * frames, frames)], out_refs[k], sems.at[k]
            )
            for k in range(outs)
        ]
        for copy in copies:
            copy.start()
        for copy in copies:
            copy.wait()

    block = (halo, cols, frames)
    return pl.pallas_call(
        kernel,
        grid_spec=pltpu.PrefetchScalarGridSpec(
            num_scalar_prefetch=1,
            grid=(1,),
            in_specs=[pl.BlockSpec(memory_space=pltpu.HBM)],
            out_specs=[pl.BlockSpec(block, lambda i, flags: (0, 0, 0))] * outs,
            scratch_shapes=[pltpu.SemaphoreType.DMA((outs,))],
        ),
        out_shape=[shaped(*block)] * outs,
        cost_estimate=cost(1, 2 * outs * halo * cols * frames * 4),
        compiler_params=grant(8),
        name="edges",
    )(flags, raw)


def diffuse_call(flags, raw, halo_up, halo_down, detour, carried, chunk):
    rows, cols, total = raw.shape
    halo, _, frames = halo_up.shape
    groups = frames // LANES
    width = 64
    pad = 8
    extended = rows + 2 * halo
    inputs = 3 if detour is None else 4

    def kernel(flags, *refs):
        sources, refs = refs[:inputs], refs[inputs:]
        if carried is not None:
            refs = refs[1:]
        out_ref, pair_ref, first_bufs, second_buf, out_bufs, in_sems, out_sems = refs
        group = pl.program_id(0)
        slot = lax.rem(group, 2)
        inside = pl.ds(pad, cols)

        def fetches(at):
            here = lax.rem(at, 2)
            lanes = pl.ds(pl.multiple_of(at * LANES, LANES), LANES)
            wide = pl.ds(pl.multiple_of(chunk * frames + at * LANES, LANES), LANES)

            def one(ref, cut, start, count, part):
                return pltpu.make_async_copy(
                    ref.at[:, :, cut], first_bufs.at[here, pl.ds(start, count), inside, :], in_sems.at[here, part]
                )

            made = [(None, one(sources[0], wide, halo, rows, 0))]
            for part, start, source in ((1, 0, 1), (2, halo + rows, 2)):
                plain = one(sources[source], lanes, start, halo, part)
                if detour is None:
                    made.append((None, plain))
                else:
                    made.append((flags[BENT + part - 1] == 0, plain))
                    made.append((flags[BENT + part - 1] == 1, one(sources[3], lanes, start, halo, part)))
            return made

        def run(at, act):
            for condition, copy in fetches(at):
                if condition is None:
                    act(copy)
                else:
                    pl.when(condition)(lambda copy=copy: act(copy))

        def give(at):
            wide = pl.ds(pl.multiple_of(chunk * frames + at * LANES, LANES), LANES)
            here = lax.rem(at, 2)
            return pltpu.make_async_copy(out_bufs.at[here], out_ref.at[:, :, wide], out_sems.at[here])

        @pl.when(group == 0)
        def _():
            run(group, lambda copy: copy.start())

        @pl.when(group + 1 < groups)
        def _():
            run(group + 1, lambda copy: copy.start())

        zero = jnp.zeros((extended, pad, LANES), jnp.float32)
        first_buf = first_bufs.at[slot]
        for buf in (first_buf, second_buf):
            buf[:, 0:pad, :] = zero
            buf[:, pad + cols :, :] = zero
        run(group, lambda copy: copy.wait())

        @pl.when(group >= 2)
        def _():
            give(group - 2).wait()

        scale_up = step_scale * flags[INSIDE].astype(jnp.float32)
        scale_down = step_scale * flags[INSIDE + 1].astype(jnp.float32)
        head = lax.broadcasted_iota(jnp.int32, (width, LANES), 0) == 0
        bufs = (first_buf, second_buf)
        for step in range(SUBSTEPS):
            src, dst = bufs[step % 2], bufs[1 - step % 2]
            top = step
            middle = range(step + 1, extended - step - 1)

            def tile(j, left_flux):
                base = pl.multiple_of(pad + j * width, 8)
                col = pl.multiple_of(j * width, width)
                kept = []
                current = src[top + 1, pl.ds(base, width), :]
                flux_up = flux_quarter(current - src[top, pl.ds(base, width), :])
                for k, row in enumerate(middle):
                    below = src[row + 1, pl.ds(base, width), :]
                    flux_down = flux_quarter(below - current)
                    flux_right = flux_quarter(src[row, pl.ds(base + 1, width), :] - current)
                    rolled = pltpu.roll(flux_right, 1, 0)
                    flux_left = jnp.where(head, left_flux[k], rolled)
                    scale = step_scale
                    if row < halo:
                        scale = scale_up
                    if row >= halo + rows:
                        scale = scale_down
                    value = current + scale * ((flux_down - flux_up) + (flux_right - flux_left))
                    kept.append(rolled)
                    if step + 1 < SUBSTEPS:
                        dst[row, pl.ds(base, width), :] = value
                    else:
                        out_bufs[slot, row - halo, pl.ds(col, width), :] = value
                        high, low = split(value)
                        pair_ref[row - halo, pl.ds(col, width), 0:LANES] = high
                        pair_ref[row - halo, pl.ds(col, width), LANES:] = low
                    current, flux_up = below, flux_down
                return tuple(kept)

            edge = tuple(flux_quarter(src[row, pl.ds(pad, width), :]) for row in middle)
            lax.fori_loop(0, cols // width, tile, edge)
        give(group).start()

        @pl.when(group == groups - 1)
        def _():
            if groups > 1:
                give(group - 1).wait()
            give(group).wait()

    outside = pl.BlockSpec(memory_space=pltpu.HBM)
    operands = [flags, raw, halo_up, halo_down]
    if detour is not None:
        operands.append(detour)
    aliases = {}
    if carried is not None:
        operands.append(carried)
        aliases = {len(operands) - 1: 0}
    padded = (extended, cols + 2 * pad, LANES)
    return pl.pallas_call(
        kernel,
        grid_spec=pltpu.PrefetchScalarGridSpec(
            num_scalar_prefetch=1,
            grid=(groups,),
            in_specs=[outside] * (len(operands) - 1),
            out_specs=[outside, pl.BlockSpec((rows, cols, 2 * LANES), lambda i, flags: (0, 0, i))],
            scratch_shapes=[
                pltpu.VMEM((2, *padded), jnp.float32),
                pltpu.VMEM(padded, jnp.float32),
                pltpu.VMEM((2, rows, cols, LANES), jnp.float32),
                pltpu.SemaphoreType.DMA((2, 3)),
                pltpu.SemaphoreType.DMA((2,)),
            ],
        ),
        out_shape=[shaped(rows, cols, total), shaped(rows, cols, 2 * frames, dtype=jnp.bfloat16)],
        input_output_aliases=aliases,
        cost_estimate=cost(rows * cols * frames * 200, rows * cols * frames * 16),
        compiler_params=grant(16),
        name="diffuse",
    )(*operands)


def footprints_call(scalars, own, pairs):
    count = len(pairs) + 1
    share, pixel_count = own.shape
    rank = share * count
    block = 512
    steps = pixel_count // block

    def kernel(scalars, *refs):
        own_ref = refs[0]
        pair_refs = [(refs[1 + 2 * k], refs[2 + 2 * k]) for k in range(count - 1)]
        out_ref, gram_ref, total = refs[2 * count - 1 :]
        here = scalars[HERE]
        step = pl.program_id(0)

        def put(slot, value):
            at = pl.multiple_of(lax.rem(here + slot, count) * share, share)
            high, low = split(value)
            out_ref[pl.ds(at, share), :] = high
            out_ref[pl.ds(rank + at, share), :] = low

        put(0, own_ref[...])
        for s, (from_above, from_below) in enumerate(pair_refs, 1):
            put(s, jnp.where(here + s < count, from_above[...], from_below[...]))

        @pl.when(step == 0)
        def _():
            total[...] = jnp.zeros_like(total)

        total[...] += dot(out_ref[...], out_ref[0:rank, :], NT)

        @pl.when(step == steps - 1)
        def _():
            cross = total[rank:, :]
            gram_ref[...] = total[0:rank, :] + (cross + cross.T)

    foot_spec = pl.BlockSpec((share, block), lambda k, s: (0, k))
    flat = [array for pair in pairs for array in pair]
    return pl.pallas_call(
        kernel,
        grid_spec=pltpu.PrefetchScalarGridSpec(
            num_scalar_prefetch=1,
            grid=(steps,),
            in_specs=[foot_spec] * (1 + len(flat)),
            out_specs=[
                pl.BlockSpec((2 * rank, block), lambda k, s: (0, k)),
                pl.BlockSpec((rank, rank), lambda k, s: (0, 0)),
            ],
            scratch_shapes=[pltpu.VMEM((2 * rank, rank), jnp.float32)],
        ),
        out_shape=[shaped(2 * rank, pixel_count, dtype=jnp.bfloat16), shaped(rank, rank)],
        cost_estimate=cost(4 * rank * rank * pixel_count, 8 * rank * pixel_count),
        compiler_params=grant(8),
        name="footprints",
    )(scalars, own, *flat)


def numerator_call(scalars, foot, movies, gram, trace_rows):
    rank = foot.shape[0] // 2
    pixel_count, pair = movies[0].shape
    frames = pair // 2
    columns = frames * len(movies) + rank
    block = 512
    steps = pixel_count // block
    chips = rank // (2 * trace_rows)

    def kernel(scalars, foot_ref, gram_ref, *refs):
        movie_refs = refs[: len(movies)]
        keep_ref, send_ref, total = refs[len(movies) :]
        step = pl.program_id(0)

        @pl.when(step == 0)
        def _():
            total[...] = jnp.zeros_like(total)

        for k, movie_ref in enumerate(movie_refs):
            part = fold(dot(foot_ref[...], movie_ref[...], NN))
            for g in range(frames // LANES):
                at = k * frames + g * LANES
                both = part[:, 2 * g * LANES : 2 * (g + 1) * LANES]
                total[:, at : at + LANES] += both[:, 0:LANES] + both[:, LANES:]

        @pl.when(step == steps - 1)
        def _():
            total[:, frames * len(movies) :] = gram_ref[...]
            core = scalars[CORE]
            for k in range(chips):
                chip = scalars[CHIP] ^ k
                mine = pl.multiple_of((2 * chip + core) * trace_rows, trace_rows)
                other = pl.multiple_of((2 * chip + 1 - core) * trace_rows, trace_rows)
                keep_ref[k] = total[pl.ds(mine, trace_rows), :]
                send_ref[k] = total[pl.ds(other, trace_rows), :]

    out_spec = pl.BlockSpec((chips, trace_rows, columns), lambda k, s: (0, 0, 0))
    return pl.pallas_call(
        kernel,
        grid_spec=pltpu.PrefetchScalarGridSpec(
            num_scalar_prefetch=1,
            grid=(steps,),
            in_specs=[
                pl.BlockSpec((2 * rank, block), lambda k, s: (0, k)),
                pl.BlockSpec((rank, rank), lambda k, s: (0, 0)),
            ]
            + [pl.BlockSpec((block, pair), lambda k, s: (k, 0))] * len(movies),
            out_specs=[out_spec, out_spec],
            scratch_shapes=[pltpu.VMEM((rank, columns), jnp.float32)],
        ),
        out_shape=[shaped(chips, trace_rows, columns)] * 2,
        cost_estimate=cost(8 * rank * pixel_count * columns, 4 * pixel_count * (rank + columns)),
        compiler_params=grant(10),
        name="numerator",
    )(scalars, foot, gram, *movies)


def traces_call(scalars, keep, arrived, parts, near, far):
    _, trace_rows, columns = keep.shape
    frames = near.shape[2]
    rank = columns - frames
    chips = near.shape[0]

    def kernel(scalars, near_ref, far_ref, *refs):
        part_refs, (out_ref, copy_ref, full) = refs[:-3], refs[-3:]
        for k in range(chips):
            device = 2 * (scalars[CHIP] ^ k) + scalars[CORE]
            full[pl.ds(pl.multiple_of(device * trace_rows, trace_rows), trace_rows), :] = near_ref[k]
            device = 2 * (scalars[CHIP] ^ k) + 1 - scalars[CORE]
            full[pl.ds(pl.multiple_of(device * trace_rows, trace_rows), trace_rows), :] = far_ref[k]
        total = part_refs[0][0] + part_refs[1][0]
        for part_ref in part_refs[2:]:
            total = total + part_ref[...]
        gram = stacked(total[:, frames:])
        high, low = split(full[...])
        below = fold(dot(gram, high, NN)) + dot(gram[0:trace_rows], low, NN)
        value = near_ref[0] * total[:, 0:frames] / below
        out_ref[...] = value
        copy_ref[...] = value

    whole = pl.BlockSpec(near.shape, lambda k, s: (0, 0, 0))
    return pl.pallas_call(
        kernel,
        grid_spec=pltpu.PrefetchScalarGridSpec(
            num_scalar_prefetch=1,
            grid=(1,),
            in_specs=[whole, whole]
            + [pl.BlockSpec((1, trace_rows, columns), lambda k, s: (0, 0, 0))] * 2
            + [pl.BlockSpec((trace_rows, columns), lambda k, s: (0, 0))] * len(parts),
            out_specs=[pl.BlockSpec((trace_rows, frames), lambda k, s: (0, 0))] * 2,
            scratch_shapes=[pltpu.VMEM((rank, frames), jnp.float32)],
        ),
        out_shape=[shaped(trace_rows, frames)] * 2,
        cost_estimate=cost(6 * trace_rows * rank * frames, 8 * rank * frames),
        compiler_params=grant(6),
        name="traces",
    )(scalars, near, far, keep, arrived, *parts)


def products_call(scalars, near, far, movies, half, count, with_gram):
    chips = len(near)
    trace_rows, frames = near[0].shape
    rank = 2 * chips * trace_rows
    share = rank // count
    pixel_count, pair = movies[0].shape
    part = pixel_count // HALVES
    block = rank
    steps = part // block
    columns = part + (rank if with_gram else 0)
    groups = frames // LANES
    outs = count + 1

    def kernel(scalars, *refs):
        near_refs, far_refs, refs = refs[:chips], refs[chips : 2 * chips], refs[2 * chips :]
        movie_refs = refs[: len(movies)]
        refs = refs[len(movies) :]
        out_refs = refs[:outs]
        full, left, result = refs[outs:]
        step = pl.program_id(0)
        here = scalars[HERE]

        @pl.when(step == 0)
        def _():
            for k in range(chips):
                device = 2 * (scalars[CHIP] ^ k) + scalars[CORE]
                full[pl.ds(pl.multiple_of(device * trace_rows, trace_rows), trace_rows), :] = near_refs[k][...]
                device = 2 * (scalars[CHIP] ^ k) + 1 - scalars[CORE]
                full[pl.ds(pl.multiple_of(device * trace_rows, trace_rows), trace_rows), :] = far_refs[k][...]
            high, low = split(full[...])
            for g in range(groups):
                cut = slice(g * LANES, (g + 1) * LANES)
                at = 2 * g * LANES
                left[0:rank, at : at + LANES] = high[:, cut]
                left[0:rank, at + LANES : at + 2 * LANES] = high[:, cut]
                left[rank:, at : at + LANES] = low[:, cut]
                left[rank:, at + LANES : at + 2 * LANES] = jnp.zeros_like(low[:, cut])

        def emit(total, at):
            result[...] = total
            for k, out_ref in enumerate(out_refs):
                slot = lax.rem(here + k, count) if k < count else scalars[FIRST]
                row = pl.multiple_of(slot * share, share)
                out_ref[:, pl.ds(at, block)] = result[pl.ds(row, share), :]

        total = dot(left[:, 0:pair], movie_refs[0][...], NT)
        for k in range(1, len(movies)):
            total += dot(left[:, k * pair : (k + 1) * pair], movie_refs[k][...], NT)
        emit(fold(total), pl.multiple_of(step * block, block))
        if with_gram:

            @pl.when(step == steps - 1)
            def _():
                high, low = split(full[...])
                both = dot(jnp.concatenate([high, low], axis=0), high, NT)
                cross = both[rank:]
                emit(both[0:rank] + (cross + cross.T), part)

    piece = pl.BlockSpec((trace_rows, frames), lambda j, s: (0, 0))
    return pl.pallas_call(
        kernel,
        grid_spec=pltpu.PrefetchScalarGridSpec(
            num_scalar_prefetch=1,
            grid=(steps,),
            in_specs=[piece] * (2 * chips)
            + [pl.BlockSpec((block, pair), lambda j, s: (half * steps + j, 0))] * len(movies),
            out_specs=[pl.BlockSpec((share, columns), lambda j, s: (0, 0))] * outs,
            scratch_shapes=[
                pltpu.VMEM((rank, frames), jnp.float32),
                pltpu.VMEM((2 * rank, 2 * frames), jnp.bfloat16),
                pltpu.VMEM((rank, block), jnp.float32),
            ],
        ),
        out_shape=[shaped(share, columns)] * outs,
        cost_estimate=cost(8 * rank * part * frames, 4 * part * (frames + rank)),
        compiler_params=grant(10),
        name="products",
    )(scalars, *near, *far, *movies)


def final_call(scalars, own, foot, parts, grams, carried, half):
    share, pixel_count = own.shape
    rank = foot.shape[0] // 2
    part = pixel_count // HALVES
    block = 512
    steps = part // block

    def kernel(scalars, own_ref, foot_ref, *refs):
        part_refs = refs[: len(parts)]
        gram_refs = refs[len(parts) : len(parts) + len(grams)]
        out_ref = refs[-1]
        above = part_refs[0][...]
        for part_ref in part_refs[1:]:
            above = above + part_ref[...]
        gram = gram_refs[0][...]
        for gram_ref in gram_refs[1:]:
            gram = gram + gram_ref[...]
        both = stacked(gram)
        below = fold(dot(both, foot_ref[0:rank, :], NN)) + dot(both[0:share], foot_ref[rank:, :], NN)
        out_ref[...] = own_ref[...] * above / below

    at = half * steps
    in_specs = [
        pl.BlockSpec((share, block), lambda k, s: (0, at + k)),
        pl.BlockSpec((2 * rank, block), lambda k, s: (0, at + k)),
    ]
    in_specs += [pl.BlockSpec((share, block), lambda k, s: (0, k))] * len(parts)
    in_specs += [pl.BlockSpec((share, rank), lambda k, s: (0, part // rank))] * len(grams)
    operands = [scalars, own, foot, *parts, *grams]
    aliases = {}
    if carried is not None:
        operands.append(carried)
        in_specs.append(pl.BlockSpec(memory_space=pl.ANY))
        aliases = {len(operands) - 1: 0}
    return pl.pallas_call(
        kernel,
        grid_spec=pltpu.PrefetchScalarGridSpec(
            num_scalar_prefetch=1,
            grid=(steps,),
            in_specs=in_specs,
            out_specs=pl.BlockSpec((share, block), lambda k, s: (0, at + k)),
        ),
        out_shape=shaped(share, pixel_count),
        input_output_aliases=aliases,
        cost_estimate=cost(6 * share * rank * part, 4 * part * (rank + 5 * share)),
        compiler_params=grant(8),
        name="final",
    )(*operands)


def choose_call(scalars, down, up):
    rows, columns = up.shape
    block = columns // 2

    def kernel(scalars, down_ref, up_ref, out_ref):
        out_ref[...] = jnp.where(scalars[TURNED] == 1, down_ref[...], up_ref[...])

    spec = pl.BlockSpec((rows, block), lambda k, s: (0, k))
    return pl.pallas_call(
        kernel,
        grid_spec=pltpu.PrefetchScalarGridSpec(
            num_scalar_prefetch=1, grid=(2,), in_specs=[spec, spec], out_specs=spec
        ),
        out_shape=shaped(rows, columns),
        cost_estimate=cost(rows * columns, 12 * rows * columns),
        compiler_params=grant(4),
        name="choose",
    )(scalars, down, up)


def line_gather(scalars, block, axis, count):
    up, down = {}, {}
    last_up = last_down = block
    for r in range(1, count):
        up_pairs = [(k, k + 1) for k in range(r - 1, count - 1)]
        down_pairs = [(k + 1, k) for k in range(0, count - r)]
        if r == count - 1 and count != 3:
            merged = choose_call(scalars, last_down, last_up) if count > 2 else block
            last_up = last_down = lax.ppermute(merged, axis, up_pairs + down_pairs)
        else:
            last_up = lax.ppermute(last_up, axis, up_pairs)
            last_down = lax.ppermute(last_down, axis, down_pairs)
        up[r], down[r] = last_up, last_down
    return [(down[s], up[count - s]) for s in range(1, count)]


def line_scatter(blocks, axis, count):
    up_last = down_last = None
    for r in range(1, count):
        up_pairs = [(k, k + 1) for k in range(r)]
        down_pairs = [(count - 1 - k, count - 2 - k) for k in range(r)]
        if r == 1 and count > 3:
            up_last = down_last = lax.ppermute(blocks[count], axis, up_pairs + down_pairs)
            continue
        up_block, down_block = blocks[count - r], blocks[r]
        if r > 1:
            up_block = up_block + up_last
            down_block = down_block + down_last
        up_last = lax.ppermute(up_block, axis, up_pairs)
        down_last = lax.ppermute(down_block, axis, down_pairs)
    return [blocks[0], up_last, down_last]


def compute(raw_movie, footprints, traces):
    rows, cols, frame_count = raw_movie.shape
    pixel_count = rows * cols
    pix_count = lax.axis_size("pix")
    count = lax.axis_size("tm")
    pix = lax.axis_index("pix")
    here = lax.axis_index("tm")
    core = lax.rem(pix, 2)
    trace_rows = traces.shape[0]
    frames = frame_count // CHUNKS
    halo = SUBSTEPS

    def swap(mask):
        return [(k, k ^ mask) for k in range(pix_count)]

    inner = (pix > 0).astype(jnp.int32)
    outer = (pix < pix_count - 1).astype(jnp.int32)
    corner = (lax.rem(pix, GROUP) == GROUP - 1).astype(jnp.int32)
    first_out = lax.rem(here + jnp.where(here == 0, count - 1, 1), count)
    turned = (here == 1).astype(jnp.int32)
    bend_up = (lax.rem(pix, GROUP) == 0) * inner
    flags = scalars = jnp.stack(
        [here, core, lax.div(pix, 2), first_out, turned, inner, outer, bend_up, corner * outer, corner]
    ).astype(jnp.int32)

    pairs = line_gather(scalars, footprints, "tm", count)

    bent = [k for k in range(pix_count - 1) if k % GROUP == GROUP - 1] if pix_count % GROUP == 0 else []
    halos = []
    for c in range(CHUNKS):
        last = c == CHUNKS - 1 and bool(bent)
        send = [(k, k + 1) for k in range(pix_count - 1) if not (last and k in bent)]
        edges = edges_call(flags, raw_movie, halo, c, frames, last)
        detour = None
        if last:
            first = [(k, k + GROUP) for k in bent] + [(k + 1, k + 1 - GROUP) for k in bent]
            second = [(k + GROUP, k + 1) for k in bent] + [(k + 1 - GROUP, k) for k in bent]
            detour = lax.ppermute(edges[2], "pix", first)
            detour = lax.ppermute(detour, "pix", second)
        from_above = lax.ppermute(edges[1], "pix", send)
        from_below = lax.ppermute(edges[0], "pix", [(b, a) for a, b in send])
        halos.append((from_above, from_below, detour))

    near = traces[None]
    mask = 2
    while mask < pix_count:
        near = jnp.concatenate([near, lax.ppermute(near, "pix", swap(mask))], axis=0)
        mask *= 2
    far = lax.ppermute(near, "pix", swap(1))

    current = None
    movies = []
    for c in range(CHUNKS):
        current, pair = diffuse_call(flags, raw_movie, *halos[c], current, c)
        movies.append(pair.reshape(pixel_count, 2 * frames))

    foot, gram = footprints_call(scalars, footprints, pairs)
    keep, send = numerator_call(scalars, foot, movies, gram, trace_rows)
    arrived = lax.ppermute(send, "pix", swap(1))
    parts = []
    for k in range(1, keep.shape[0]):
        parts.append(lax.ppermute(keep[k] + arrived[k], "pix", swap(2 * k)))
    new_traces, again = traces_call(scalars, keep, arrived, parts, near, far)
    near = [again]
    for k in range(1, keep.shape[0]):
        near.append(lax.ppermute(again, "pix", swap(2 * k)))
    far = []
    for piece in near:
        far.append(lax.ppermute(piece, "pix", swap(1)))

    products = []
    for h in range(HALVES):
        products.append(products_call(scalars, near, far, movies, h, count, h == 0))
    sums = [line_scatter(blocks, "tm", count) for blocks in products]
    new_footprints = None
    for h in range(HALVES):
        new_footprints = final_call(scalars, footprints, foot, sums[h], sums[0], new_footprints, h)
    return current, new_footprints, new_traces


def solution(mesh):
    placed = (P("pix", None, "tm"), P("tm", "pix"), P("pix", "tm"))
    return jax.shard_map(
        compute,
        mesh=mesh,
        in_specs=placed,
        out_specs=(P("pix", None, "tm"), P("tm", "pix"), P("pix", "tm")),
        check_vma=False,
    )
```

```python
import jax
import jax.numpy as jnp
from jax import lax
from jax.experimental import pallas as pl
from jax.experimental.pallas import tpu as pltpu
from jax.sharding import PartitionSpec as P


edge_square = 0.25
step_scale = 0.06
SUBSTEPS = 4
LANES = 128
GROUP = 4
HALVES = 2

HERE, CORE, CHIP, FIRST, TURNED, INSIDE, BENT, CORNER = 0, 1, 2, 3, 4, 5, 7, 9

NN = ((1,), (0,))
NT = ((1,), (1,))


def flux_quarter(change):
    return change / (change * change + edge_square)


def split(value):
    high = value.astype(jnp.bfloat16)
    low = (value - high.astype(jnp.float32)).astype(jnp.bfloat16)
    return high, low


def stacked(value):
    return jnp.concatenate(split(value), axis=0)


def dot(left, right, dims):
    return lax.dot_general(left, right, (dims, ((), ())), preferred_element_type=jnp.float32)


def fold(value):
    half = value.shape[0] // 2
    return value[:half] + value[half:]


def grant(mebibytes):
    return pltpu.CompilerParams(vmem_limit_bytes=mebibytes * 1024 * 1024)


def cost(flops, moved):
    return pl.CostEstimate(flops=flops, bytes_accessed=moved, transcendentals=0)


def shaped(*shape, dtype=jnp.float32):
    return jax.ShapeDtypeStruct(shape, dtype)


def edges_call(flags, raw, halo, begin, frames, with_corner):
    rows, cols, _ = raw.shape
    shift = rows - halo
    outs = 3 if with_corner else 2

    def kernel(flags, raw_ref, *refs):
        out_refs, sems = refs[:outs], refs[outs]
        starts = [0, shift, flags[CORNER] * shift]
        copies = [
            pltpu.make_async_copy(
                raw_ref.at[pl.ds(starts[k], halo), :, pl.ds(begin, frames)], out_refs[k], sems.at[k]
            )
            for k in range(outs)
        ]
        for copy in copies:
            copy.start()
        for copy in copies:
            copy.wait()

    block = (halo, cols, frames)
    return pl.pallas_call(
        kernel,
        grid_spec=pltpu.PrefetchScalarGridSpec(
            num_scalar_prefetch=1,
            grid=(1,),
            in_specs=[pl.BlockSpec(memory_space=pltpu.HBM)],
            out_specs=[pl.BlockSpec(block, lambda i, flags: (0, 0, 0))] * outs,
            scratch_shapes=[pltpu.SemaphoreType.DMA((outs,))],
        ),
        out_shape=[shaped(*block)] * outs,
        cost_estimate=cost(1, 2 * outs * halo * cols * frames * 4),
        compiler_params=grant(8),
        name="edges",
    )(flags, raw)


def diffuse_call(flags, raw, halo_up, halo_down, detour, movie, pair, begin, pair_begin, pair_frames):
    rows, cols, total = raw.shape
    halo, _, frames = halo_up.shape
    groups = frames // LANES
    carried = [array for array in (movie, *pair) if array is not None]
    width = 64
    pad = 8
    extended = rows + 2 * halo
    inputs = 3 if detour is None else 4

    def kernel(flags, *refs):
        sources, refs = refs[:inputs], refs[inputs:]
        refs = refs[len(carried) :]
        out_ref, high_ref, low_ref, first_bufs, second_buf, out_bufs, in_sems, out_sems = refs
        group = pl.program_id(0)
        slot = lax.rem(group, 2)
        inside = pl.ds(pad, cols)

        def fetches(at):
            here = lax.rem(at, 2)
            lanes = pl.ds(pl.multiple_of(at * LANES, LANES), LANES)
            wide = pl.ds(pl.multiple_of((begin + at) * LANES, LANES), LANES)

            def one(ref, cut, start, count, part):
                return pltpu.make_async_copy(
                    ref.at[:, :, cut], first_bufs.at[here, pl.ds(start, count), inside, :], in_sems.at[here, part]
                )

            made = [(None, one(sources[0], wide, halo, rows, 0))]
            for part, start, source in ((1, 0, 1), (2, halo + rows, 2)):
                plain = one(sources[source], lanes, start, halo, part)
                if detour is None:
                    made.append((None, plain))
                else:
                    made.append((flags[BENT + part - 1] == 0, plain))
                    made.append((flags[BENT + part - 1] == 1, one(sources[3], lanes, start, halo, part)))
            return made

        def run(at, act):
            for condition, copy in fetches(at):
                if condition is None:
                    act(copy)
                else:
                    pl.when(condition)(lambda copy=copy: act(copy))

        def give(at):
            wide = pl.ds(pl.multiple_of((begin + at) * LANES, LANES), LANES)
            here = lax.rem(at, 2)
            return pltpu.make_async_copy(out_bufs.at[here], out_ref.at[:, :, wide], out_sems.at[here])

        @pl.when(group == 0)
        def _():
            run(group, lambda copy: copy.start())

        @pl.when(group + 1 < groups)
        def _():
            run(group + 1, lambda copy: copy.start())

        zero = jnp.zeros((extended, pad, LANES), jnp.float32)
        first_buf = first_bufs.at[slot]
        for buf in (first_buf, second_buf):
            buf[:, 0:pad, :] = zero
            buf[:, pad + cols :, :] = zero
        run(group, lambda copy: copy.wait())

        @pl.when(group >= 2)
        def _():
            give(group - 2).wait()

        scale_up = step_scale * flags[INSIDE].astype(jnp.float32)
        scale_down = step_scale * flags[INSIDE + 1].astype(jnp.float32)
        head = lax.broadcasted_iota(jnp.int32, (width, LANES), 0) == 0
        bufs = (first_buf, second_buf)
        for step in range(SUBSTEPS):
            src, dst = bufs[step % 2], bufs[1 - step % 2]
            top = step
            middle = range(step + 1, extended - step - 1)

            def tile(j, left_flux):
                base = pl.multiple_of(pad + j * width, 8)
                col = pl.multiple_of(j * width, width)
                kept = []
                current = src[top + 1, pl.ds(base, width), :]
                flux_up = flux_quarter(current - src[top, pl.ds(base, width), :])
                for k, row in enumerate(middle):
                    below = src[row + 1, pl.ds(base, width), :]
                    flux_down = flux_quarter(below - current)
                    flux_right = flux_quarter(src[row, pl.ds(base + 1, width), :] - current)
                    rolled = pltpu.roll(flux_right, 1, 0)
                    flux_left = jnp.where(head, left_flux[k], rolled)
                    scale = step_scale
                    if row < halo:
                        scale = scale_up
                    if row >= halo + rows:
                        scale = scale_down
                    value = current + scale * ((flux_down - flux_up) + (flux_right - flux_left))
                    kept.append(rolled)
                    if step + 1 < SUBSTEPS:
                        dst[row, pl.ds(base, width), :] = value
                    else:
                        out_bufs[slot, row - halo, pl.ds(col, width), :] = value
                        high, low = split(value)
                        high_ref[row - halo, pl.ds(col, width), :] = high
                        low_ref[row - halo, pl.ds(col, width), :] = low
                    current, flux_up = below, flux_down
                return tuple(kept)

            edge = tuple(flux_quarter(src[row, pl.ds(pad, width), :]) for row in middle)
            lax.fori_loop(0, cols // width, tile, edge)
        give(group).start()

        @pl.when(group == groups - 1)
        def _():
            if groups > 1:
                give(group - 1).wait()
            give(group).wait()

    outside = pl.BlockSpec(memory_space=pltpu.HBM)
    operands = [flags, raw, halo_up, halo_down]
    if detour is not None:
        operands.append(detour)
    outputs = [k for k, array in enumerate((movie, *pair)) if array is not None]
    aliases = {len(operands) + k: output for k, output in enumerate(outputs)}
    operands += carried
    padded = (extended, cols + 2 * pad, LANES)
    return pl.pallas_call(
        kernel,
        grid_spec=pltpu.PrefetchScalarGridSpec(
            num_scalar_prefetch=1,
            grid=(groups,),
            in_specs=[outside] * (len(operands) - 1 - len(carried))
            + [pl.BlockSpec(memory_space=pl.ANY)] * len(carried),
            out_specs=[outside] + [pl.BlockSpec((rows, cols, LANES), lambda i, flags: (0, 0, pair_begin + i))] * 2,
            scratch_shapes=[
                pltpu.VMEM((2, *padded), jnp.float32),
                pltpu.VMEM(padded, jnp.float32),
                pltpu.VMEM((2, rows, cols, LANES), jnp.float32),
                pltpu.SemaphoreType.DMA((2, 3)),
                pltpu.SemaphoreType.DMA((2,)),
            ],
        ),
        out_shape=[shaped(rows, cols, total)] + [shaped(rows, cols, pair_frames, dtype=jnp.bfloat16)] * 2,
        input_output_aliases=aliases,
        cost_estimate=cost(rows * cols * groups * LANES * 200, rows * cols * groups * LANES * 16),
        compiler_params=grant(16),
        name="diffuse",
    )(*operands)


def footprints_call(scalars, own, pairs):
    count = len(pairs) + 1
    share, pixel_count = own.shape
    rank = share * count
    block = 512
    steps = pixel_count // block

    def kernel(scalars, *refs):
        own_ref = refs[0]
        pair_refs = [(refs[1 + 2 * k], refs[2 + 2 * k]) for k in range(count - 1)]
        out_ref, gram_ref, total = refs[2 * count - 1 :]
        here = scalars[HERE]
        step = pl.program_id(0)

        def put(slot, value):
            at = pl.multiple_of(lax.rem(here + slot, count) * share, share)
            high, low = split(value)
            out_ref[pl.ds(at, share), :] = high
            out_ref[pl.ds(rank + at, share), :] = low

        put(0, own_ref[...])
        for s, (from_above, from_below) in enumerate(pair_refs, 1):
            put(s, jnp.where(here + s < count, from_above[...], from_below[...]))

        @pl.when(step == 0)
        def _():
            total[...] = jnp.zeros_like(total)

        total[...] += dot(out_ref[...], out_ref[0:rank, :], NT)

        @pl.when(step == steps - 1)
        def _():
            cross = total[rank:, :]
            gram_ref[...] = total[0:rank, :] + (cross + cross.T)

    foot_spec = pl.BlockSpec((share, block), lambda k, s: (0, k))
    flat = [array for pair in pairs for array in pair]
    return pl.pallas_call(
        kernel,
        grid_spec=pltpu.PrefetchScalarGridSpec(
            num_scalar_prefetch=1,
            grid=(steps,),
            in_specs=[foot_spec] * (1 + len(flat)),
            out_specs=[
                pl.BlockSpec((2 * rank, block), lambda k, s: (0, k)),
                pl.BlockSpec((rank, rank), lambda k, s: (0, 0)),
            ],
            scratch_shapes=[pltpu.VMEM((2 * rank, rank), jnp.float32)],
        ),
        out_shape=[shaped(2 * rank, pixel_count, dtype=jnp.bfloat16), shaped(rank, rank)],
        cost_estimate=cost(4 * rank * rank * pixel_count, 8 * rank * pixel_count),
        compiler_params=grant(8),
        name="footprints",
    )(scalars, own, *flat)


def numerator_call(scalars, foot, movies, gram, trace_rows):
    rank = foot.shape[0] // 2
    pixel_count = movies[0][0].shape[0]
    spans = [high.shape[1] for high, _ in movies]
    frames = sum(spans)
    columns = frames + rank
    block = 512
    steps = pixel_count // block
    chips = rank // (2 * trace_rows)

    def kernel(scalars, foot_ref, gram_ref, *refs):
        movie_refs = refs[: 2 * len(movies)]
        keep_ref, send_ref, total = refs[2 * len(movies) :]
        step = pl.program_id(0)

        @pl.when(step == 0)
        def _():
            total[...] = jnp.zeros_like(total)

        for k in range(len(movies)):
            high_ref, low_ref = movie_refs[2 * k : 2 * k + 2]
            part = fold(dot(foot_ref[...], high_ref[...], NN)) + dot(foot_ref[0:rank, :], low_ref[...], NN)
            total[:, sum(spans[:k]) : sum(spans[: k + 1])] += part

        @pl.when(step == steps - 1)
        def _():
            total[:, frames:] = gram_ref[...]
            core = scalars[CORE]
            for k in range(chips):
                chip = scalars[CHIP] ^ k
                mine = pl.multiple_of((2 * chip + core) * trace_rows, trace_rows)
                other = pl.multiple_of((2 * chip + 1 - core) * trace_rows, trace_rows)
                keep_ref[k] = total[pl.ds(mine, trace_rows), :]
                send_ref[k] = total[pl.ds(other, trace_rows), :]

    out_spec = pl.BlockSpec((chips, trace_rows, columns), lambda k, s: (0, 0, 0))
    return pl.pallas_call(
        kernel,
        grid_spec=pltpu.PrefetchScalarGridSpec(
            num_scalar_prefetch=1,
            grid=(steps,),
            in_specs=[
                pl.BlockSpec((2 * rank, block), lambda k, s: (0, k)),
                pl.BlockSpec((rank, rank), lambda k, s: (0, 0)),
            ]
            + [pl.BlockSpec((block, array.shape[1]), lambda k, s: (k, 0)) for movie in movies for array in movie],
            out_specs=[out_spec, out_spec],
            scratch_shapes=[pltpu.VMEM((rank, columns), jnp.float32)],
        ),
        out_shape=[shaped(chips, trace_rows, columns)] * 2,
        cost_estimate=cost(8 * rank * pixel_count * columns, 4 * pixel_count * (rank + columns)),
        compiler_params=grant(10),
        name="numerator",
    )(scalars, foot, gram, *[array for movie in movies for array in movie])


def traces_call(scalars, keep, arrived, parts, gathered):
    _, trace_rows, columns = keep.shape
    frames = gathered[0][0].shape[2]
    rank = columns - frames
    stacks = [stack for stack, _ in gathered]

    def kernel(scalars, *refs):
        stack_refs, refs = refs[: len(stacks)], refs[len(stacks) :]
        part_refs, (out_ref, copy_ref, full) = refs[:-3], refs[-3:]
        for stack_ref, (_, masks) in zip(stack_refs, gathered):
            for k, mask in enumerate(masks):
                device = 2 * (scalars[CHIP] ^ (mask // 2))
                device = device + (1 - scalars[CORE] if mask % 2 else scalars[CORE])
                full[pl.ds(pl.multiple_of(device * trace_rows, trace_rows), trace_rows), :] = stack_ref[k]
        total = part_refs[0][0] + part_refs[1][0]
        for part_ref in part_refs[2:]:
            total = total + part_ref[...]
        gram = stacked(total[:, frames:])
        high, low = split(full[...])
        below = fold(dot(gram, high, NN)) + dot(gram[0:trace_rows], low, NN)
        value = stack_refs[0][0] * total[:, 0:frames] / below
        out_ref[...] = value
        copy_ref[...] = value

    return pl.pallas_call(
        kernel,
        grid_spec=pltpu.PrefetchScalarGridSpec(
            num_scalar_prefetch=1,
            grid=(1,),
            in_specs=[pl.BlockSpec(stack.shape, lambda k, s: (0, 0, 0)) for stack in stacks]
            + [pl.BlockSpec((1, trace_rows, columns), lambda k, s: (0, 0, 0))] * 2
            + [pl.BlockSpec((trace_rows, columns), lambda k, s: (0, 0))] * len(parts),
            out_specs=[pl.BlockSpec((trace_rows, frames), lambda k, s: (0, 0))] * 2,
            scratch_shapes=[pltpu.VMEM((rank, frames), jnp.float32)],
        ),
        out_shape=[shaped(trace_rows, frames)] * 2,
        cost_estimate=cost(6 * trace_rows * rank * frames, 8 * rank * frames),
        compiler_params=grant(6),
        name="traces",
    )(scalars, *stacks, keep, arrived, *parts)


def products_call(scalars, near, far, movies, half, count, with_gram):
    chips = len(near)
    trace_rows, frames = near[0].shape
    rank = 2 * chips * trace_rows
    half_rank = rank // 2
    share = rank // count
    pixel_count = movies[0][0].shape[0]
    spans = [high.shape[1] for high, _ in movies]
    part = pixel_count // HALVES
    block = rank
    steps = part // block
    columns = part + (half_rank if with_gram else 0)
    outs = count + 1

    def kernel(scalars, *refs):
        near_refs, far_refs, refs = refs[:chips], refs[chips : 2 * chips], refs[2 * chips :]
        movie_refs = refs[: 2 * len(movies)]
        refs = refs[2 * len(movies) :]
        out_refs = refs[:outs]
        full, left, result = refs[outs:]
        step = pl.program_id(0)
        here = scalars[HERE]

        @pl.when(step == 0)
        def _():
            for k in range(chips):
                device = 2 * (scalars[CHIP] ^ k) + scalars[CORE]
                full[pl.ds(pl.multiple_of(device * trace_rows, trace_rows), trace_rows), :] = near_refs[k][...]
                device = 2 * (scalars[CHIP] ^ k) + 1 - scalars[CORE]
                full[pl.ds(pl.multiple_of(device * trace_rows, trace_rows), trace_rows), :] = far_refs[k][...]
            left[...] = stacked(full[...])

        def emit(total, at):
            width = total.shape[1]
            result[:, 0:width] = total
            for k, out_ref in enumerate(out_refs):
                slot = lax.rem(here + k, count) if k < count else scalars[FIRST]
                row = pl.multiple_of(slot * share, share)
                out_ref[:, pl.ds(at, width)] = result[pl.ds(row, share), 0:width]

        both = jnp.zeros((2 * rank, block), jnp.float32)
        upper = jnp.zeros((rank, block), jnp.float32)
        for k in range(len(movies)):
            high_ref, low_ref = movie_refs[2 * k : 2 * k + 2]
            cut = slice(sum(spans[:k]), sum(spans[: k + 1]))
            both += dot(left[:, cut], high_ref[...], NT)
            upper += dot(left[0:rank, cut], low_ref[...], NT)
        emit(fold(both) + upper, pl.multiple_of(step * block, block))
        if with_gram:

            @pl.when(step == steps - 1)
            def _():
                at = pl.multiple_of(scalars[CORE] * half_rank, half_rank)
                both = dot(left[...], left[pl.ds(at, half_rank), :], NT)
                upper = dot(left[0:rank, :], left[pl.ds(rank + at, half_rank), :], NT)
                emit(fold(both) + upper, part)

    piece = pl.BlockSpec((trace_rows, frames), lambda j, s: (0, 0))
    return pl.pallas_call(
        kernel,
        grid_spec=pltpu.PrefetchScalarGridSpec(
            num_scalar_prefetch=1,
            grid=(steps,),
            in_specs=[piece] * (2 * chips)
            + [
                pl.BlockSpec((block, array.shape[1]), lambda j, s: (half * steps + j, 0))
                for movie in movies
                for array in movie
            ],
            out_specs=[pl.BlockSpec((share, columns), lambda j, s: (0, 0))] * outs,
            scratch_shapes=[
                pltpu.VMEM((rank, frames), jnp.float32),
                pltpu.VMEM((2 * rank, frames), jnp.bfloat16),
                pltpu.VMEM((rank, block), jnp.float32),
            ],
        ),
        out_shape=[shaped(share, columns)] * outs,
        cost_estimate=cost(8 * rank * part * frames, 4 * part * (frames + rank)),
        compiler_params=grant(10),
        name="products",
    )(scalars, *near, *far, *[array for movie in movies for array in movie])


def final_call(scalars, own, foot, parts, gram_mine, gram_other, carried, half):
    share, pixel_count = own.shape
    rank = foot.shape[0] // 2
    part = pixel_count // HALVES
    block = 512
    steps = part // block

    def kernel(scalars, own_ref, foot_ref, *refs):
        part_refs = refs[: len(parts)]
        mine, other = refs[len(parts)][...], refs[len(parts) + 1][...]
        out_ref = refs[-1]
        above = part_refs[0][...]
        for part_ref in part_refs[1:]:
            above = above + part_ref[...]
        first = scalars[CORE] == 0
        gram = jnp.concatenate([jnp.where(first, mine, other), jnp.where(first, other, mine)], axis=1)
        both = stacked(gram)
        below = fold(dot(both, foot_ref[0:rank, :], NN)) + dot(both[0:share], foot_ref[rank:, :], NN)
        out_ref[...] = own_ref[...] * above / below

    at = half * steps
    in_specs = [
        pl.BlockSpec((share, block), lambda k, s: (0, at + k)),
        pl.BlockSpec((2 * rank, block), lambda k, s: (0, at + k)),
    ]
    in_specs += [pl.BlockSpec((share, block), lambda k, s: (0, k))] * len(parts)
    in_specs += [pl.BlockSpec((share, rank // 2), lambda k, s: (0, 0))] * 2
    operands = [scalars, own, foot, *parts, gram_mine, gram_other]
    aliases = {}
    if carried is not None:
        operands.append(carried)
        in_specs.append(pl.BlockSpec(memory_space=pl.ANY))
        aliases = {len(operands) - 1: 0}
    return pl.pallas_call(
        kernel,
        grid_spec=pltpu.PrefetchScalarGridSpec(
            num_scalar_prefetch=1,
            grid=(steps,),
            in_specs=in_specs,
            out_specs=pl.BlockSpec((share, block), lambda k, s: (0, at + k)),
        ),
        out_shape=shaped(share, pixel_count),
        input_output_aliases=aliases,
        cost_estimate=cost(6 * share * rank * part, 4 * part * (rank + 5 * share)),
        compiler_params=grant(8),
        name="final",
    )(*operands)


def choose_call(scalars, down, up):
    rows, columns = up.shape
    block = columns // 2

    def kernel(scalars, down_ref, up_ref, out_ref):
        out_ref[...] = jnp.where(scalars[TURNED] == 1, down_ref[...], up_ref[...])

    spec = pl.BlockSpec((rows, block), lambda k, s: (0, k))
    return pl.pallas_call(
        kernel,
        grid_spec=pltpu.PrefetchScalarGridSpec(
            num_scalar_prefetch=1, grid=(2,), in_specs=[spec, spec], out_specs=spec
        ),
        out_shape=shaped(rows, columns),
        cost_estimate=cost(rows * columns, 12 * rows * columns),
        compiler_params=grant(4),
        name="choose",
    )(scalars, down, up)


def line_gather(scalars, block, axis, count):
    up, down = {}, {}
    last_up = last_down = block
    for r in range(1, count):
        up_pairs = [(k, k + 1) for k in range(r - 1, count - 1)]
        down_pairs = [(k + 1, k) for k in range(0, count - r)]
        if r == count - 1 and count != 3:
            merged = choose_call(scalars, last_down, last_up) if count > 2 else block
            last_up = last_down = lax.ppermute(merged, axis, up_pairs + down_pairs)
        else:
            last_up = lax.ppermute(last_up, axis, up_pairs)
            last_down = lax.ppermute(last_down, axis, down_pairs)
        up[r], down[r] = last_up, last_down
    return [(down[s], up[count - s]) for s in range(1, count)]


def line_scatter(blocks, axis, count):
    up_last = down_last = None
    for r in range(1, count):
        up_pairs = [(k, k + 1) for k in range(r)]
        down_pairs = [(count - 1 - k, count - 2 - k) for k in range(r)]
        if r == 1 and count > 3:
            up_last = down_last = lax.ppermute(blocks[count], axis, up_pairs + down_pairs)
            continue
        up_block, down_block = blocks[count - r], blocks[r]
        if r > 1:
            up_block = up_block + up_last
            down_block = down_block + down_last
        up_last = lax.ppermute(up_block, axis, up_pairs)
        down_last = lax.ppermute(down_block, axis, down_pairs)
    return [blocks[0], up_last, down_last]


def compute(raw_movie, footprints, traces):
    rows, cols, frame_count = raw_movie.shape
    pixel_count = rows * cols
    pix_count = lax.axis_size("pix")
    count = lax.axis_size("tm")
    pix = lax.axis_index("pix")
    here = lax.axis_index("tm")
    core = lax.rem(pix, 2)
    trace_rows = traces.shape[0]
    blocks = frame_count // LANES
    quarter = max(blocks // 4, 1)
    widths = [2 * quarter, blocks - 2 * quarter]
    halo = SUBSTEPS

    def swap(mask):
        return [(k, k ^ mask) for k in range(pix_count)]

    inner = (pix > 0).astype(jnp.int32)
    outer = (pix < pix_count - 1).astype(jnp.int32)
    corner = (lax.rem(pix, GROUP) == GROUP - 1).astype(jnp.int32)
    first_out = lax.rem(here + jnp.where(here == 0, count - 1, 1), count)
    turned = (here == 1).astype(jnp.int32)
    bend_up = (lax.rem(pix, GROUP) == 0) * inner
    flags = scalars = jnp.stack(
        [here, core, lax.div(pix, 2), first_out, turned, inner, outer, bend_up, corner * outer, corner]
    ).astype(jnp.int32)

    pairs = line_gather(scalars, footprints, "tm", count)

    bent = [k for k in range(pix_count - 1) if k % GROUP == GROUP - 1] if pix_count % GROUP == 0 else []
    halos = []
    for c, width in enumerate(widths):
        begin = sum(widths[:c]) * LANES
        last = c == len(widths) - 1 and bool(bent)
        send = [(k, k + 1) for k in range(pix_count - 1) if not (last and k in bent)]
        if c == 0:
            edges = raw_movie[:halo, :, : width * LANES], raw_movie[rows - halo :, :, : width * LANES]
        else:
            edges = edges_call(flags, raw_movie, halo, begin, width * LANES, last)
        detour = None
        if last:
            first = [(k, k + GROUP) for k in bent] + [(k + 1, k + 1 - GROUP) for k in bent]
            second = [(k + GROUP, k + 1) for k in bent] + [(k + 1 - GROUP, k) for k in bent]
            detour = lax.ppermute(edges[2], "pix", first)
            detour = lax.ppermute(detour, "pix", second)
        from_above = lax.ppermute(edges[1], "pix", send)
        from_below = lax.ppermute(edges[0], "pix", [(b, a) for a, b in send])
        halos.append((from_above, from_below, detour))

    held, masks = traces[None], [0]
    hops = [mask for mask in (4, 8, 16, 32, 64, 1) if mask < pix_count]
    for mask in hops:
        held = jnp.concatenate([held, lax.ppermute(held, "pix", swap(mask))], axis=0)
        masks = masks + [mask ^ m for m in masks]
    gathered = [(held, masks)]
    if pix_count > 2:
        gathered.append((lax.ppermute(held, "pix", swap(2)), [2 ^ m for m in masks]))

    current = None
    movies = []
    for members in ((0,), (1,)):
        pair = (None, None)
        pair_frames = sum(widths[c] for c in members) * LANES
        pair_begin = 0
        for c in members:
            current, *pair = diffuse_call(
                flags, raw_movie, *halos[c], current, pair, sum(widths[:c]), pair_begin, pair_frames
            )
            pair_begin += widths[c]
        movies.append(tuple(array.reshape(pixel_count, pair_frames) for array in pair))

    foot, gram = footprints_call(scalars, footprints, pairs)
    keep, send = numerator_call(scalars, foot, movies, gram, trace_rows)
    arrived = lax.ppermute(send, "pix", swap(1))
    parts = []
    for k in range(1, keep.shape[0]):
        parts.append(lax.ppermute(keep[k] + arrived[k], "pix", swap(2 * k)))
    new_traces, again = traces_call(scalars, keep, arrived, parts, gathered)
    near = [again]
    for k in range(1, keep.shape[0]):
        near.append(lax.ppermute(again, "pix", swap(2 * k)))
    far = []
    for piece in near:
        far.append(lax.ppermute(piece, "pix", swap(1)))

    products = []
    for h in range(HALVES):
        products.append(products_call(scalars, near, far, movies, h, count, h == 0))
    sums = [line_scatter(blocks, "tm", count) for blocks in products]
    part = pixel_count // HALVES
    gram_mine = sum(array[:, part:] for array in sums[0])
    gram_other = lax.ppermute(gram_mine, "pix", swap(1))
    new_footprints = None
    for h in range(HALVES):
        new_footprints = final_call(
            scalars, footprints, foot, sums[h], gram_mine, gram_other, new_footprints, h
        )
    return current, new_footprints, new_traces


def solution(mesh):
    placed = (P("pix", None, "tm"), P("tm", "pix"), P("pix", "tm"))
    return jax.shard_map(
        compute,
        mesh=mesh,
        in_specs=placed,
        out_specs=(P("pix", None, "tm"), P("tm", "pix"), P("pix", "tm")),
        check_vma=False,
    )
```

```python
import jax
import jax.numpy as jnp
from jax import lax
from jax.experimental import pallas as pl
from jax.experimental.pallas import tpu as pltpu
from jax.sharding import PartitionSpec as P


edge_square = 0.25
step_scale = 0.06
SUBSTEPS = 4
LANES = 128
GROUP = 4
HALVES = 2

HERE, CORE, CHIP, TURNED, INSIDE, BENT = 0, 1, 2, 3, 4, 6

NN = ((1,), (0,))
NT = ((1,), (1,))


def flux_quarter(change):
    return change / (change * change + edge_square)


def split(value):
    high = value.astype(jnp.bfloat16)
    low = (value - high.astype(jnp.float32)).astype(jnp.bfloat16)
    return high, low


def stacked(value):
    return jnp.concatenate(split(value), axis=0)


def dot(left, right, dims):
    return lax.dot_general(left, right, (dims, ((), ())), preferred_element_type=jnp.float32)


def fold(value):
    half = value.shape[0] // 2
    return value[:half] + value[half:]


def grant(mebibytes):
    return pltpu.CompilerParams(vmem_limit_bytes=mebibytes * 1024 * 1024)


def cost(flops, moved):
    return pl.CostEstimate(flops=flops, bytes_accessed=moved, transcendentals=0)


def shaped(*shape, dtype=jnp.float32):
    return jax.ShapeDtypeStruct(shape, dtype)


def edges_call(flags, raw, halo, begin, frames):
    rows, cols, _ = raw.shape
    shift = rows - halo

    def kernel(flags, raw_ref, inner_ref, outer_ref, sems):
        core = flags[CORE]
        lanes = pl.ds(begin, frames)
        copies = [
            pltpu.make_async_copy(raw_ref.at[pl.ds(start, halo), :, lanes], out_ref, sems.at[k])
            for k, (start, out_ref) in enumerate((((1 - core) * shift, inner_ref), (core * shift, outer_ref)))
        ]
        for copy in copies:
            copy.start()
        for copy in copies:
            copy.wait()

    block = (halo, cols, frames)
    return pl.pallas_call(
        kernel,
        grid_spec=pltpu.PrefetchScalarGridSpec(
            num_scalar_prefetch=1,
            grid=(1,),
            in_specs=[pl.BlockSpec(memory_space=pltpu.HBM)],
            out_specs=[pl.BlockSpec(block, lambda i, flags: (0, 0, 0))] * 2,
            scratch_shapes=[pltpu.SemaphoreType.DMA((2,))],
        ),
        out_shape=[shaped(*block)] * 2,
        cost_estimate=cost(1, 4 * halo * cols * frames * 4),
        compiler_params=grant(8),
        name="edges",
    )(flags, raw)


def diffuse_call(flags, raw, halo_inner, halo_outer, detour, movie, pair, begin, pair_begin, pair_frames):
    rows, cols, total = raw.shape
    halo, _, frames = halo_inner.shape
    groups = frames // LANES
    carried = [array for array in (movie, *pair) if array is not None]
    width = 64
    pad = 8
    extended = rows + 2 * halo
    inputs = 3 if detour is None else 4

    def kernel(flags, *refs):
        sources, refs = refs[:inputs], refs[inputs:]
        refs = refs[len(carried) :]
        out_ref, high_ref, low_ref, first_bufs, second_buf, out_bufs, in_sems, out_sems = refs
        group = pl.program_id(0)
        slot = lax.rem(group, 2)
        inside = pl.ds(pad, cols)

        def fetches(at):
            here = lax.rem(at, 2)
            lanes = pl.ds(pl.multiple_of(at * LANES, LANES), LANES)
            wide = pl.ds(pl.multiple_of((begin + at) * LANES, LANES), LANES)

            def one(ref, cut, start, count, part):
                return pltpu.make_async_copy(
                    ref.at[:, :, cut], first_bufs.at[here, pl.ds(start, count), inside, :], in_sems.at[here, part]
                )

            far_side = halo + rows
            inner_at = (1 - flags[CORE]) * far_side
            outer_at = flags[CORE] * far_side
            made = [
                (None, one(sources[0], wide, halo, rows, 0)),
                (None, one(sources[1], lanes, inner_at, halo, 1)),
            ]
            plain = one(sources[2], lanes, outer_at, halo, 2)
            if detour is None:
                made.append((None, plain))
            else:
                made.append((flags[BENT] == 0, plain))
                made.append((flags[BENT] == 1, one(sources[3], lanes, outer_at, halo, 2)))
            return made

        def run(at, act):
            for condition, copy in fetches(at):
                if condition is None:
                    act(copy)
                else:
                    pl.when(condition)(lambda copy=copy: act(copy))

        def give(at):
            wide = pl.ds(pl.multiple_of((begin + at) * LANES, LANES), LANES)
            here = lax.rem(at, 2)
            return pltpu.make_async_copy(out_bufs.at[here], out_ref.at[:, :, wide], out_sems.at[here])

        @pl.when(group == 0)
        def _():
            run(group, lambda copy: copy.start())

        @pl.when(group + 1 < groups)
        def _():
            run(group + 1, lambda copy: copy.start())

        zero = jnp.zeros((extended, pad, LANES), jnp.float32)
        first_buf = first_bufs.at[slot]
        for buf in (first_buf, second_buf):
            buf[:, 0:pad, :] = zero
            buf[:, pad + cols :, :] = zero
        run(group, lambda copy: copy.wait())

        @pl.when(group >= 2)
        def _():
            give(group - 2).wait()

        scale_up = step_scale * flags[INSIDE].astype(jnp.float32)
        scale_down = step_scale * flags[INSIDE + 1].astype(jnp.float32)
        head = lax.broadcasted_iota(jnp.int32, (width, LANES), 0) == 0
        bufs = (first_buf, second_buf)
        for step in range(SUBSTEPS):
            src, dst = bufs[step % 2], bufs[1 - step % 2]
            top = step
            middle = range(step + 1, extended - step - 1)

            def tile(j, left_flux):
                base = pl.multiple_of(pad + j * width, 8)
                col = pl.multiple_of(j * width, width)
                kept = []
                current = src[top + 1, pl.ds(base, width), :]
                flux_up = flux_quarter(current - src[top, pl.ds(base, width), :])
                for k, row in enumerate(middle):
                    below = src[row + 1, pl.ds(base, width), :]
                    flux_down = flux_quarter(below - current)
                    flux_right = flux_quarter(src[row, pl.ds(base + 1, width), :] - current)
                    rolled = pltpu.roll(flux_right, 1, 0)
                    flux_left = jnp.where(head, left_flux[k], rolled)
                    scale = step_scale
                    if row < halo:
                        scale = scale_up
                    if row >= halo + rows:
                        scale = scale_down
                    value = current + scale * ((flux_down - flux_up) + (flux_right - flux_left))
                    kept.append(rolled)
                    if step + 1 < SUBSTEPS:
                        dst[row, pl.ds(base, width), :] = value
                    else:
                        out_bufs[slot, row - halo, pl.ds(col, width), :] = value
                        high, low = split(value)
                        high_ref[row - halo, pl.ds(col, width), :] = high
                        low_ref[row - halo, pl.ds(col, width), :] = low
                    current, flux_up = below, flux_down
                return tuple(kept)

            edge = tuple(flux_quarter(src[row, pl.ds(pad, width), :]) for row in middle)
            lax.fori_loop(0, cols // width, tile, edge)
        give(group).start()

        @pl.when(group == groups - 1)
        def _():
            if groups > 1:
                give(group - 1).wait()
            give(group).wait()

    outside = pl.BlockSpec(memory_space=pltpu.HBM)
    operands = [flags, raw, halo_inner, halo_outer]
    if detour is not None:
        operands.append(detour)
    outputs = [k for k, array in enumerate((movie, *pair)) if array is not None]
    aliases = {len(operands) + k: output for k, output in enumerate(outputs)}
    operands += carried
    padded = (extended, cols + 2 * pad, LANES)
    return pl.pallas_call(
        kernel,
        grid_spec=pltpu.PrefetchScalarGridSpec(
            num_scalar_prefetch=1,
            grid=(groups,),
            in_specs=[outside] * (len(operands) - 1 - len(carried))
            + [pl.BlockSpec(memory_space=pl.ANY)] * len(carried),
            out_specs=[outside] + [pl.BlockSpec((rows, cols, LANES), lambda i, flags: (0, 0, pair_begin + i))] * 2,
            scratch_shapes=[
                pltpu.VMEM((2, *padded), jnp.float32),
                pltpu.VMEM(padded, jnp.float32),
                pltpu.VMEM((2, rows, cols, LANES), jnp.float32),
                pltpu.SemaphoreType.DMA((2, 3)),
                pltpu.SemaphoreType.DMA((2,)),
            ],
        ),
        out_shape=[shaped(rows, cols, total)] + [shaped(rows, cols, pair_frames, dtype=jnp.bfloat16)] * 2,
        input_output_aliases=aliases,
        cost_estimate=cost(rows * cols * groups * LANES * 200, rows * cols * groups * LANES * 16),
        compiler_params=grant(16),
        name="diffuse",
    )(*operands)


def footprints_call(scalars, own, entries):
    count = len(entries) + 1
    share, pixel_count = own.shape
    rank = share * count
    block = 512
    steps = pixel_count // block

    def kernel(scalars, *refs):
        own_ref = refs[0]
        entry_refs = [(refs[1 + 2 * k], refs[2 + 2 * k]) for k in range(count - 1)]
        out_ref, gram_ref, total = refs[2 * count - 1 :]
        here = scalars[HERE]
        step = pl.program_id(0)

        def put(place, value):
            at = pl.multiple_of(place * share, share)
            high, low = split(value)
            out_ref[pl.ds(at, share), :] = high
            out_ref[pl.ds(rank + at, share), :] = low

        put(here, own_ref[...])
        for (first_ref, second_ref), (_, _, test, place) in zip(entry_refs, entries):
            put(place(here), jnp.where(test(here), first_ref[...], second_ref[...]))

        @pl.when(step == 0)
        def _():
            total[...] = jnp.zeros_like(total)

        total[...] += dot(out_ref[...], out_ref[0:rank, :], NT)

        @pl.when(step == steps - 1)
        def _():
            cross = total[rank:, :]
            gram_ref[...] = total[0:rank, :] + (cross + cross.T)

    foot_spec = pl.BlockSpec((share, block), lambda k, s: (0, k))
    flat = [array for entry in entries for array in entry[:2]]
    return pl.pallas_call(
        kernel,
        grid_spec=pltpu.PrefetchScalarGridSpec(
            num_scalar_prefetch=1,
            grid=(steps,),
            in_specs=[foot_spec] * (1 + len(flat)),
            out_specs=[
                pl.BlockSpec((2 * rank, block), lambda k, s: (0, k)),
                pl.BlockSpec((rank, rank), lambda k, s: (0, 0)),
            ],
            scratch_shapes=[pltpu.VMEM((2 * rank, rank), jnp.float32)],
        ),
        out_shape=[shaped(2 * rank, pixel_count, dtype=jnp.bfloat16), shaped(rank, rank)],
        cost_estimate=cost(4 * rank * rank * pixel_count, 8 * rank * pixel_count),
        compiler_params=grant(8),
        name="footprints",
    )(scalars, own, *flat)


def numerator_call(scalars, foot, movies, gram, trace_rows):
    rank = foot.shape[0] // 2
    pixel_count = movies[0][0].shape[0]
    spans = [high.shape[1] for high, _ in movies]
    frames = sum(spans)
    columns = frames + rank
    block = 512
    steps = pixel_count // block
    chips = rank // (2 * trace_rows)

    def kernel(scalars, foot_ref, gram_ref, *refs):
        movie_refs = refs[: 2 * len(movies)]
        keep_ref, send_ref, total = refs[2 * len(movies) :]
        step = pl.program_id(0)

        @pl.when(step == 0)
        def _():
            total[...] = jnp.zeros_like(total)

        for k in range(len(movies)):
            high_ref, low_ref = movie_refs[2 * k : 2 * k + 2]
            part = fold(dot(foot_ref[...], high_ref[...], NN)) + dot(foot_ref[0:rank, :], low_ref[...], NN)
            total[:, sum(spans[:k]) : sum(spans[: k + 1])] += part

        @pl.when(step == steps - 1)
        def _():
            total[:, frames:] = gram_ref[...]
            core = scalars[CORE]
            for k in range(chips):
                chip = scalars[CHIP] ^ k
                mine = pl.multiple_of((2 * chip + core) * trace_rows, trace_rows)
                other = pl.multiple_of((2 * chip + 1 - core) * trace_rows, trace_rows)
                keep_ref[k] = total[pl.ds(mine, trace_rows), :]
                send_ref[k] = total[pl.ds(other, trace_rows), :]

    out_spec = pl.BlockSpec((chips, trace_rows, columns), lambda k, s: (0, 0, 0))
    return pl.pallas_call(
        kernel,
        grid_spec=pltpu.PrefetchScalarGridSpec(
            num_scalar_prefetch=1,
            grid=(steps,),
            in_specs=[
                pl.BlockSpec((2 * rank, block), lambda k, s: (0, k)),
                pl.BlockSpec((rank, rank), lambda k, s: (0, 0)),
            ]
            + [pl.BlockSpec((block, array.shape[1]), lambda k, s: (k, 0)) for movie in movies for array in movie],
            out_specs=[out_spec, out_spec],
            scratch_shapes=[pltpu.VMEM((rank, columns), jnp.float32)],
        ),
        out_shape=[shaped(chips, trace_rows, columns)] * 2,
        cost_estimate=cost(8 * rank * pixel_count * columns, 4 * pixel_count * (rank + columns)),
        compiler_params=grant(10),
        name="numerator",
    )(scalars, foot, gram, *[array for movie in movies for array in movie])


def traces_call(scalars, keep, arrived, parts, gathered):
    _, trace_rows, columns = keep.shape
    frames = gathered[0][0].shape[2]
    rank = columns - frames
    stacks = [stack for stack, _ in gathered]

    def kernel(scalars, *refs):
        stack_refs, refs = refs[: len(stacks)], refs[len(stacks) :]
        part_refs, (out_ref, copy_ref, full) = refs[:-3], refs[-3:]
        for stack_ref, (_, masks) in zip(stack_refs, gathered):
            for k, mask in enumerate(masks):
                device = 2 * (scalars[CHIP] ^ (mask // 2))
                device = device + (1 - scalars[CORE] if mask % 2 else scalars[CORE])
                full[pl.ds(pl.multiple_of(device * trace_rows, trace_rows), trace_rows), :] = stack_ref[k]
        total = part_refs[0][0] + part_refs[1][0]
        for part_ref in part_refs[2:]:
            total = total + part_ref[...]
        gram = stacked(total[:, frames:])
        high, low = split(full[...])
        below = fold(dot(gram, high, NN)) + dot(gram[0:trace_rows], low, NN)
        value = stack_refs[0][0] * total[:, 0:frames] / below
        out_ref[...] = value
        copy_ref[...] = value

    return pl.pallas_call(
        kernel,
        grid_spec=pltpu.PrefetchScalarGridSpec(
            num_scalar_prefetch=1,
            grid=(1,),
            in_specs=[pl.BlockSpec(stack.shape, lambda k, s: (0, 0, 0)) for stack in stacks]
            + [pl.BlockSpec((1, trace_rows, columns), lambda k, s: (0, 0, 0))] * 2
            + [pl.BlockSpec((trace_rows, columns), lambda k, s: (0, 0))] * len(parts),
            out_specs=[pl.BlockSpec((trace_rows, frames), lambda k, s: (0, 0))] * 2,
            scratch_shapes=[pltpu.VMEM((rank, frames), jnp.float32)],
        ),
        out_shape=[shaped(trace_rows, frames)] * 2,
        cost_estimate=cost(6 * trace_rows * rank * frames, 8 * rank * frames),
        compiler_params=grant(6),
        name="traces",
    )(scalars, *stacks, keep, arrived, *parts)


def products_call(scalars, near, far, movies, half, count, places, with_gram):
    chips = len(near)
    trace_rows, frames = near[0].shape
    rank = 2 * chips * trace_rows
    half_rank = rank // 2
    share = rank // count
    pixel_count = movies[0][0].shape[0]
    spans = [high.shape[1] for high, _ in movies]
    part = pixel_count // HALVES
    block = rank
    steps = part // block
    columns = part + (half_rank if with_gram else 0)
    outs = len(places)

    def kernel(scalars, *refs):
        near_refs, far_refs, refs = refs[:chips], refs[chips : 2 * chips], refs[2 * chips :]
        movie_refs = refs[: 2 * len(movies)]
        refs = refs[2 * len(movies) :]
        out_refs = refs[:outs]
        full, left, result = refs[outs:]
        step = pl.program_id(0)
        here = scalars[HERE]

        @pl.when(step == 0)
        def _():
            for k in range(chips):
                device = 2 * (scalars[CHIP] ^ k) + scalars[CORE]
                full[pl.ds(pl.multiple_of(device * trace_rows, trace_rows), trace_rows), :] = near_refs[k][...]
                device = 2 * (scalars[CHIP] ^ k) + 1 - scalars[CORE]
                full[pl.ds(pl.multiple_of(device * trace_rows, trace_rows), trace_rows), :] = far_refs[k][...]
            left[...] = stacked(full[...])

        def emit(total, at):
            width = total.shape[1]
            result[:, 0:width] = total
            for k, out_ref in enumerate(out_refs):
                row = pl.multiple_of(places[k](here) * share, share)
                out_ref[:, pl.ds(at, width)] = result[pl.ds(row, share), 0:width]

        both = jnp.zeros((2 * rank, block), jnp.float32)
        upper = jnp.zeros((rank, block), jnp.float32)
        for k in range(len(movies)):
            high_ref, low_ref = movie_refs[2 * k : 2 * k + 2]
            cut = slice(sum(spans[:k]), sum(spans[: k + 1]))
            both += dot(left[:, cut], high_ref[...], NT)
            upper += dot(left[0:rank, cut], low_ref[...], NT)
        emit(fold(both) + upper, pl.multiple_of(step * block, block))
        if with_gram:

            @pl.when(step == steps - 1)
            def _():
                at = pl.multiple_of(scalars[CORE] * half_rank, half_rank)
                both = dot(left[...], left[pl.ds(at, half_rank), :], NT)
                upper = dot(left[0:rank, :], left[pl.ds(rank + at, half_rank), :], NT)
                emit(fold(both) + upper, part)

    piece = pl.BlockSpec((trace_rows, frames), lambda j, s: (0, 0))
    return pl.pallas_call(
        kernel,
        grid_spec=pltpu.PrefetchScalarGridSpec(
            num_scalar_prefetch=1,
            grid=(steps,),
            in_specs=[piece] * (2 * chips)
            + [
                pl.BlockSpec((block, array.shape[1]), lambda j, s: (half * steps + j, 0))
                for movie in movies
                for array in movie
            ],
            out_specs=[pl.BlockSpec((share, columns), lambda j, s: (0, 0))] * outs,
            scratch_shapes=[
                pltpu.VMEM((rank, frames), jnp.float32),
                pltpu.VMEM((2 * rank, frames), jnp.bfloat16),
                pltpu.VMEM((rank, block), jnp.float32),
            ],
        ),
        out_shape=[shaped(share, columns)] * outs,
        cost_estimate=cost(8 * rank * part * frames, 4 * part * (frames + rank)),
        compiler_params=grant(10),
        name="products",
    )(scalars, *near, *far, *[array for movie in movies for array in movie])


def final_call(scalars, own, foot, parts, gram_mine, gram_other, carried, half):
    share, pixel_count = own.shape
    rank = foot.shape[0] // 2
    part = pixel_count // HALVES
    block = 512
    steps = part // block

    def kernel(scalars, own_ref, foot_ref, *refs):
        part_refs = refs[: len(parts)]
        mine, other = refs[len(parts)][...], refs[len(parts) + 1][...]
        out_ref = refs[-1]
        above = part_refs[0][...]
        for part_ref in part_refs[1:]:
            above = above + part_ref[...]
        first = scalars[CORE] == 0
        gram = jnp.concatenate([jnp.where(first, mine, other), jnp.where(first, other, mine)], axis=1)
        both = stacked(gram)
        below = fold(dot(both, foot_ref[0:rank, :], NN)) + dot(both[0:share], foot_ref[rank:, :], NN)
        out_ref[...] = own_ref[...] * above / below

    at = half * steps
    in_specs = [
        pl.BlockSpec((share, block), lambda k, s: (0, at + k)),
        pl.BlockSpec((2 * rank, block), lambda k, s: (0, at + k)),
    ]
    in_specs += [pl.BlockSpec((share, block), lambda k, s: (0, k))] * len(parts)
    in_specs += [pl.BlockSpec((share, rank // 2), lambda k, s: (0, 0))] * 2
    operands = [scalars, own, foot, *parts, gram_mine, gram_other]
    aliases = {}
    if carried is not None:
        operands.append(carried)
        in_specs.append(pl.BlockSpec(memory_space=pl.ANY))
        aliases = {len(operands) - 1: 0}
    return pl.pallas_call(
        kernel,
        grid_spec=pltpu.PrefetchScalarGridSpec(
            num_scalar_prefetch=1,
            grid=(steps,),
            in_specs=in_specs,
            out_specs=pl.BlockSpec((share, block), lambda k, s: (0, at + k)),
        ),
        out_shape=shaped(share, pixel_count),
        input_output_aliases=aliases,
        cost_estimate=cost(6 * share * rank * part, 4 * part * (rank + 5 * share)),
        compiler_params=grant(8),
        name="final",
    )(*operands)


def choose_call(scalars, down, up):
    rows, columns = up.shape
    block = columns // 2

    def kernel(scalars, down_ref, up_ref, out_ref):
        out_ref[...] = jnp.where(scalars[TURNED] == 1, down_ref[...], up_ref[...])

    spec = pl.BlockSpec((rows, block), lambda k, s: (0, k))
    return pl.pallas_call(
        kernel,
        grid_spec=pltpu.PrefetchScalarGridSpec(
            num_scalar_prefetch=1, grid=(2,), in_specs=[spec, spec], out_specs=spec
        ),
        out_shape=shaped(rows, columns),
        cost_estimate=cost(rows * columns, 12 * rows * columns),
        compiler_params=grant(4),
        name="choose",
    )(scalars, down, up)


def line_gather(scalars, block, axis, count):
    if count == 4:
        middle = [(1, 2), (2, 1)]
        outward = [(1, 0), (2, 3)]
        near = lax.ppermute(block, axis, [(k, k ^ 1) for k in range(count)])
        across = lax.ppermute(block, axis, middle)
        far = lax.ppermute(near, axis, middle)
        out_across = lax.ppermute(across, axis, outward)
        out_far = lax.ppermute(far, axis, outward)

        def between(here):
            return (here == 1) | (here == 2)

        return [
            (near, near, between, lambda here: here ^ 1),
            (across, out_across, between, lambda here: jnp.where(here < 2, 2, 1)),
            (far, out_far, between, lambda here: jnp.where(here < 2, 3, 0)),
        ]
    up, down = {}, {}
    last_up = last_down = block
    for r in range(1, count):
        up_pairs = [(k, k + 1) for k in range(r - 1, count - 1)]
        down_pairs = [(k + 1, k) for k in range(0, count - r)]
        if r == count - 1 and count != 3:
            merged = choose_call(scalars, last_down, last_up) if count > 2 else block
            last_up = last_down = lax.ppermute(merged, axis, up_pairs + down_pairs)
        else:
            last_up = lax.ppermute(last_up, axis, up_pairs)
            last_down = lax.ppermute(last_down, axis, down_pairs)
        up[r], down[r] = last_up, last_down
    return [
        (down[s], up[count - s], lambda here, s=s: here + s < count, lambda here, s=s: lax.rem(here + s, count))
        for s in range(1, count)
    ]


def scatter_places(count):
    if count == 4:
        return [
            lambda here: here,
            lambda here: here ^ 1,
            lambda here: 3 - here,
            lambda here: lax.rem(here + 2, count),
        ]
    slots = [lambda here, s=s: lax.rem(here + s, count) for s in range(count)]
    return slots + [lambda here: lax.rem(here + jnp.where(here == 0, count - 1, 1), count)]


def line_scatter(blocks, axis, count):
    if count == 4:
        own, beside, opposite, remaining = blocks
        inward = [(0, 1), (3, 2)]
        middle = [(1, 2), (2, 1)]
        first = lax.ppermute(opposite, axis, inward)
        second = lax.ppermute(remaining, axis, inward)
        third = lax.ppermute(remaining + first, axis, middle)
        fourth = lax.ppermute(beside + third, axis, [(k, k ^ 1) for k in range(count)])
        fifth = lax.ppermute(opposite + second, axis, middle)
        return [own, fourth, fifth]
    up_last = down_last = None
    for r in range(1, count):
        up_pairs = [(k, k + 1) for k in range(r)]
        down_pairs = [(count - 1 - k, count - 2 - k) for k in range(r)]
        if r == 1 and count > 3:
            up_last = down_last = lax.ppermute(blocks[count], axis, up_pairs + down_pairs)
            continue
        up_block, down_block = blocks[count - r], blocks[r]
        if r > 1:
            up_block = up_block + up_last
            down_block = down_block + down_last
        up_last = lax.ppermute(up_block, axis, up_pairs)
        down_last = lax.ppermute(down_block, axis, down_pairs)
    return [blocks[0], up_last, down_last]


def compute(raw_movie, footprints, traces):
    rows, cols, frame_count = raw_movie.shape
    pixel_count = rows * cols
    pix_count = lax.axis_size("pix")
    count = lax.axis_size("tm")
    pix = lax.axis_index("pix")
    here = lax.axis_index("tm")
    core = lax.rem(pix, 2)
    trace_rows = traces.shape[0]
    blocks = frame_count // LANES
    quarter = max(blocks // 4, 1)
    widths = [2 * quarter, blocks - 2 * quarter]
    halo = SUBSTEPS

    def swap(mask):
        return [(k, k ^ mask) for k in range(pix_count)]

    inner = (pix > 0).astype(jnp.int32)
    outer = (pix < pix_count - 1).astype(jnp.int32)
    turned = (here == 1).astype(jnp.int32)
    bend = (lax.rem(pix, GROUP) == 0) * inner + (lax.rem(pix, GROUP) == GROUP - 1) * outer
    flags = scalars = jnp.stack([here, core, lax.div(pix, 2), turned, inner, outer, bend]).astype(jnp.int32)

    entries = line_gather(scalars, footprints, "tm", count)

    bent = [k for k in range(pix_count - 1) if k % GROUP == GROUP - 1] if pix_count % GROUP == 0 else []
    halos = []
    for c, width in enumerate(widths):
        begin = sum(widths[:c]) * LANES
        last = c == len(widths) - 1 and bool(bent)
        joins = [(k, k + 1) for k in range(1, pix_count - 1, 2) if not (last and k in bent)]
        joins += [(b, a) for a, b in joins]
        if c == 0:
            shift = rows - halo
            size = (halo, cols, width * LANES)
            inward = lax.dynamic_slice(raw_movie, ((1 - core) * shift, 0, begin), size)
            outward = lax.dynamic_slice(raw_movie, (core * shift, 0, begin), size)
        else:
            inward, outward = edges_call(flags, raw_movie, halo, begin, width * LANES)
        detour = None
        if last:
            first = [(k, k + GROUP) for k in bent] + [(k + 1, k + 1 - GROUP) for k in bent]
            second = [(k + GROUP, k + 1) for k in bent] + [(k + 1 - GROUP, k) for k in bent]
            detour = lax.ppermute(outward, "pix", first)
            detour = lax.ppermute(detour, "pix", second)
        from_outer = lax.ppermute(outward, "pix", joins)
        from_inner = lax.ppermute(inward, "pix", swap(1))
        halos.append((from_inner, from_outer, detour))

    held, masks = traces[None], [0]
    hops = [mask for mask in (4, 8, 16, 32, 64, 1) if mask < pix_count]
    for mask in hops:
        held = jnp.concatenate([held, lax.ppermute(held, "pix", swap(mask))], axis=0)
        masks = masks + [mask ^ m for m in masks]
    gathered = [(held, masks)]
    if pix_count > 2:
        gathered.append((lax.ppermute(held, "pix", swap(2)), [2 ^ m for m in masks]))

    current = None
    movies = []
    for members in ((0,), (1,)):
        pair = (None, None)
        pair_frames = sum(widths[c] for c in members) * LANES
        pair_begin = 0
        for c in members:
            current, *pair = diffuse_call(
                flags, raw_movie, *halos[c], current, pair, sum(widths[:c]), pair_begin, pair_frames
            )
            pair_begin += widths[c]
        movies.append(tuple(array.reshape(pixel_count, pair_frames) for array in pair))

    foot, gram = footprints_call(scalars, footprints, entries)
    keep, send = numerator_call(scalars, foot, movies, gram, trace_rows)
    arrived = lax.ppermute(send, "pix", swap(1))
    parts = []
    for k in range(1, keep.shape[0]):
        parts.append(lax.ppermute(keep[k] + arrived[k], "pix", swap(2 * k)))
    new_traces, again = traces_call(scalars, keep, arrived, parts, gathered)
    near = [again]
    for k in range(1, keep.shape[0]):
        near.append(lax.ppermute(again, "pix", swap(2 * k)))
    far = []
    for piece in near:
        far.append(lax.ppermute(piece, "pix", swap(1)))

    products = []
    for h in range(HALVES):
        products.append(products_call(scalars, near, far, movies, h, count, scatter_places(count), h == 0))
    sums = [line_scatter(blocks, "tm", count) for blocks in products]
    part = pixel_count // HALVES
    gram_mine = sum(array[:, part:] for array in sums[0])
    gram_other = lax.ppermute(gram_mine, "pix", swap(1))
    new_footprints = None
    for h in range(HALVES):
        new_footprints = final_call(
            scalars, footprints, foot, sums[h], gram_mine, gram_other, new_footprints, h
        )
    return current, new_footprints, new_traces


def solution(mesh):
    placed = (P("pix", None, "tm"), P("tm", "pix"), P("pix", "tm"))
    return jax.shard_map(
        compute,
        mesh=mesh,
        in_specs=placed,
        out_specs=(P("pix", None, "tm"), P("tm", "pix"), P("pix", "tm")),
        check_vma=False,
    )
```

```python
import jax
import jax.numpy as jnp
from jax import lax
from jax.experimental import pallas as pl
from jax.experimental.pallas import tpu as pltpu
from jax.sharding import PartitionSpec as P


edge_square = 0.25
step_scale = 0.06
SUBSTEPS = 4
LANES = 128
GROUP = 4
HALVES = 2

HERE, CORE, CHIP, TURNED, INSIDE, BENT = 0, 1, 2, 3, 4, 6

NN = ((1,), (0,))
NT = ((1,), (1,))


def flux_quarter(change):
    return change / (change * change + edge_square)


def split(value):
    high = value.astype(jnp.bfloat16)
    low = (value - high.astype(jnp.float32)).astype(jnp.bfloat16)
    return high, low


def stacked(value):
    return jnp.concatenate(split(value), axis=0)


def dot(left, right, dims):
    return lax.dot_general(left, right, (dims, ((), ())), preferred_element_type=jnp.float32)


def fold(value):
    half = value.shape[0] // 2
    return value[:half] + value[half:]


def grant(mebibytes):
    return pltpu.CompilerParams(vmem_limit_bytes=mebibytes * 1024 * 1024)


def cost(flops, moved):
    return pl.CostEstimate(flops=flops, bytes_accessed=moved, transcendentals=0)


def shaped(*shape, dtype=jnp.float32):
    return jax.ShapeDtypeStruct(shape, dtype)


def edges_call(flags, raw, halo, wanted):
    rows, cols, _ = raw.shape
    shift = rows - halo

    def kernel(flags, raw_ref, *refs):
        out_refs, sems = refs[:-1], refs[-1]
        core = flags[CORE]
        copies = []
        for k, (outward, begin, frames) in enumerate(wanted):
            start = (core if outward else 1 - core) * shift
            copies.append(
                pltpu.make_async_copy(
                    raw_ref.at[pl.ds(start, halo), :, pl.ds(begin, frames)], out_refs[k], sems.at[k]
                )
            )
        for copy in copies:
            copy.start()
        for copy in copies:
            copy.wait()

    blocks = [(halo, cols, frames) for _, _, frames in wanted]
    return pl.pallas_call(
        kernel,
        grid_spec=pltpu.PrefetchScalarGridSpec(
            num_scalar_prefetch=1,
            grid=(1,),
            in_specs=[pl.BlockSpec(memory_space=pltpu.HBM)],
            out_specs=[pl.BlockSpec(block, lambda i, flags: (0, 0, 0)) for block in blocks],
            scratch_shapes=[pltpu.SemaphoreType.DMA((len(wanted),))],
        ),
        out_shape=[shaped(*block) for block in blocks],
        cost_estimate=cost(1, sum(8 * halo * cols * frames for _, _, frames in wanted)),
        compiler_params=grant(10),
        name="edges",
    )(flags, raw)


def diffuse_call(flags, raw, halo_inner, halo_outer, detour, movie, pair, begin, pair_begin, pair_frames, skip, groups):
    rows, cols, total = raw.shape
    halo = halo_inner.shape[0]
    carried = [array for array in (movie, *pair) if array is not None]
    width = 64
    pad = 8
    extended = rows + 2 * halo
    inputs = 3 if detour is None else 4

    def kernel(flags, *refs):
        sources, refs = refs[:inputs], refs[inputs:]
        refs = refs[len(carried) :]
        out_ref, high_ref, low_ref, first_bufs, second_buf, out_bufs, in_sems, out_sems = refs
        group = pl.program_id(0)
        slot = lax.rem(group, 2)
        inside = pl.ds(pad, cols)

        def fetches(at):
            here = lax.rem(at, 2)
            lanes = pl.ds(pl.multiple_of((skip + at) * LANES, LANES), LANES)
            wide = pl.ds(pl.multiple_of((begin + at) * LANES, LANES), LANES)

            def one(ref, cut, start, count, part):
                return pltpu.make_async_copy(
                    ref.at[:, :, cut], first_bufs.at[here, pl.ds(start, count), inside, :], in_sems.at[here, part]
                )

            far_side = halo + rows
            inner_at = (1 - flags[CORE]) * far_side
            outer_at = flags[CORE] * far_side
            made = [
                (None, one(sources[0], wide, halo, rows, 0)),
                (None, one(sources[1], lanes, inner_at, halo, 1)),
            ]
            plain = one(sources[2], lanes, outer_at, halo, 2)
            if detour is None:
                made.append((None, plain))
            else:
                made.append((flags[BENT] == 0, plain))
                made.append((flags[BENT] == 1, one(sources[3], lanes, outer_at, halo, 2)))
            return made

        def run(at, act):
            for condition, copy in fetches(at):
                if condition is None:
                    act(copy)
                else:
                    pl.when(condition)(lambda copy=copy: act(copy))

        def give(at):
            wide = pl.ds(pl.multiple_of((begin + at) * LANES, LANES), LANES)
            here = lax.rem(at, 2)
            return pltpu.make_async_copy(out_bufs.at[here], out_ref.at[:, :, wide], out_sems.at[here])

        @pl.when(group == 0)
        def _():
            run(group, lambda copy: copy.start())

        @pl.when(group + 1 < groups)
        def _():
            run(group + 1, lambda copy: copy.start())

        zero = jnp.zeros((extended, pad, LANES), jnp.float32)
        first_buf = first_bufs.at[slot]
        for buf in (first_buf, second_buf):
            buf[:, 0:pad, :] = zero
            buf[:, pad + cols :, :] = zero
        run(group, lambda copy: copy.wait())

        @pl.when(group >= 2)
        def _():
            give(group - 2).wait()

        scale_up = step_scale * flags[INSIDE].astype(jnp.float32)
        scale_down = step_scale * flags[INSIDE + 1].astype(jnp.float32)
        head = lax.broadcasted_iota(jnp.int32, (width, LANES), 0) == 0
        bufs = (first_buf, second_buf)
        for step in range(SUBSTEPS):
            src, dst = bufs[step % 2], bufs[1 - step % 2]
            top = step
            middle = range(step + 1, extended - step - 1)

            def tile(j, left_flux):
                base = pl.multiple_of(pad + j * width, 8)
                col = pl.multiple_of(j * width, width)
                kept = []
                current = src[top + 1, pl.ds(base, width), :]
                flux_up = flux_quarter(current - src[top, pl.ds(base, width), :])
                for k, row in enumerate(middle):
                    below = src[row + 1, pl.ds(base, width), :]
                    flux_down = flux_quarter(below - current)
                    flux_right = flux_quarter(src[row, pl.ds(base + 1, width), :] - current)
                    rolled = pltpu.roll(flux_right, 1, 0)
                    flux_left = jnp.where(head, left_flux[k], rolled)
                    scale = step_scale
                    if row < halo:
                        scale = scale_up
                    if row >= halo + rows:
                        scale = scale_down
                    value = current + scale * ((flux_down - flux_up) + (flux_right - flux_left))
                    kept.append(rolled)
                    if step + 1 < SUBSTEPS:
                        dst[row, pl.ds(base, width), :] = value
                    else:
                        out_bufs[slot, row - halo, pl.ds(col, width), :] = value
                        high, low = split(value)
                        high_ref[row - halo, pl.ds(col, width), :] = high
                        low_ref[row - halo, pl.ds(col, width), :] = low
                    current, flux_up = below, flux_down
                return tuple(kept)

            edge = tuple(flux_quarter(src[row, pl.ds(pad, width), :]) for row in middle)
            lax.fori_loop(0, cols // width, tile, edge)
        give(group).start()

        @pl.when(group == groups - 1)
        def _():
            if groups > 1:
                give(group - 1).wait()
            give(group).wait()

    outside = pl.BlockSpec(memory_space=pltpu.HBM)
    operands = [flags, raw, halo_inner, halo_outer]
    if detour is not None:
        operands.append(detour)
    outputs = [k for k, array in enumerate((movie, *pair)) if array is not None]
    aliases = {len(operands) + k: output for k, output in enumerate(outputs)}
    operands += carried
    padded = (extended, cols + 2 * pad, LANES)
    return pl.pallas_call(
        kernel,
        grid_spec=pltpu.PrefetchScalarGridSpec(
            num_scalar_prefetch=1,
            grid=(groups,),
            in_specs=[outside] * (len(operands) - 1 - len(carried))
            + [pl.BlockSpec(memory_space=pl.ANY)] * len(carried),
            out_specs=[outside] + [pl.BlockSpec((rows, cols, LANES), lambda i, flags: (0, 0, pair_begin + i))] * 2,
            scratch_shapes=[
                pltpu.VMEM((2, *padded), jnp.float32),
                pltpu.VMEM(padded, jnp.float32),
                pltpu.VMEM((2, rows, cols, LANES), jnp.float32),
                pltpu.SemaphoreType.DMA((2, 3)),
                pltpu.SemaphoreType.DMA((2,)),
            ],
        ),
        out_shape=[shaped(rows, cols, total)] + [shaped(rows, cols, pair_frames, dtype=jnp.bfloat16)] * 2,
        input_output_aliases=aliases,
        cost_estimate=cost(rows * cols * groups * LANES * 200, rows * cols * groups * LANES * 16),
        compiler_params=grant(16),
        name="diffuse",
    )(*operands)


def footprints_call(scalars, own, entries):
    count = len(entries) + 1
    share, pixel_count = own.shape
    rank = share * count
    block = 512
    steps = pixel_count // block

    def kernel(scalars, *refs):
        own_ref = refs[0]
        entry_refs = [(refs[1 + 2 * k], refs[2 + 2 * k]) for k in range(count - 1)]
        out_ref, gram_ref, total = refs[2 * count - 1 :]
        here = scalars[HERE]
        step = pl.program_id(0)

        def put(place, value):
            at = pl.multiple_of(place * share, share)
            high, low = split(value)
            out_ref[pl.ds(at, share), :] = high
            out_ref[pl.ds(rank + at, share), :] = low

        put(here, own_ref[...])
        for (first_ref, second_ref), (_, _, test, place) in zip(entry_refs, entries):
            put(place(here), jnp.where(test(here), first_ref[...], second_ref[...]))

        @pl.when(step == 0)
        def _():
            total[...] = jnp.zeros_like(total)

        total[...] += dot(out_ref[...], out_ref[0:rank, :], NT)

        @pl.when(step == steps - 1)
        def _():
            cross = total[rank:, :]
            gram_ref[...] = total[0:rank, :] + (cross + cross.T)

    foot_spec = pl.BlockSpec((share, block), lambda k, s: (0, k))
    flat = [array for entry in entries for array in entry[:2]]
    return pl.pallas_call(
        kernel,
        grid_spec=pltpu.PrefetchScalarGridSpec(
            num_scalar_prefetch=1,
            grid=(steps,),
            in_specs=[foot_spec] * (1 + len(flat)),
            out_specs=[
                pl.BlockSpec((2 * rank, block), lambda k, s: (0, k)),
                pl.BlockSpec((rank, rank), lambda k, s: (0, 0)),
            ],
            scratch_shapes=[pltpu.VMEM((2 * rank, rank), jnp.float32)],
        ),
        out_shape=[shaped(2 * rank, pixel_count, dtype=jnp.bfloat16), shaped(rank, rank)],
        cost_estimate=cost(4 * rank * rank * pixel_count, 8 * rank * pixel_count),
        compiler_params=grant(8),
        name="footprints",
    )(scalars, own, *flat)


def numerator_call(scalars, foot, movies, gram, trace_rows):
    rank = foot.shape[0] // 2
    pixel_count = movies[0][0].shape[0]
    spans = [high.shape[1] for high, _ in movies]
    frames = sum(spans)
    columns = frames + rank
    block = 512
    steps = pixel_count // block
    chips = rank // (2 * trace_rows)

    def kernel(scalars, foot_ref, gram_ref, *refs):
        movie_refs = refs[: 2 * len(movies)]
        keep_ref, send_ref, total = refs[2 * len(movies) :]
        step = pl.program_id(0)

        @pl.when(step == 0)
        def _():
            total[...] = jnp.zeros_like(total)

        for k in range(len(movies)):
            high_ref, low_ref = movie_refs[2 * k : 2 * k + 2]
            part = fold(dot(foot_ref[...], high_ref[...], NN)) + dot(foot_ref[0:rank, :], low_ref[...], NN)
            total[:, sum(spans[:k]) : sum(spans[: k + 1])] += part

        @pl.when(step == steps - 1)
        def _():
            total[:, frames:] = gram_ref[...]
            core = scalars[CORE]
            for k in range(chips):
                chip = scalars[CHIP] ^ k
                mine = pl.multiple_of((2 * chip + core) * trace_rows, trace_rows)
                other = pl.multiple_of((2 * chip + 1 - core) * trace_rows, trace_rows)
                keep_ref[k] = total[pl.ds(mine, trace_rows), :]
                send_ref[k] = total[pl.ds(other, trace_rows), :]

    out_spec = pl.BlockSpec((chips, trace_rows, columns), lambda k, s: (0, 0, 0))
    return pl.pallas_call(
        kernel,
        grid_spec=pltpu.PrefetchScalarGridSpec(
            num_scalar_prefetch=1,
            grid=(steps,),
            in_specs=[
                pl.BlockSpec((2 * rank, block), lambda k, s: (0, k)),
                pl.BlockSpec((rank, rank), lambda k, s: (0, 0)),
            ]
            + [pl.BlockSpec((block, array.shape[1]), lambda k, s: (k, 0)) for movie in movies for array in movie],
            out_specs=[out_spec, out_spec],
            scratch_shapes=[pltpu.VMEM((rank, columns), jnp.float32)],
        ),
        out_shape=[shaped(chips, trace_rows, columns)] * 2,
        cost_estimate=cost(8 * rank * pixel_count * columns, 4 * pixel_count * (rank + columns)),
        compiler_params=grant(10),
        name="numerator",
    )(scalars, foot, gram, *[array for movie in movies for array in movie])


def traces_call(scalars, keep, arrived, parts, gathered):
    _, trace_rows, columns = keep.shape
    frames = gathered[0][0].shape[2]
    rank = columns - frames
    stacks = [stack for stack, _ in gathered]

    def kernel(scalars, *refs):
        stack_refs, refs = refs[: len(stacks)], refs[len(stacks) :]
        part_refs, (out_ref, copy_ref, full) = refs[:-3], refs[-3:]
        for stack_ref, (_, masks) in zip(stack_refs, gathered):
            for k, mask in enumerate(masks):
                device = 2 * (scalars[CHIP] ^ (mask // 2))
                device = device + (1 - scalars[CORE] if mask % 2 else scalars[CORE])
                full[pl.ds(pl.multiple_of(device * trace_rows, trace_rows), trace_rows), :] = stack_ref[k]
        total = part_refs[0][0] + part_refs[1][0]
        for part_ref in part_refs[2:]:
            total = total + part_ref[...]
        gram = stacked(total[:, frames:])
        high, low = split(full[...])
        below = fold(dot(gram, high, NN)) + dot(gram[0:trace_rows], low, NN)
        value = stack_refs[0][0] * total[:, 0:frames] / below
        out_ref[...] = value
        copy_ref[...] = value

    return pl.pallas_call(
        kernel,
        grid_spec=pltpu.PrefetchScalarGridSpec(
            num_scalar_prefetch=1,
            grid=(1,),
            in_specs=[pl.BlockSpec(stack.shape, lambda k, s: (0, 0, 0)) for stack in stacks]
            + [pl.BlockSpec((1, trace_rows, columns), lambda k, s: (0, 0, 0))] * 2
            + [pl.BlockSpec((trace_rows, columns), lambda k, s: (0, 0))] * len(parts),
            out_specs=[pl.BlockSpec((trace_rows, frames), lambda k, s: (0, 0))] * 2,
            scratch_shapes=[pltpu.VMEM((rank, frames), jnp.float32)],
        ),
        out_shape=[shaped(trace_rows, frames)] * 2,
        cost_estimate=cost(6 * trace_rows * rank * frames, 8 * rank * frames),
        compiler_params=grant(6),
        name="traces",
    )(scalars, *stacks, keep, arrived, *parts)


def products_call(scalars, near, far, movies, half, count, places, with_gram):
    chips = len(near)
    trace_rows, frames = near[0].shape
    rank = 2 * chips * trace_rows
    half_rank = rank // 2
    share = rank // count
    pixel_count = movies[0][0].shape[0]
    spans = [high.shape[1] for high, _ in movies]
    part = pixel_count // HALVES
    block = rank
    steps = part // block
    columns = part + (half_rank if with_gram else 0)
    outs = len(places)

    def kernel(scalars, *refs):
        near_refs, far_refs, refs = refs[:chips], refs[chips : 2 * chips], refs[2 * chips :]
        movie_refs = refs[: 2 * len(movies)]
        refs = refs[2 * len(movies) :]
        out_refs = refs[:outs]
        full, left, result = refs[outs:]
        step = pl.program_id(0)
        here = scalars[HERE]

        @pl.when(step == 0)
        def _():
            for k in range(chips):
                device = 2 * (scalars[CHIP] ^ k) + scalars[CORE]
                full[pl.ds(pl.multiple_of(device * trace_rows, trace_rows), trace_rows), :] = near_refs[k][...]
                device = 2 * (scalars[CHIP] ^ k) + 1 - scalars[CORE]
                full[pl.ds(pl.multiple_of(device * trace_rows, trace_rows), trace_rows), :] = far_refs[k][...]
            left[...] = stacked(full[...])

        def emit(total, at):
            width = total.shape[1]
            result[:, 0:width] = total
            for k, out_ref in enumerate(out_refs):
                row = pl.multiple_of(places[k](here) * share, share)
                out_ref[:, pl.ds(at, width)] = result[pl.ds(row, share), 0:width]

        both = jnp.zeros((2 * rank, block), jnp.float32)
        upper = jnp.zeros((rank, block), jnp.float32)
        for k in range(len(movies)):
            high_ref, low_ref = movie_refs[2 * k : 2 * k + 2]
            cut = slice(sum(spans[:k]), sum(spans[: k + 1]))
            both += dot(left[:, cut], high_ref[...], NT)
            upper += dot(left[0:rank, cut], low_ref[...], NT)
        emit(fold(both) + upper, pl.multiple_of(step * block, block))
        if with_gram:

            @pl.when(step == steps - 1)
            def _():
                at = pl.multiple_of(scalars[CORE] * half_rank, half_rank)
                both = dot(left[...], left[pl.ds(at, half_rank), :], NT)
                upper = dot(left[0:rank, :], left[pl.ds(rank + at, half_rank), :], NT)
                emit(fold(both) + upper, part)

    piece = pl.BlockSpec((trace_rows, frames), lambda j, s: (0, 0))
    return pl.pallas_call(
        kernel,
        grid_spec=pltpu.PrefetchScalarGridSpec(
            num_scalar_prefetch=1,
            grid=(steps,),
            in_specs=[piece] * (2 * chips)
            + [
                pl.BlockSpec((block, array.shape[1]), lambda j, s: (half * steps + j, 0))
                for movie in movies
                for array in movie
            ],
            out_specs=[pl.BlockSpec((share, columns), lambda j, s: (0, 0))] * outs,
            scratch_shapes=[
                pltpu.VMEM((rank, frames), jnp.float32),
                pltpu.VMEM((2 * rank, frames), jnp.bfloat16),
                pltpu.VMEM((rank, block), jnp.float32),
            ],
        ),
        out_shape=[shaped(share, columns)] * outs,
        cost_estimate=cost(8 * rank * part * frames, 4 * part * (frames + rank)),
        compiler_params=grant(10),
        name="products",
    )(scalars, *near, *far, *[array for movie in movies for array in movie])


def first_final_call(scalars, own, foot, parts, gram_mine, gram_other):
    share, pixel_count = own.shape
    rank = foot.shape[0] // 2
    part = pixel_count // HALVES
    block = 512
    steps = part // block

    def kernel(scalars, own_ref, foot_ref, later_ref, *refs):
        part_refs = refs[: len(parts)]
        mine, other = refs[len(parts)][...], refs[len(parts) + 1][...]
        out_ref, below_ref = refs[-2:]
        above = part_refs[0][...]
        for part_ref in part_refs[1:]:
            above = above + part_ref[...]
        first = scalars[CORE] == 0
        gram = jnp.concatenate([jnp.where(first, mine, other), jnp.where(first, other, mine)], axis=1)
        both = stacked(gram)

        def divisor(ref):
            return fold(dot(both, ref[0:rank, :], NN)) + dot(both[0:share], ref[rank:, :], NN)

        out_ref[...] = own_ref[...] * above / divisor(foot_ref)
        below_ref[...] = divisor(later_ref)

    in_specs = [
        pl.BlockSpec((share, block), lambda k, s: (0, k)),
        pl.BlockSpec((2 * rank, block), lambda k, s: (0, k)),
        pl.BlockSpec((2 * rank, block), lambda k, s: (0, steps + k)),
    ]
    in_specs += [pl.BlockSpec((share, block), lambda k, s: (0, k))] * len(parts)
    in_specs += [pl.BlockSpec((share, rank // 2), lambda k, s: (0, 0))] * 2
    return pl.pallas_call(
        kernel,
        grid_spec=pltpu.PrefetchScalarGridSpec(
            num_scalar_prefetch=1,
            grid=(steps,),
            in_specs=in_specs,
            out_specs=[pl.BlockSpec((share, block), lambda k, s: (0, k))] * 2,
        ),
        out_shape=[shaped(share, pixel_count), shaped(share, part)],
        cost_estimate=cost(12 * share * rank * part, 4 * part * (2 * rank + 5 * share)),
        compiler_params=grant(8),
        name="final",
    )(scalars, own, foot, foot, *parts, gram_mine, gram_other)


def second_final_call(own, parts, below, carried):
    share, pixel_count = own.shape
    part = pixel_count // HALVES
    block = 512
    steps = part // block

    def kernel(own_ref, below_ref, *refs):
        above = refs[0][...]
        for part_ref in refs[1 : len(parts)]:
            above = above + part_ref[...]
        refs[-1][...] = own_ref[...] * above / below_ref[...]

    near = pl.BlockSpec((share, block), lambda k: (0, k))
    far = pl.BlockSpec((share, block), lambda k: (0, steps + k))
    operands = [own, below, *parts, carried]
    return pl.pallas_call(
        kernel,
        grid=(steps,),
        in_specs=[far, near] + [near] * len(parts) + [pl.BlockSpec(memory_space=pl.ANY)],
        out_specs=far,
        out_shape=shaped(share, pixel_count),
        input_output_aliases={len(operands) - 1: 0},
        cost_estimate=cost(4 * share * part, 24 * share * part),
        compiler_params=grant(6),
        name="final",
    )(*operands)


def choose_call(scalars, down, up):
    rows, columns = up.shape
    block = columns // 2

    def kernel(scalars, down_ref, up_ref, out_ref):
        out_ref[...] = jnp.where(scalars[TURNED] == 1, down_ref[...], up_ref[...])

    spec = pl.BlockSpec((rows, block), lambda k, s: (0, k))
    return pl.pallas_call(
        kernel,
        grid_spec=pltpu.PrefetchScalarGridSpec(
            num_scalar_prefetch=1, grid=(2,), in_specs=[spec, spec], out_specs=spec
        ),
        out_shape=shaped(rows, columns),
        cost_estimate=cost(rows * columns, 12 * rows * columns),
        compiler_params=grant(4),
        name="choose",
    )(scalars, down, up)


def line_gather(scalars, block, axis, count):
    if count == 4:
        middle = [(1, 2), (2, 1)]
        outward = [(1, 0), (2, 3)]
        near = lax.ppermute(block, axis, [(k, k ^ 1) for k in range(count)])
        across = lax.ppermute(block, axis, middle)
        far = lax.ppermute(near, axis, middle)
        out_across = lax.ppermute(across, axis, outward)
        out_far = lax.ppermute(far, axis, outward)

        def between(here):
            return (here == 1) | (here == 2)

        return [
            (near, near, between, lambda here: here ^ 1),
            (across, out_across, between, lambda here: jnp.where(here < 2, 2, 1)),
            (far, out_far, between, lambda here: jnp.where(here < 2, 3, 0)),
        ]
    up, down = {}, {}
    last_up = last_down = block
    for r in range(1, count):
        up_pairs = [(k, k + 1) for k in range(r - 1, count - 1)]
        down_pairs = [(k + 1, k) for k in range(0, count - r)]
        if r == count - 1 and count != 3:
            merged = choose_call(scalars, last_down, last_up) if count > 2 else block
            last_up = last_down = lax.ppermute(merged, axis, up_pairs + down_pairs)
        else:
            last_up = lax.ppermute(last_up, axis, up_pairs)
            last_down = lax.ppermute(last_down, axis, down_pairs)
        up[r], down[r] = last_up, last_down
    return [
        (down[s], up[count - s], lambda here, s=s: here + s < count, lambda here, s=s: lax.rem(here + s, count))
        for s in range(1, count)
    ]


def scatter_places(count):
    if count == 4:
        return [
            lambda here: here,
            lambda here: here ^ 1,
            lambda here: 3 - here,
            lambda here: lax.rem(here + 2, count),
        ]
    slots = [lambda here, s=s: lax.rem(here + s, count) for s in range(count)]
    return slots + [lambda here: lax.rem(here + jnp.where(here == 0, count - 1, 1), count)]


def line_scatter(blocks, axis, count):
    if count == 4:
        own, beside, opposite, remaining = blocks
        inward = [(0, 1), (3, 2)]
        middle = [(1, 2), (2, 1)]
        first = lax.ppermute(opposite, axis, inward)
        second = lax.ppermute(remaining, axis, inward)
        third = lax.ppermute(remaining + first, axis, middle)
        fourth = lax.ppermute(beside + third, axis, [(k, k ^ 1) for k in range(count)])
        fifth = lax.ppermute(opposite + second, axis, middle)
        return [own, fourth, fifth]
    up_last = down_last = None
    for r in range(1, count):
        up_pairs = [(k, k + 1) for k in range(r)]
        down_pairs = [(count - 1 - k, count - 2 - k) for k in range(r)]
        if r == 1 and count > 3:
            up_last = down_last = lax.ppermute(blocks[count], axis, up_pairs + down_pairs)
            continue
        up_block, down_block = blocks[count - r], blocks[r]
        if r > 1:
            up_block = up_block + up_last
            down_block = down_block + down_last
        up_last = lax.ppermute(up_block, axis, up_pairs)
        down_last = lax.ppermute(down_block, axis, down_pairs)
    return [blocks[0], up_last, down_last]


def compute(raw_movie, footprints, traces):
    rows, cols, frame_count = raw_movie.shape
    pixel_count = rows * cols
    pix_count = lax.axis_size("pix")
    count = lax.axis_size("tm")
    pix = lax.axis_index("pix")
    here = lax.axis_index("tm")
    core = lax.rem(pix, 2)
    trace_rows = traces.shape[0]
    blocks = frame_count // LANES
    quarter = max(blocks // 4, 1)
    widths = [2 * quarter, blocks - 2 * quarter]
    halo = SUBSTEPS

    def swap(mask):
        return [(k, k ^ mask) for k in range(pix_count)]

    inner = (pix > 0).astype(jnp.int32)
    outer = (pix < pix_count - 1).astype(jnp.int32)
    turned = (here == 1).astype(jnp.int32)
    bend = (lax.rem(pix, GROUP) == 0) * inner + (lax.rem(pix, GROUP) == GROUP - 1) * outer
    flags = scalars = jnp.stack([here, core, lax.div(pix, 2), turned, inner, outer, bend]).astype(jnp.int32)

    entries = line_gather(scalars, footprints, "tm", count)

    bent = [k for k in range(pix_count - 1) if k % GROUP == GROUP - 1] if pix_count % GROUP == 0 else []
    begins = [sum(widths[:c]) * LANES for c in range(len(widths))]
    spans = [(begin, width * LANES) for begin, width in zip(begins, widths)]
    outward_rows = [
        lax.dynamic_slice(raw_movie, (core * (rows - halo), 0, 0), (halo, cols, widths[0] * LANES))
    ]
    later = edges_call(
        flags, raw_movie, halo, [(True, *span) for span in spans[1:]] + [(False, *span) for span in spans]
    )
    outward_rows += later[: len(spans) - 1]
    inward_rows = later[len(spans) - 1 :]
    halos = []
    for c, (inward, outward) in enumerate(zip(inward_rows, outward_rows)):
        last = c == len(widths) - 1 and bool(bent)
        joins = [(k, k + 1) for k in range(1, pix_count - 1, 2) if not (last and k in bent)]
        joins += [(b, a) for a, b in joins]
        detour = None
        if last:
            first = [(k, k + GROUP) for k in bent] + [(k + 1, k + 1 - GROUP) for k in bent]
            second = [(k + GROUP, k + 1) for k in bent] + [(k + 1 - GROUP, k) for k in bent]
            detour = lax.ppermute(outward, "pix", first)
            detour = lax.ppermute(detour, "pix", second)
        from_outer = lax.ppermute(outward, "pix", joins)
        from_inner = lax.ppermute(inward, "pix", swap(1))
        halos.append((from_inner, from_outer, detour))

    held, masks = traces[None], [0]
    hops = [mask for mask in (4, 8, 16, 32, 64, 1) if mask < pix_count]
    for mask in hops:
        held = jnp.concatenate([held, lax.ppermute(held, "pix", swap(mask))], axis=0)
        masks = masks + [mask ^ m for m in masks]
    gathered = [(held, masks)]
    if pix_count > 2:
        gathered.append((lax.ppermute(held, "pix", swap(2)), [2 ^ m for m in masks]))

    current = None
    movies = []
    for c, width in enumerate(widths):
        pair = (None, None)
        calls = 1
        for part in range(calls):
            groups = width // calls
            skip = part * groups
            current, *pair = diffuse_call(
                flags, raw_movie, *halos[c], current, pair,
                sum(widths[:c]) + skip, skip, width * LANES, skip, groups,
            )
        movies.append(tuple(array.reshape(pixel_count, width * LANES) for array in pair))

    foot, gram = footprints_call(scalars, footprints, entries)
    keep, send = numerator_call(scalars, foot, movies, gram, trace_rows)
    arrived = lax.ppermute(send, "pix", swap(1))
    parts = []
    for k in range(1, keep.shape[0]):
        parts.append(lax.ppermute(keep[k] + arrived[k], "pix", swap(2 * k)))
    new_traces, again = traces_call(scalars, keep, arrived, parts, gathered)
    near = [again]
    for k in range(1, keep.shape[0]):
        near.append(lax.ppermute(again, "pix", swap(2 * k)))
    far = []
    for piece in near:
        far.append(lax.ppermute(piece, "pix", swap(1)))

    products = []
    for h in range(HALVES):
        products.append(products_call(scalars, near, far, movies, h, count, scatter_places(count), h == 0))
    sums = [line_scatter(blocks, "tm", count) for blocks in products]
    part = pixel_count // HALVES
    gram_mine = sum(array[:, part:] for array in sums[0])
    gram_other = lax.ppermute(gram_mine, "pix", swap(1))
    new_footprints, below = first_final_call(scalars, footprints, foot, sums[0], gram_mine, gram_other)
    new_footprints = second_final_call(footprints, sums[1], below, new_footprints)
    return current, new_footprints, new_traces


def solution(mesh):
    placed = (P("pix", None, "tm"), P("tm", "pix"), P("pix", "tm"))
    return jax.shard_map(
        compute,
        mesh=mesh,
        in_specs=placed,
        out_specs=(P("pix", None, "tm"), P("tm", "pix"), P("pix", "tm")),
        check_vma=False,
    )
```

```python
import jax
import jax.numpy as jnp
from jax import lax
from jax.experimental import pallas as pl
from jax.experimental.pallas import tpu as pltpu
from jax.sharding import PartitionSpec as P


edge_square = 0.25
step_scale = 0.06
SUBSTEPS = 4
LANES = 128
GROUP = 4
HALVES = 2

HERE, CORE, CHIP, TURNED, INSIDE, BENT = 0, 1, 2, 3, 4, 6

NN = ((1,), (0,))
NT = ((1,), (1,))


def flux_quarter(change):
    return change / (change * change + edge_square)


def split(value):
    high = value.astype(jnp.bfloat16)
    low = (value - high.astype(jnp.float32)).astype(jnp.bfloat16)
    return high, low


def stacked(value):
    return jnp.concatenate(split(value), axis=0)


def dot(left, right, dims):
    return lax.dot_general(left, right, (dims, ((), ())), preferred_element_type=jnp.float32)


def fold(value):
    half = value.shape[0] // 2
    return value[:half] + value[half:]


def grant(mebibytes):
    return pltpu.CompilerParams(vmem_limit_bytes=mebibytes * 1024 * 1024)


def cost(flops, moved):
    return pl.CostEstimate(flops=flops, bytes_accessed=moved, transcendentals=0)


def shaped(*shape, dtype=jnp.float32):
    return jax.ShapeDtypeStruct(shape, dtype)


def edges_call(flags, raw, halo, wanted):
    rows, cols, _ = raw.shape
    shift = rows - halo

    def kernel(flags, raw_ref, *refs):
        out_refs, sems = refs[:-1], refs[-1]
        core = flags[CORE]
        copies = []
        for k, (outward, begin, frames) in enumerate(wanted):
            start = (core if outward else 1 - core) * shift
            copies.append(
                pltpu.make_async_copy(
                    raw_ref.at[pl.ds(start, halo), :, pl.ds(begin, frames)], out_refs[k], sems.at[k]
                )
            )
        for copy in copies:
            copy.start()
        for copy in copies:
            copy.wait()

    blocks = [(halo, cols, frames) for _, _, frames in wanted]
    return pl.pallas_call(
        kernel,
        grid_spec=pltpu.PrefetchScalarGridSpec(
            num_scalar_prefetch=1,
            grid=(1,),
            in_specs=[pl.BlockSpec(memory_space=pltpu.HBM)],
            out_specs=[pl.BlockSpec(block, lambda i, flags: (0, 0, 0)) for block in blocks],
            scratch_shapes=[pltpu.SemaphoreType.DMA((len(wanted),))],
        ),
        out_shape=[shaped(*block) for block in blocks],
        cost_estimate=cost(1, sum(8 * halo * cols * frames for _, _, frames in wanted)),
        compiler_params=grant(10),
        name="edges",
    )(flags, raw)


def diffuse_call(flags, raw, halo_inner, halo_outer, detour, movie, pair, begin, pair_begin, pair_frames, skip, groups):
    rows, cols, total = raw.shape
    halo = halo_inner.shape[0]
    carried = [array for array in (movie, *pair) if array is not None]
    width = 128
    pad = 8
    extended = rows + 2 * halo
    inputs = 3 if detour is None else 4

    def kernel(flags, *refs):
        sources, refs = refs[:inputs], refs[inputs:]
        refs = refs[len(carried) :]
        out_ref, high_ref, low_ref, first_bufs, second_buf, out_bufs, in_sems, out_sems = refs
        group = pl.program_id(0)
        slot = lax.rem(group, 2)
        inside = pl.ds(pad, cols)

        def fetches(at):
            here = lax.rem(at, 2)
            lanes = pl.ds(pl.multiple_of((skip + at) * LANES, LANES), LANES)
            wide = pl.ds(pl.multiple_of((begin + at) * LANES, LANES), LANES)

            def one(ref, cut, start, count, part):
                return pltpu.make_async_copy(
                    ref.at[:, :, cut], first_bufs.at[here, pl.ds(start, count), inside, :], in_sems.at[here, part]
                )

            far_side = halo + rows
            inner_at = (1 - flags[CORE]) * far_side
            outer_at = flags[CORE] * far_side
            made = [
                (None, one(sources[0], wide, halo, rows, 0)),
                (None, one(sources[1], lanes, inner_at, halo, 1)),
            ]
            plain = one(sources[2], lanes, outer_at, halo, 2)
            if detour is None:
                made.append((None, plain))
            else:
                made.append((flags[BENT] == 0, plain))
                made.append((flags[BENT] == 1, one(sources[3], lanes, outer_at, halo, 2)))
            return made

        def run(at, act):
            for condition, copy in fetches(at):
                if condition is None:
                    act(copy)
                else:
                    pl.when(condition)(lambda copy=copy: act(copy))

        def give(at):
            wide = pl.ds(pl.multiple_of((begin + at) * LANES, LANES), LANES)
            here = lax.rem(at, 2)
            return pltpu.make_async_copy(out_bufs.at[here], out_ref.at[:, :, wide], out_sems.at[here])

        @pl.when(group == 0)
        def _():
            run(group, lambda copy: copy.start())

        @pl.when(group + 1 < groups)
        def _():
            run(group + 1, lambda copy: copy.start())

        zero = jnp.zeros((extended, pad, LANES), jnp.float32)
        first_buf = first_bufs.at[slot]
        for buf in (first_buf, second_buf):
            buf[:, 0:pad, :] = zero
            buf[:, pad + cols :, :] = zero
        run(group, lambda copy: copy.wait())

        @pl.when(group >= 2)
        def _():
            give(group - 2).wait()

        scale_up = step_scale * flags[INSIDE].astype(jnp.float32)
        scale_down = step_scale * flags[INSIDE + 1].astype(jnp.float32)
        head = lax.broadcasted_iota(jnp.int32, (width, LANES), 0) == 0
        bufs = (first_buf, second_buf)
        for step in range(SUBSTEPS):
            src, dst = bufs[step % 2], bufs[1 - step % 2]
            top = step
            middle = range(step + 1, extended - step - 1)

            def tile(j, left_flux):
                base = pl.multiple_of(pad + j * width, 8)
                col = pl.multiple_of(j * width, width)
                kept = []
                current = src[top + 1, pl.ds(base, width), :]
                flux_up = flux_quarter(current - src[top, pl.ds(base, width), :])
                for k, row in enumerate(middle):
                    below = src[row + 1, pl.ds(base, width), :]
                    flux_down = flux_quarter(below - current)
                    flux_right = flux_quarter(src[row, pl.ds(base + 1, width), :] - current)
                    rolled = pltpu.roll(flux_right, 1, 0)
                    flux_left = jnp.where(head, left_flux[k], rolled)
                    scale = step_scale
                    if row < halo:
                        scale = scale_up
                    if row >= halo + rows:
                        scale = scale_down
                    value = current + scale * ((flux_down - flux_up) + (flux_right - flux_left))
                    kept.append(rolled)
                    if step + 1 < SUBSTEPS:
                        dst[row, pl.ds(base, width), :] = value
                    else:
                        out_bufs[slot, row - halo, pl.ds(col, width), :] = value
                        high, low = split(value)
                        high_ref[row - halo, pl.ds(col, width), :] = high
                        low_ref[row - halo, pl.ds(col, width), :] = low
                    current, flux_up = below, flux_down
                return tuple(kept)

            edge = tuple(flux_quarter(src[row, pl.ds(pad, width), :]) for row in middle)
            lax.fori_loop(0, cols // width, tile, edge)
        give(group).start()

        @pl.when(group == groups - 1)
        def _():
            if groups > 1:
                give(group - 1).wait()
            give(group).wait()

    outside = pl.BlockSpec(memory_space=pltpu.HBM)
    operands = [flags, raw, halo_inner, halo_outer]
    if detour is not None:
        operands.append(detour)
    outputs = [k for k, array in enumerate((movie, *pair)) if array is not None]
    aliases = {len(operands) + k: output for k, output in enumerate(outputs)}
    operands += carried
    padded = (extended, cols + 2 * pad, LANES)
    return pl.pallas_call(
        kernel,
        grid_spec=pltpu.PrefetchScalarGridSpec(
            num_scalar_prefetch=1,
            grid=(groups,),
            in_specs=[outside] * (len(operands) - 1 - len(carried))
            + [pl.BlockSpec(memory_space=pl.ANY)] * len(carried),
            out_specs=[outside] + [pl.BlockSpec((rows, cols, LANES), lambda i, flags: (0, 0, pair_begin + i))] * 2,
            scratch_shapes=[
                pltpu.VMEM((2, *padded), jnp.float32),
                pltpu.VMEM(padded, jnp.float32),
                pltpu.VMEM((2, rows, cols, LANES), jnp.float32),
                pltpu.SemaphoreType.DMA((2, 3)),
                pltpu.SemaphoreType.DMA((2,)),
            ],
        ),
        out_shape=[shaped(rows, cols, total)] + [shaped(rows, cols, pair_frames, dtype=jnp.bfloat16)] * 2,
        input_output_aliases=aliases,
        cost_estimate=cost(rows * cols * groups * LANES * 200, rows * cols * groups * LANES * 16),
        compiler_params=grant(16),
        name="diffuse",
    )(*operands)


def footprints_call(scalars, own, entries):
    count = len(entries) + 1
    share, pixel_count = own.shape
    rank = share * count
    block = pixel_count
    steps = pixel_count // block

    def kernel(scalars, *refs):
        own_ref = refs[0]
        entry_refs = [(refs[1 + 2 * k], refs[2 + 2 * k]) for k in range(count - 1)]
        out_ref, gram_ref, total = refs[2 * count - 1 :]
        here = scalars[HERE]
        step = pl.program_id(0)

        def put(place, value):
            at = pl.multiple_of(place * share, share)
            high, low = split(value)
            out_ref[pl.ds(at, share), :] = high
            out_ref[pl.ds(rank + at, share), :] = low

        put(here, own_ref[...])
        for (first_ref, second_ref), (_, _, test, place) in zip(entry_refs, entries):
            put(place(here), jnp.where(test(here), first_ref[...], second_ref[...]))

        @pl.when(step == 0)
        def _():
            total[...] = jnp.zeros_like(total)

        total[...] += dot(out_ref[...], out_ref[0:rank, :], NT)

        @pl.when(step == steps - 1)
        def _():
            cross = total[rank:, :]
            gram_ref[...] = total[0:rank, :] + (cross + cross.T)

    foot_spec = pl.BlockSpec((share, block), lambda k, s: (0, k))
    flat = [array for entry in entries for array in entry[:2]]
    return pl.pallas_call(
        kernel,
        grid_spec=pltpu.PrefetchScalarGridSpec(
            num_scalar_prefetch=1,
            grid=(steps,),
            in_specs=[foot_spec] * (1 + len(flat)),
            out_specs=[
                pl.BlockSpec((2 * rank, block), lambda k, s: (0, k)),
                pl.BlockSpec((rank, rank), lambda k, s: (0, 0)),
            ],
            scratch_shapes=[pltpu.VMEM((2 * rank, rank), jnp.float32)],
        ),
        out_shape=[shaped(2 * rank, pixel_count, dtype=jnp.bfloat16), shaped(rank, rank)],
        cost_estimate=cost(4 * rank * rank * pixel_count, 8 * rank * pixel_count),
        compiler_params=grant(20),
        name="footprints",
    )(scalars, own, *flat)


def numerator_call(scalars, foot, movies, gram, trace_rows):
    rank = foot.shape[0] // 2
    pixel_count = movies[0][0].shape[0]
    spans = [high.shape[1] for high, _ in movies]
    frames = sum(spans)
    columns = frames + rank
    block = pixel_count
    steps = pixel_count // block
    chips = rank // (2 * trace_rows)

    def kernel(scalars, foot_ref, gram_ref, *refs):
        movie_refs = refs[: 2 * len(movies)]
        keep_ref, send_ref, total = refs[2 * len(movies) :]
        step = pl.program_id(0)

        @pl.when(step == 0)
        def _():
            total[...] = jnp.zeros_like(total)

        for k in range(len(movies)):
            high_ref, low_ref = movie_refs[2 * k : 2 * k + 2]
            part = fold(dot(foot_ref[...], high_ref[...], NN)) + dot(foot_ref[0:rank, :], low_ref[...], NN)
            total[:, sum(spans[:k]) : sum(spans[: k + 1])] += part

        @pl.when(step == steps - 1)
        def _():
            total[:, frames:] = gram_ref[...]
            core = scalars[CORE]
            for k in range(chips):
                chip = scalars[CHIP] ^ k
                mine = pl.multiple_of((2 * chip + core) * trace_rows, trace_rows)
                other = pl.multiple_of((2 * chip + 1 - core) * trace_rows, trace_rows)
                keep_ref[k] = total[pl.ds(mine, trace_rows), :]
                send_ref[k] = total[pl.ds(other, trace_rows), :]

    out_spec = pl.BlockSpec((chips, trace_rows, columns), lambda k, s: (0, 0, 0))
    return pl.pallas_call(
        kernel,
        grid_spec=pltpu.PrefetchScalarGridSpec(
            num_scalar_prefetch=1,
            grid=(steps,),
            in_specs=[
                pl.BlockSpec((2 * rank, block), lambda k, s: (0, k)),
                pl.BlockSpec((rank, rank), lambda k, s: (0, 0)),
            ]
            + [pl.BlockSpec((block, array.shape[1]), lambda k, s: (k, 0)) for movie in movies for array in movie],
            out_specs=[out_spec, out_spec],
            scratch_shapes=[pltpu.VMEM((rank, columns), jnp.float32)],
        ),
        out_shape=[shaped(chips, trace_rows, columns)] * 2,
        cost_estimate=cost(8 * rank * pixel_count * columns, 4 * pixel_count * (rank + columns)),
        compiler_params=grant(24),
        name="numerator",
    )(scalars, foot, gram, *[array for movie in movies for array in movie])


def traces_call(scalars, keep, arrived, parts, gathered):
    _, trace_rows, columns = keep.shape
    frames = gathered[0][0].shape[2]
    rank = columns - frames
    stacks = [stack for stack, _ in gathered]

    def kernel(scalars, *refs):
        stack_refs, refs = refs[: len(stacks)], refs[len(stacks) :]
        part_refs, (out_ref, copy_ref, full) = refs[:-3], refs[-3:]
        for stack_ref, (_, masks) in zip(stack_refs, gathered):
            for k, mask in enumerate(masks):
                device = 2 * (scalars[CHIP] ^ (mask // 2))
                device = device + (1 - scalars[CORE] if mask % 2 else scalars[CORE])
                full[pl.ds(pl.multiple_of(device * trace_rows, trace_rows), trace_rows), :] = stack_ref[k]
        total = part_refs[0][0] + part_refs[1][0]
        for part_ref in part_refs[2:]:
            total = total + part_ref[...]
        gram = stacked(total[:, frames:])
        high, low = split(full[...])
        below = fold(dot(gram, high, NN)) + dot(gram[0:trace_rows], low, NN)
        value = stack_refs[0][0] * total[:, 0:frames] / below
        out_ref[...] = value
        copy_ref[...] = value

    return pl.pallas_call(
        kernel,
        grid_spec=pltpu.PrefetchScalarGridSpec(
            num_scalar_prefetch=1,
            grid=(1,),
            in_specs=[pl.BlockSpec(stack.shape, lambda k, s: (0, 0, 0)) for stack in stacks]
            + [pl.BlockSpec((1, trace_rows, columns), lambda k, s: (0, 0, 0))] * 2
            + [pl.BlockSpec((trace_rows, columns), lambda k, s: (0, 0))] * len(parts),
            out_specs=[pl.BlockSpec((trace_rows, frames), lambda k, s: (0, 0))] * 2,
            scratch_shapes=[pltpu.VMEM((rank, frames), jnp.float32)],
        ),
        out_shape=[shaped(trace_rows, frames)] * 2,
        cost_estimate=cost(6 * trace_rows * rank * frames, 8 * rank * frames),
        compiler_params=grant(6),
        name="traces",
    )(scalars, *stacks, keep, arrived, *parts)


def products_call(scalars, near, far, movies, half, count, places, with_gram):
    chips = len(near)
    trace_rows, frames = near[0].shape
    rank = 2 * chips * trace_rows
    half_rank = rank // 2
    share = rank // count
    pixel_count = movies[0][0].shape[0]
    spans = [high.shape[1] for high, _ in movies]
    part = pixel_count // HALVES
    block = part
    steps = part // block
    columns = part + (half_rank if with_gram else 0)
    outs = len(places)

    def kernel(scalars, *refs):
        near_refs, far_refs, refs = refs[:chips], refs[chips : 2 * chips], refs[2 * chips :]
        movie_refs = refs[: 2 * len(movies)]
        refs = refs[2 * len(movies) :]
        out_refs = refs[:outs]
        full, left, result = refs[outs:]
        step = pl.program_id(0)
        here = scalars[HERE]

        @pl.when(step == 0)
        def _():
            for k in range(chips):
                device = 2 * (scalars[CHIP] ^ k) + scalars[CORE]
                full[pl.ds(pl.multiple_of(device * trace_rows, trace_rows), trace_rows), :] = near_refs[k][...]
                device = 2 * (scalars[CHIP] ^ k) + 1 - scalars[CORE]
                full[pl.ds(pl.multiple_of(device * trace_rows, trace_rows), trace_rows), :] = far_refs[k][...]
            left[...] = stacked(full[...])

        def emit(total, at):
            width = total.shape[1]
            result[:, 0:width] = total
            for k, out_ref in enumerate(out_refs):
                row = pl.multiple_of(places[k](here) * share, share)
                out_ref[:, pl.ds(at, width)] = result[pl.ds(row, share), 0:width]

        both = jnp.zeros((2 * rank, block), jnp.float32)
        upper = jnp.zeros((rank, block), jnp.float32)
        for k in range(len(movies)):
            high_ref, low_ref = movie_refs[2 * k : 2 * k + 2]
            cut = slice(sum(spans[:k]), sum(spans[: k + 1]))
            both += dot(left[:, cut], high_ref[...], NT)
            upper += dot(left[0:rank, cut], low_ref[...], NT)
        emit(fold(both) + upper, pl.multiple_of(step * block, block))
        if with_gram:

            @pl.when(step == steps - 1)
            def _():
                at = pl.multiple_of(scalars[CORE] * half_rank, half_rank)
                both = dot(left[...], left[pl.ds(at, half_rank), :], NT)
                upper = dot(left[0:rank, :], left[pl.ds(rank + at, half_rank), :], NT)
                emit(fold(both) + upper, part)

    piece = pl.BlockSpec((trace_rows, frames), lambda j, s: (0, 0))
    return pl.pallas_call(
        kernel,
        grid_spec=pltpu.PrefetchScalarGridSpec(
            num_scalar_prefetch=1,
            grid=(steps,),
            in_specs=[piece] * (2 * chips)
            + [
                pl.BlockSpec((block, array.shape[1]), lambda j, s: (half * steps + j, 0))
                for movie in movies
                for array in movie
            ],
            out_specs=[pl.BlockSpec((share, columns), lambda j, s: (0, 0))] * outs,
            scratch_shapes=[
                pltpu.VMEM((rank, frames), jnp.float32),
                pltpu.VMEM((2 * rank, frames), jnp.bfloat16),
                pltpu.VMEM((rank, block), jnp.float32),
            ],
        ),
        out_shape=[shaped(share, columns)] * outs,
        cost_estimate=cost(8 * rank * part * frames, 4 * part * (frames + rank)),
        compiler_params=grant(18),
        name="products",
    )(scalars, *near, *far, *[array for movie in movies for array in movie])


def first_final_call(scalars, own, foot, parts, gram_mine, gram_other):
    share, pixel_count = own.shape
    rank = foot.shape[0] // 2
    part = pixel_count // HALVES
    block = part
    steps = part // block

    def kernel(scalars, own_ref, foot_ref, later_ref, *refs):
        part_refs = refs[: len(parts)]
        mine, other = refs[len(parts)][...], refs[len(parts) + 1][...]
        out_ref, below_ref = refs[-2:]
        above = part_refs[0][...]
        for part_ref in part_refs[1:]:
            above = above + part_ref[...]
        first = scalars[CORE] == 0
        gram = jnp.concatenate([jnp.where(first, mine, other), jnp.where(first, other, mine)], axis=1)
        both = stacked(gram)

        def divisor(ref):
            return fold(dot(both, ref[0:rank, :], NN)) + dot(both[0:share], ref[rank:, :], NN)

        out_ref[...] = own_ref[...] * above / divisor(foot_ref)
        below_ref[...] = divisor(later_ref)

    in_specs = [
        pl.BlockSpec((share, block), lambda k, s: (0, k)),
        pl.BlockSpec((2 * rank, block), lambda k, s: (0, k)),
        pl.BlockSpec((2 * rank, block), lambda k, s: (0, steps + k)),
    ]
    in_specs += [pl.BlockSpec((share, block), lambda k, s: (0, k))] * len(parts)
    in_specs += [pl.BlockSpec((share, rank // 2), lambda k, s: (0, 0))] * 2
    return pl.pallas_call(
        kernel,
        grid_spec=pltpu.PrefetchScalarGridSpec(
            num_scalar_prefetch=1,
            grid=(steps,),
            in_specs=in_specs,
            out_specs=[pl.BlockSpec((share, block), lambda k, s: (0, k))] * 2,
        ),
        out_shape=[shaped(share, pixel_count), shaped(share, part)],
        cost_estimate=cost(12 * share * rank * part, 4 * part * (2 * rank + 5 * share)),
        compiler_params=grant(8),
        name="final",
    )(scalars, own, foot, foot, *parts, gram_mine, gram_other)


def second_final_call(own, parts, below, carried):
    share, pixel_count = own.shape
    part = pixel_count // HALVES
    block = part
    steps = part // block

    def kernel(own_ref, below_ref, *refs):
        above = refs[0][...]
        for part_ref in refs[1 : len(parts)]:
            above = above + part_ref[...]
        refs[-1][...] = own_ref[...] * above / below_ref[...]

    near = pl.BlockSpec((share, block), lambda k: (0, k))
    far = pl.BlockSpec((share, block), lambda k: (0, steps + k))
    operands = [own, below, *parts, carried]
    return pl.pallas_call(
        kernel,
        grid=(steps,),
        in_specs=[far, near] + [near] * len(parts) + [pl.BlockSpec(memory_space=pl.ANY)],
        out_specs=far,
        out_shape=shaped(share, pixel_count),
        input_output_aliases={len(operands) - 1: 0},
        cost_estimate=cost(4 * share * part, 24 * share * part),
        compiler_params=grant(6),
        name="final",
    )(*operands)


def choose_call(scalars, down, up):
    rows, columns = up.shape
    block = columns // 2

    def kernel(scalars, down_ref, up_ref, out_ref):
        out_ref[...] = jnp.where(scalars[TURNED] == 1, down_ref[...], up_ref[...])

    spec = pl.BlockSpec((rows, block), lambda k, s: (0, k))
    return pl.pallas_call(
        kernel,
        grid_spec=pltpu.PrefetchScalarGridSpec(
            num_scalar_prefetch=1, grid=(2,), in_specs=[spec, spec], out_specs=spec
        ),
        out_shape=shaped(rows, columns),
        cost_estimate=cost(rows * columns, 12 * rows * columns),
        compiler_params=grant(4),
        name="choose",
    )(scalars, down, up)


def line_gather(scalars, block, axis, count):
    if count == 4:
        middle = [(1, 2), (2, 1)]
        outward = [(1, 0), (2, 3)]
        near = lax.ppermute(block, axis, [(k, k ^ 1) for k in range(count)])
        across = lax.ppermute(block, axis, middle)
        far = lax.ppermute(near, axis, middle)
        out_across = lax.ppermute(across, axis, outward)
        out_far = lax.ppermute(far, axis, outward)

        def between(here):
            return (here == 1) | (here == 2)

        return [
            (near, near, between, lambda here: here ^ 1),
            (across, out_across, between, lambda here: jnp.where(here < 2, 2, 1)),
            (far, out_far, between, lambda here: jnp.where(here < 2, 3, 0)),
        ]
    up, down = {}, {}
    last_up = last_down = block
    for r in range(1, count):
        up_pairs = [(k, k + 1) for k in range(r - 1, count - 1)]
        down_pairs = [(k + 1, k) for k in range(0, count - r)]
        if r == count - 1 and count != 3:
            merged = choose_call(scalars, last_down, last_up) if count > 2 else block
            last_up = last_down = lax.ppermute(merged, axis, up_pairs + down_pairs)
        else:
            last_up = lax.ppermute(last_up, axis, up_pairs)
            last_down = lax.ppermute(last_down, axis, down_pairs)
        up[r], down[r] = last_up, last_down
    return [
        (down[s], up[count - s], lambda here, s=s: here + s < count, lambda here, s=s: lax.rem(here + s, count))
        for s in range(1, count)
    ]


def scatter_places(count):
    if count == 4:
        return [
            lambda here: here,
            lambda here: here ^ 1,
            lambda here: 3 - here,
            lambda here: lax.rem(here + 2, count),
        ]
    slots = [lambda here, s=s: lax.rem(here + s, count) for s in range(count)]
    return slots + [lambda here: lax.rem(here + jnp.where(here == 0, count - 1, 1), count)]


def line_scatter(blocks, axis, count):
    if count == 4:
        own, beside, opposite, remaining = blocks
        inward = [(0, 1), (3, 2)]
        middle = [(1, 2), (2, 1)]
        first = lax.ppermute(opposite, axis, inward)
        second = lax.ppermute(remaining, axis, inward)
        third = lax.ppermute(remaining + first, axis, middle)
        fourth = lax.ppermute(beside + third, axis, [(k, k ^ 1) for k in range(count)])
        fifth = lax.ppermute(opposite + second, axis, middle)
        return [own, fourth, fifth]
    up_last = down_last = None
    for r in range(1, count):
        up_pairs = [(k, k + 1) for k in range(r)]
        down_pairs = [(count - 1 - k, count - 2 - k) for k in range(r)]
        if r == 1 and count > 3:
            up_last = down_last = lax.ppermute(blocks[count], axis, up_pairs + down_pairs)
            continue
        up_block, down_block = blocks[count - r], blocks[r]
        if r > 1:
            up_block = up_block + up_last
            down_block = down_block + down_last
        up_last = lax.ppermute(up_block, axis, up_pairs)
        down_last = lax.ppermute(down_block, axis, down_pairs)
    return [blocks[0], up_last, down_last]


def compute(raw_movie, footprints, traces):
    rows, cols, frame_count = raw_movie.shape
    pixel_count = rows * cols
    pix_count = lax.axis_size("pix")
    count = lax.axis_size("tm")
    pix = lax.axis_index("pix")
    here = lax.axis_index("tm")
    core = lax.rem(pix, 2)
    trace_rows = traces.shape[0]
    blocks = frame_count // LANES
    quarter = max(blocks // 4, 1)
    widths = [2 * quarter, blocks - 2 * quarter]
    halo = SUBSTEPS

    def swap(mask):
        return [(k, k ^ mask) for k in range(pix_count)]

    inner = (pix > 0).astype(jnp.int32)
    outer = (pix < pix_count - 1).astype(jnp.int32)
    turned = (here == 1).astype(jnp.int32)
    bend = (lax.rem(pix, GROUP) == 0) * inner + (lax.rem(pix, GROUP) == GROUP - 1) * outer
    flags = scalars = jnp.stack([here, core, lax.div(pix, 2), turned, inner, outer, bend]).astype(jnp.int32)

    entries = line_gather(scalars, footprints, "tm", count)

    bent = [k for k in range(pix_count - 1) if k % GROUP == GROUP - 1] if pix_count % GROUP == 0 else []
    begins = [sum(widths[:c]) * LANES for c in range(len(widths))]
    spans = [(begin, width * LANES) for begin, width in zip(begins, widths)]
    outward_rows = [
        lax.dynamic_slice(raw_movie, (core * (rows - halo), 0, 0), (halo, cols, widths[0] * LANES))
    ]
    later = edges_call(
        flags, raw_movie, halo, [(True, *span) for span in spans[1:]] + [(False, *span) for span in spans]
    )
    outward_rows += later[: len(spans) - 1]
    inward_rows = later[len(spans) - 1 :]
    halos = []
    for c, (inward, outward) in enumerate(zip(inward_rows, outward_rows)):
        last = c == len(widths) - 1 and bool(bent)
        joins = [(k, k + 1) for k in range(1, pix_count - 1, 2) if not (last and k in bent)]
        joins += [(b, a) for a, b in joins]
        detour = None
        if last:
            first = [(k, k + GROUP) for k in bent] + [(k + 1, k + 1 - GROUP) for k in bent]
            second = [(k + GROUP, k + 1) for k in bent] + [(k + 1 - GROUP, k) for k in bent]
            detour = lax.ppermute(outward, "pix", first)
            detour = lax.ppermute(detour, "pix", second)
        from_outer = lax.ppermute(outward, "pix", joins)
        from_inner = lax.ppermute(inward, "pix", swap(1))
        halos.append((from_inner, from_outer, detour))

    held, masks = traces[None], [0]
    hops = [mask for mask in (4, 8, 16, 32, 64, 1) if mask < pix_count]
    for mask in hops:
        held = jnp.concatenate([held, lax.ppermute(held, "pix", swap(mask))], axis=0)
        masks = masks + [mask ^ m for m in masks]
    gathered = [(held, masks)]
    if pix_count > 2:
        gathered.append((lax.ppermute(held, "pix", swap(2)), [2 ^ m for m in masks]))

    current = None
    movies = []
    for c, width in enumerate(widths):
        pair = (None, None)
        calls = 1
        for part in range(calls):
            groups = width // calls
            skip = part * groups
            current, *pair = diffuse_call(
                flags, raw_movie, *halos[c], current, pair,
                sum(widths[:c]) + skip, skip, width * LANES, skip, groups,
            )
        movies.append(tuple(array.reshape(pixel_count, width * LANES) for array in pair))

    foot, gram = footprints_call(scalars, footprints, entries)
    keep, send = numerator_call(scalars, foot, movies, gram, trace_rows)
    arrived = lax.ppermute(send, "pix", swap(1))
    parts = []
    for k in range(1, keep.shape[0]):
        parts.append(lax.ppermute(keep[k] + arrived[k], "pix", swap(2 * k)))
    new_traces, again = traces_call(scalars, keep, arrived, parts, gathered)
    near = [again]
    for k in range(1, keep.shape[0]):
        near.append(lax.ppermute(again, "pix", swap(2 * k)))
    far = []
    for piece in near:
        far.append(lax.ppermute(piece, "pix", swap(1)))

    products = []
    for h in range(HALVES):
        products.append(products_call(scalars, near, far, movies, h, count, scatter_places(count), h == 0))
    sums = [line_scatter(blocks, "tm", count) for blocks in products]
    part = pixel_count // HALVES
    gram_mine = sum(array[:, part:] for array in sums[0])
    gram_other = lax.ppermute(gram_mine, "pix", swap(1))
    new_footprints, below = first_final_call(scalars, footprints, foot, sums[0], gram_mine, gram_other)
    new_footprints = second_final_call(footprints, sums[1], below, new_footprints)
    return current, new_footprints, new_traces


def solution(mesh):
    placed = (P("pix", None, "tm"), P("tm", "pix"), P("pix", "tm"))
    return jax.shard_map(
        compute,
        mesh=mesh,
        in_specs=placed,
        out_specs=(P("pix", None, "tm"), P("tm", "pix"), P("pix", "tm")),
        check_vma=False,
    )
```

```python
import jax
import jax.numpy as jnp
from jax import lax
from jax.experimental import pallas as pl
from jax.experimental.pallas import tpu as pltpu
from jax.sharding import PartitionSpec as P


edge_square = 0.25
step_scale = 0.06
SUBSTEPS = 4
LANES = 128
GROUP = 4
HALVES = 2

HERE, CORE, CHIP, TURNED, INSIDE, BENT = 0, 1, 2, 3, 4, 6

NN = ((1,), (0,))
NT = ((1,), (1,))


def flux_quarter(change):
    return change / (change * change + edge_square)


def split(value):
    high = value.astype(jnp.bfloat16)
    low = (value - high.astype(jnp.float32)).astype(jnp.bfloat16)
    return high, low


def stacked(value):
    return jnp.concatenate(split(value), axis=0)


def dot(left, right, dims):
    return lax.dot_general(left, right, (dims, ((), ())), preferred_element_type=jnp.float32)


def fold(value):
    half = value.shape[0] // 2
    return value[:half] + value[half:]


def grant(mebibytes):
    return pltpu.CompilerParams(vmem_limit_bytes=mebibytes * 1024 * 1024)


def cost(flops, moved):
    return pl.CostEstimate(flops=flops, bytes_accessed=moved, transcendentals=0)


def shaped(*shape, dtype=jnp.float32):
    return jax.ShapeDtypeStruct(shape, dtype)


def edges_call(flags, raw, halo, wanted):
    rows, cols, _ = raw.shape
    shift = rows - halo

    def kernel(flags, raw_ref, *refs):
        out_refs, sems = refs[:-1], refs[-1]
        core = flags[CORE]
        copies = []
        for k, (outward, begin, frames) in enumerate(wanted):
            start = (core if outward else 1 - core) * shift
            copies.append(
                pltpu.make_async_copy(
                    raw_ref.at[pl.ds(start, halo), :, pl.ds(begin, frames)], out_refs[k], sems.at[k]
                )
            )
        for copy in copies:
            copy.start()
        for copy in copies:
            copy.wait()

    blocks = [(halo, cols, frames) for _, _, frames in wanted]
    return pl.pallas_call(
        kernel,
        grid_spec=pltpu.PrefetchScalarGridSpec(
            num_scalar_prefetch=1,
            grid=(1,),
            in_specs=[pl.BlockSpec(memory_space=pltpu.HBM)],
            out_specs=[pl.BlockSpec(block, lambda i, flags: (0, 0, 0)) for block in blocks],
            scratch_shapes=[pltpu.SemaphoreType.DMA((len(wanted),))],
        ),
        out_shape=[shaped(*block) for block in blocks],
        cost_estimate=cost(1, sum(8 * halo * cols * frames for _, _, frames in wanted)),
        compiler_params=grant(10),
        name="edges",
    )(flags, raw)


def diffuse_call(flags, raw, halo_inner, halo_outer, detour, movie, pair, begin, pair_begin, pair_frames, skip, groups):
    rows, cols, total = raw.shape
    halo = halo_inner.shape[0]
    carried = [array for array in (movie, *pair) if array is not None]
    width = 128
    pad = 8
    extended = rows + 2 * halo
    inputs = 3 if detour is None else 4

    def kernel(flags, *refs):
        sources, refs = refs[:inputs], refs[inputs:]
        refs = refs[len(carried) :]
        out_ref, high_ref, low_ref, first_bufs, second_buf, out_bufs, in_sems, out_sems = refs
        group = pl.program_id(0)
        slot = lax.rem(group, 2)
        inside = pl.ds(pad, cols)

        def fetches(at):
            here = lax.rem(at, 2)
            lanes = pl.ds(pl.multiple_of((skip + at) * LANES, LANES), LANES)
            wide = pl.ds(pl.multiple_of((begin + at) * LANES, LANES), LANES)

            def one(ref, cut, start, count, part):
                return pltpu.make_async_copy(
                    ref.at[:, :, cut], first_bufs.at[here, pl.ds(start, count), inside, :], in_sems.at[here, part]
                )

            far_side = halo + rows
            inner_at = (1 - flags[CORE]) * far_side
            outer_at = flags[CORE] * far_side
            made = [
                (None, one(sources[0], wide, halo, rows, 0)),
                (None, one(sources[1], lanes, inner_at, halo, 1)),
            ]
            plain = one(sources[2], lanes, outer_at, halo, 2)
            if detour is None:
                made.append((None, plain))
            else:
                made.append((flags[BENT] == 0, plain))
                made.append((flags[BENT] == 1, one(sources[3], lanes, outer_at, halo, 2)))
            return made

        def run(at, act):
            for condition, copy in fetches(at):
                if condition is None:
                    act(copy)
                else:
                    pl.when(condition)(lambda copy=copy: act(copy))

        def give(at):
            wide = pl.ds(pl.multiple_of((begin + at) * LANES, LANES), LANES)
            here = lax.rem(at, 2)
            return pltpu.make_async_copy(out_bufs.at[here], out_ref.at[:, :, wide], out_sems.at[here])

        @pl.when(group == 0)
        def _():
            run(group, lambda copy: copy.start())

        @pl.when(group + 1 < groups)
        def _():
            run(group + 1, lambda copy: copy.start())

        zero = jnp.zeros((extended, pad, LANES), jnp.float32)
        first_buf = first_bufs.at[slot]
        for buf in (first_buf, second_buf):
            buf[:, 0:pad, :] = zero
            buf[:, pad + cols :, :] = zero
        run(group, lambda copy: copy.wait())

        @pl.when(group >= 2)
        def _():
            give(group - 2).wait()

        scale_up = step_scale * flags[INSIDE].astype(jnp.float32)
        scale_down = step_scale * flags[INSIDE + 1].astype(jnp.float32)
        head = lax.broadcasted_iota(jnp.int32, (width, LANES), 0) == 0
        bufs = (first_buf, second_buf)
        for step in range(SUBSTEPS):
            src, dst = bufs[step % 2], bufs[1 - step % 2]
            top = step
            middle = range(step + 1, extended - step - 1)

            def tile(j, left_flux):
                base = pl.multiple_of(pad + j * width, 8)
                col = pl.multiple_of(j * width, width)
                kept = []
                current = src[top + 1, pl.ds(base, width), :]
                flux_up = flux_quarter(current - src[top, pl.ds(base, width), :])
                for k, row in enumerate(middle):
                    below = src[row + 1, pl.ds(base, width), :]
                    flux_down = flux_quarter(below - current)
                    flux_right = flux_quarter(src[row, pl.ds(base + 1, width), :] - current)
                    rolled = pltpu.roll(flux_right, 1, 0)
                    flux_left = jnp.where(head, left_flux[k], rolled)
                    scale = step_scale
                    if row < halo:
                        scale = scale_up
                    if row >= halo + rows:
                        scale = scale_down
                    value = current + scale * ((flux_down - flux_up) + (flux_right - flux_left))
                    kept.append(rolled)
                    if step + 1 < SUBSTEPS:
                        dst[row, pl.ds(base, width), :] = value
                    else:
                        out_bufs[slot, row - halo, pl.ds(col, width), :] = value
                        high, low = split(value)
                        high_ref[row - halo, pl.ds(col, width), :] = high
                        low_ref[row - halo, pl.ds(col, width), :] = low
                    current, flux_up = below, flux_down
                return tuple(kept)

            edge = tuple(flux_quarter(src[row, pl.ds(pad, width), :]) for row in middle)
            lax.fori_loop(0, cols // width, tile, edge)
        give(group).start()

        @pl.when(group == groups - 1)
        def _():
            if groups > 1:
                give(group - 1).wait()
            give(group).wait()

    outside = pl.BlockSpec(memory_space=pltpu.HBM)
    operands = [flags, raw, halo_inner, halo_outer]
    if detour is not None:
        operands.append(detour)
    outputs = [k for k, array in enumerate((movie, *pair)) if array is not None]
    aliases = {len(operands) + k: output for k, output in enumerate(outputs)}
    operands += carried
    padded = (extended, cols + 2 * pad, LANES)
    return pl.pallas_call(
        kernel,
        grid_spec=pltpu.PrefetchScalarGridSpec(
            num_scalar_prefetch=1,
            grid=(groups,),
            in_specs=[outside] * (len(operands) - 1 - len(carried))
            + [pl.BlockSpec(memory_space=pl.ANY)] * len(carried),
            out_specs=[outside] + [pl.BlockSpec((rows, cols, LANES), lambda i, flags: (0, 0, pair_begin + i))] * 2,
            scratch_shapes=[
                pltpu.VMEM((2, *padded), jnp.float32),
                pltpu.VMEM(padded, jnp.float32),
                pltpu.VMEM((2, rows, cols, LANES), jnp.float32),
                pltpu.SemaphoreType.DMA((2, 3)),
                pltpu.SemaphoreType.DMA((2,)),
            ],
        ),
        out_shape=[shaped(rows, cols, total)] + [shaped(rows, cols, pair_frames, dtype=jnp.bfloat16)] * 2,
        input_output_aliases=aliases,
        cost_estimate=cost(rows * cols * groups * LANES * 200, rows * cols * groups * LANES * 16),
        compiler_params=grant(16),
        name="diffuse",
    )(*operands)


def footprints_call(scalars, own, entries):
    count = len(entries) + 1
    flat, positions = [], []
    for first, second, _, _ in entries:
        at = len(flat)
        flat += [first] if second is first else [first, second]
        positions.append((at, len(flat) - 1))
    share, pixel_count = own.shape
    rank = share * count
    block = pixel_count
    steps = pixel_count // block

    def kernel(scalars, *refs):
        own_ref = refs[0]
        entry_refs = [(refs[1 + a], refs[1 + b]) for a, b in positions]
        out_ref, gram_ref, total = refs[1 + len(flat) :]
        here = scalars[HERE]
        step = pl.program_id(0)

        def put(place, value):
            at = pl.multiple_of(place * share, share)
            high, low = split(value)
            out_ref[pl.ds(at, share), :] = high
            out_ref[pl.ds(rank + at, share), :] = low

        put(here, own_ref[...])
        for (first_ref, second_ref), (_, _, test, place) in zip(entry_refs, entries):
            put(place(here), jnp.where(test(here), first_ref[...], second_ref[...]))

        @pl.when(step == 0)
        def _():
            total[...] = jnp.zeros_like(total)

        total[...] += dot(out_ref[...], out_ref[0:rank, :], NT)

        @pl.when(step == steps - 1)
        def _():
            cross = total[rank:, :]
            gram_ref[...] = total[0:rank, :] + (cross + cross.T)

    foot_spec = pl.BlockSpec((share, block), lambda k, s: (0, k))
    return pl.pallas_call(
        kernel,
        grid_spec=pltpu.PrefetchScalarGridSpec(
            num_scalar_prefetch=1,
            grid=(steps,),
            in_specs=[foot_spec] * (1 + len(flat)),
            out_specs=[
                pl.BlockSpec((2 * rank, block), lambda k, s: (0, k)),
                pl.BlockSpec((rank, rank), lambda k, s: (0, 0)),
            ],
            scratch_shapes=[pltpu.VMEM((2 * rank, rank), jnp.float32)],
        ),
        out_shape=[shaped(2 * rank, pixel_count, dtype=jnp.bfloat16), shaped(rank, rank)],
        cost_estimate=cost(4 * rank * rank * pixel_count, 8 * rank * pixel_count),
        compiler_params=grant(20),
        name="footprints",
    )(scalars, own, *flat)


def numerator_call(scalars, foot, movies, gram, trace_rows):
    rank = foot.shape[0] // 2
    pixel_count = movies[0][0].shape[0]
    spans = [high.shape[1] for high, _ in movies]
    frames = sum(spans)
    columns = frames + rank
    block = pixel_count
    steps = pixel_count // block
    chips = rank // (2 * trace_rows)

    def kernel(scalars, foot_ref, gram_ref, *refs):
        movie_refs = refs[: 2 * len(movies)]
        keep_ref, send_ref, total = refs[2 * len(movies) :]
        step = pl.program_id(0)

        @pl.when(step == 0)
        def _():
            total[...] = jnp.zeros_like(total)

        for k in range(len(movies)):
            high_ref, low_ref = movie_refs[2 * k : 2 * k + 2]
            part = fold(dot(foot_ref[...], high_ref[...], NN)) + dot(foot_ref[0:rank, :], low_ref[...], NN)
            total[:, sum(spans[:k]) : sum(spans[: k + 1])] += part

        @pl.when(step == steps - 1)
        def _():
            total[:, frames:] = gram_ref[...]
            core = scalars[CORE]
            for k in range(chips):
                chip = scalars[CHIP] ^ k
                mine = pl.multiple_of((2 * chip + core) * trace_rows, trace_rows)
                other = pl.multiple_of((2 * chip + 1 - core) * trace_rows, trace_rows)
                keep_ref[k] = total[pl.ds(mine, trace_rows), :]
                send_ref[k] = total[pl.ds(other, trace_rows), :]

    out_spec = pl.BlockSpec((chips, trace_rows, columns), lambda k, s: (0, 0, 0))
    return pl.pallas_call(
        kernel,
        grid_spec=pltpu.PrefetchScalarGridSpec(
            num_scalar_prefetch=1,
            grid=(steps,),
            in_specs=[
                pl.BlockSpec((2 * rank, block), lambda k, s: (0, k)),
                pl.BlockSpec((rank, rank), lambda k, s: (0, 0)),
            ]
            + [pl.BlockSpec((block, array.shape[1]), lambda k, s: (k, 0)) for movie in movies for array in movie],
            out_specs=[out_spec, out_spec],
            scratch_shapes=[pltpu.VMEM((rank, columns), jnp.float32)],
        ),
        out_shape=[shaped(chips, trace_rows, columns)] * 2,
        cost_estimate=cost(8 * rank * pixel_count * columns, 4 * pixel_count * (rank + columns)),
        compiler_params=grant(24),
        name="numerator",
    )(scalars, foot, gram, *[array for movie in movies for array in movie])


def traces_call(scalars, keep, arrived, parts, gathered):
    _, trace_rows, columns = keep.shape
    frames = gathered[0][0].shape[2]
    rank = columns - frames
    stacks = [stack for stack, _ in gathered]

    def kernel(scalars, *refs):
        stack_refs, refs = refs[: len(stacks)], refs[len(stacks) :]
        part_refs, (out_ref, copy_ref, full) = refs[:-3], refs[-3:]
        for stack_ref, (_, masks) in zip(stack_refs, gathered):
            for k, mask in enumerate(masks):
                device = 2 * (scalars[CHIP] ^ (mask // 2))
                device = device + (1 - scalars[CORE] if mask % 2 else scalars[CORE])
                full[pl.ds(pl.multiple_of(device * trace_rows, trace_rows), trace_rows), :] = stack_ref[k]
        total = part_refs[0][0] + part_refs[1][0]
        for part_ref in part_refs[2:]:
            total = total + part_ref[...]
        gram = stacked(total[:, frames:])
        high, low = split(full[...])
        below = fold(dot(gram, high, NN)) + dot(gram[0:trace_rows], low, NN)
        value = stack_refs[0][0] * total[:, 0:frames] / below
        out_ref[...] = value
        copy_ref[...] = value

    return pl.pallas_call(
        kernel,
        grid_spec=pltpu.PrefetchScalarGridSpec(
            num_scalar_prefetch=1,
            grid=(1,),
            in_specs=[pl.BlockSpec(stack.shape, lambda k, s: (0, 0, 0)) for stack in stacks]
            + [pl.BlockSpec((1, trace_rows, columns), lambda k, s: (0, 0, 0))] * 2
            + [pl.BlockSpec((trace_rows, columns), lambda k, s: (0, 0))] * len(parts),
            out_specs=[pl.BlockSpec((trace_rows, frames), lambda k, s: (0, 0))] * 2,
            scratch_shapes=[pltpu.VMEM((rank, frames), jnp.float32)],
        ),
        out_shape=[shaped(trace_rows, frames)] * 2,
        cost_estimate=cost(6 * trace_rows * rank * frames, 8 * rank * frames),
        compiler_params=grant(6),
        name="traces",
    )(scalars, *stacks, keep, arrived, *parts)


def products_call(scalars, near, far, movies, half, count, places, with_gram):
    chips = len(near)
    trace_rows, frames = near[0].shape
    rank = 2 * chips * trace_rows
    half_rank = rank // 2
    share = rank // count
    pixel_count = movies[0][0].shape[0]
    spans = [high.shape[1] for high, _ in movies]
    part = pixel_count // HALVES
    block = part
    steps = part // block
    columns = part + (half_rank if with_gram else 0)
    outs = len(places)

    def kernel(scalars, *refs):
        near_refs, far_refs, refs = refs[:chips], refs[chips : 2 * chips], refs[2 * chips :]
        movie_refs = refs[: 2 * len(movies)]
        refs = refs[2 * len(movies) :]
        out_refs = refs[:outs]
        full, left, result = refs[outs:]
        step = pl.program_id(0)
        here = scalars[HERE]

        @pl.when(step == 0)
        def _():
            for k in range(chips):
                device = 2 * (scalars[CHIP] ^ k) + scalars[CORE]
                full[pl.ds(pl.multiple_of(device * trace_rows, trace_rows), trace_rows), :] = near_refs[k][...]
                device = 2 * (scalars[CHIP] ^ k) + 1 - scalars[CORE]
                full[pl.ds(pl.multiple_of(device * trace_rows, trace_rows), trace_rows), :] = far_refs[k][...]
            left[...] = stacked(full[...])

        def emit(total, at):
            width = total.shape[1]
            result[:, 0:width] = total
            for k, out_ref in enumerate(out_refs):
                row = pl.multiple_of(places[k](here) * share, share)
                out_ref[:, pl.ds(at, width)] = result[pl.ds(row, share), 0:width]

        both = jnp.zeros((2 * rank, block), jnp.float32)
        upper = jnp.zeros((rank, block), jnp.float32)
        for k in range(len(movies)):
            high_ref, low_ref = movie_refs[2 * k : 2 * k + 2]
            cut = slice(sum(spans[:k]), sum(spans[: k + 1]))
            both += dot(left[:, cut], high_ref[...], NT)
            upper += dot(left[0:rank, cut], low_ref[...], NT)
        emit(fold(both) + upper, pl.multiple_of(step * block, block))
        if with_gram:

            @pl.when(step == steps - 1)
            def _():
                at = pl.multiple_of(scalars[CORE] * half_rank, half_rank)
                both = dot(left[...], left[pl.ds(at, half_rank), :], NT)
                upper = dot(left[0:rank, :], left[pl.ds(rank + at, half_rank), :], NT)
                emit(fold(both) + upper, part)

    piece = pl.BlockSpec((trace_rows, frames), lambda j, s: (0, 0))
    return pl.pallas_call(
        kernel,
        grid_spec=pltpu.PrefetchScalarGridSpec(
            num_scalar_prefetch=1,
            grid=(steps,),
            in_specs=[piece] * (2 * chips)
            + [
                pl.BlockSpec((block, array.shape[1]), lambda j, s: (half * steps + j, 0))
                for movie in movies
                for array in movie
            ],
            out_specs=[pl.BlockSpec((share, columns), lambda j, s: (0, 0))] * outs,
            scratch_shapes=[
                pltpu.VMEM((rank, frames), jnp.float32),
                pltpu.VMEM((2 * rank, frames), jnp.bfloat16),
                pltpu.VMEM((rank, block), jnp.float32),
            ],
        ),
        out_shape=[shaped(share, columns)] * outs,
        cost_estimate=cost(8 * rank * part * frames, 4 * part * (frames + rank)),
        compiler_params=grant(18),
        name="products",
    )(scalars, *near, *far, *[array for movie in movies for array in movie])


def first_final_call(scalars, own, foot, parts, gram_mine, gram_other):
    share, pixel_count = own.shape
    rank = foot.shape[0] // 2
    part = pixel_count // HALVES
    block = part
    steps = part // block

    def kernel(scalars, own_ref, foot_ref, later_ref, *refs):
        part_refs = refs[: len(parts)]
        mine, other = refs[len(parts)][...], refs[len(parts) + 1][...]
        out_ref, below_ref = refs[-2:]
        above = part_refs[0][...]
        for part_ref in part_refs[1:]:
            above = above + part_ref[...]
        first = scalars[CORE] == 0
        gram = jnp.concatenate([jnp.where(first, mine, other), jnp.where(first, other, mine)], axis=1)
        both = stacked(gram)

        def divisor(ref):
            return fold(dot(both, ref[0:rank, :], NN)) + dot(both[0:share], ref[rank:, :], NN)

        out_ref[...] = own_ref[...] * above / divisor(foot_ref)
        below_ref[...] = divisor(later_ref)

    in_specs = [
        pl.BlockSpec((share, block), lambda k, s: (0, k)),
        pl.BlockSpec((2 * rank, block), lambda k, s: (0, k)),
        pl.BlockSpec((2 * rank, block), lambda k, s: (0, steps + k)),
    ]
    in_specs += [pl.BlockSpec((share, block), lambda k, s: (0, k))] * len(parts)
    in_specs += [pl.BlockSpec((share, rank // 2), lambda k, s: (0, 0))] * 2
    return pl.pallas_call(
        kernel,
        grid_spec=pltpu.PrefetchScalarGridSpec(
            num_scalar_prefetch=1,
            grid=(steps,),
            in_specs=in_specs,
            out_specs=[pl.BlockSpec((share, block), lambda k, s: (0, k))] * 2,
        ),
        out_shape=[shaped(share, pixel_count), shaped(share, part)],
        cost_estimate=cost(12 * share * rank * part, 4 * part * (2 * rank + 5 * share)),
        compiler_params=grant(8),
        name="final",
    )(scalars, own, foot, foot, *parts, gram_mine, gram_other)


def second_final_call(own, parts, below, carried):
    share, pixel_count = own.shape
    part = pixel_count // HALVES
    block = part
    steps = part // block

    def kernel(own_ref, below_ref, *refs):
        above = refs[0][...]
        for part_ref in refs[1 : len(parts)]:
            above = above + part_ref[...]
        refs[-1][...] = own_ref[...] * above / below_ref[...]

    near = pl.BlockSpec((share, block), lambda k: (0, k))
    far = pl.BlockSpec((share, block), lambda k: (0, steps + k))
    operands = [own, below, *parts, carried]
    return pl.pallas_call(
        kernel,
        grid=(steps,),
        in_specs=[far, near] + [near] * len(parts) + [pl.BlockSpec(memory_space=pl.ANY)],
        out_specs=far,
        out_shape=shaped(share, pixel_count),
        input_output_aliases={len(operands) - 1: 0},
        cost_estimate=cost(4 * share * part, 24 * share * part),
        compiler_params=grant(6),
        name="final",
    )(*operands)


def choose_call(scalars, down, up):
    rows, columns = up.shape
    block = columns // 2

    def kernel(scalars, down_ref, up_ref, out_ref):
        out_ref[...] = jnp.where(scalars[TURNED] == 1, down_ref[...], up_ref[...])

    spec = pl.BlockSpec((rows, block), lambda k, s: (0, k))
    return pl.pallas_call(
        kernel,
        grid_spec=pltpu.PrefetchScalarGridSpec(
            num_scalar_prefetch=1, grid=(2,), in_specs=[spec, spec], out_specs=spec
        ),
        out_shape=shaped(rows, columns),
        cost_estimate=cost(rows * columns, 12 * rows * columns),
        compiler_params=grant(4),
        name="choose",
    )(scalars, down, up)


def line_gather(scalars, block, axis, count):
    if count == 4:
        middle = [(1, 2), (2, 1)]
        outward = [(1, 0), (2, 3)]
        near = lax.ppermute(block, axis, [(k, k ^ 1) for k in range(count)])
        across = lax.ppermute(block, axis, middle)
        far = lax.ppermute(near, axis, middle)
        out_across = lax.ppermute(across, axis, outward)
        out_far = lax.ppermute(far, axis, outward)

        def between(here):
            return (here == 1) | (here == 2)

        return [
            (near, near, between, lambda here: here ^ 1),
            (across, out_across, between, lambda here: jnp.where(here < 2, 2, 1)),
            (far, out_far, between, lambda here: jnp.where(here < 2, 3, 0)),
        ]
    up, down = {}, {}
    last_up = last_down = block
    for r in range(1, count):
        up_pairs = [(k, k + 1) for k in range(r - 1, count - 1)]
        down_pairs = [(k + 1, k) for k in range(0, count - r)]
        if r == count - 1 and count != 3:
            merged = choose_call(scalars, last_down, last_up) if count > 2 else block
            last_up = last_down = lax.ppermute(merged, axis, up_pairs + down_pairs)
        else:
            last_up = lax.ppermute(last_up, axis, up_pairs)
            last_down = lax.ppermute(last_down, axis, down_pairs)
        up[r], down[r] = last_up, last_down
    return [
        (down[s], up[count - s], lambda here, s=s: here + s < count, lambda here, s=s: lax.rem(here + s, count))
        for s in range(1, count)
    ]


def scatter_places(count):
    if count == 4:
        return [
            lambda here: here,
            lambda here: here ^ 1,
            lambda here: 3 - here,
            lambda here: lax.rem(here + 2, count),
        ]
    slots = [lambda here, s=s: lax.rem(here + s, count) for s in range(count)]
    return slots + [lambda here: lax.rem(here + jnp.where(here == 0, count - 1, 1), count)]


def line_scatter(blocks, axis, count):
    if count == 4:
        own, beside, opposite, remaining = blocks
        inward = [(0, 1), (3, 2)]
        middle = [(1, 2), (2, 1)]
        first = lax.ppermute(opposite, axis, inward)
        second = lax.ppermute(remaining, axis, inward)
        third = lax.ppermute(remaining + first, axis, middle)
        fourth = lax.ppermute(beside + third, axis, [(k, k ^ 1) for k in range(count)])
        fifth = lax.ppermute(opposite + second, axis, middle)
        return [own, fourth, fifth]
    up_last = down_last = None
    for r in range(1, count):
        up_pairs = [(k, k + 1) for k in range(r)]
        down_pairs = [(count - 1 - k, count - 2 - k) for k in range(r)]
        if r == 1 and count > 3:
            up_last = down_last = lax.ppermute(blocks[count], axis, up_pairs + down_pairs)
            continue
        up_block, down_block = blocks[count - r], blocks[r]
        if r > 1:
            up_block = up_block + up_last
            down_block = down_block + down_last
        up_last = lax.ppermute(up_block, axis, up_pairs)
        down_last = lax.ppermute(down_block, axis, down_pairs)
    return [blocks[0], up_last, down_last]


def compute(raw_movie, footprints, traces):
    rows, cols, frame_count = raw_movie.shape
    pixel_count = rows * cols
    pix_count = lax.axis_size("pix")
    count = lax.axis_size("tm")
    pix = lax.axis_index("pix")
    here = lax.axis_index("tm")
    core = lax.rem(pix, 2)
    trace_rows = traces.shape[0]
    blocks = frame_count // LANES
    quarter = max(blocks // 4, 1)
    widths = [2 * quarter, blocks - 2 * quarter]
    halo = SUBSTEPS

    def swap(mask):
        return [(k, k ^ mask) for k in range(pix_count)]

    inner = (pix > 0).astype(jnp.int32)
    outer = (pix < pix_count - 1).astype(jnp.int32)
    turned = (here == 1).astype(jnp.int32)
    bend = (lax.rem(pix, GROUP) == 0) * inner + (lax.rem(pix, GROUP) == GROUP - 1) * outer
    flags = scalars = jnp.stack([here, core, lax.div(pix, 2), turned, inner, outer, bend]).astype(jnp.int32)

    entries = line_gather(scalars, footprints, "tm", count)

    bent = [k for k in range(pix_count - 1) if k % GROUP == GROUP - 1] if pix_count % GROUP == 0 else []
    begins = [sum(widths[:c]) * LANES for c in range(len(widths))]
    spans = [(begin, width * LANES) for begin, width in zip(begins, widths)]
    outward_rows = [
        lax.dynamic_slice(raw_movie, (core * (rows - halo), 0, 0), (halo, cols, widths[0] * LANES))
    ]
    later = edges_call(
        flags, raw_movie, halo, [(True, *span) for span in spans[1:]] + [(False, *span) for span in spans]
    )
    outward_rows += later[: len(spans) - 1]
    inward_rows = later[len(spans) - 1 :]
    halos = []
    for c, (inward, outward) in enumerate(zip(inward_rows, outward_rows)):
        last = c == len(widths) - 1 and bool(bent)
        joins = [(k, k + 1) for k in range(1, pix_count - 1, 2) if not (last and k in bent)]
        joins += [(b, a) for a, b in joins]
        detour = None
        if last:
            first = [(k, k + GROUP) for k in bent] + [(k + 1, k + 1 - GROUP) for k in bent]
            second = [(k + GROUP, k + 1) for k in bent] + [(k + 1 - GROUP, k) for k in bent]
            detour = lax.ppermute(outward, "pix", first)
            detour = lax.ppermute(detour, "pix", second)
        from_outer = lax.ppermute(outward, "pix", joins)
        from_inner = lax.ppermute(inward, "pix", swap(1))
        halos.append((from_inner, from_outer, detour))

    held, masks = traces[None], [0]
    hops = [mask for mask in (4, 8, 16, 32, 64, 1) if mask < pix_count]
    for mask in hops:
        held = jnp.concatenate([held, lax.ppermute(held, "pix", swap(mask))], axis=0)
        masks = masks + [mask ^ m for m in masks]
    gathered = [(held, masks)]
    if pix_count > 2:
        gathered.append((lax.ppermute(held, "pix", swap(2)), [2 ^ m for m in masks]))

    current = None
    movies = []
    for c, width in enumerate(widths):
        pair = (None, None)
        calls = 1
        for part in range(calls):
            groups = width // calls
            skip = part * groups
            current, *pair = diffuse_call(
                flags, raw_movie, *halos[c], current, pair,
                sum(widths[:c]) + skip, skip, width * LANES, skip, groups,
            )
        movies.append(tuple(array.reshape(pixel_count, width * LANES) for array in pair))

    foot, gram = footprints_call(scalars, footprints, entries)
    keep, send = numerator_call(scalars, foot, movies, gram, trace_rows)
    arrived = lax.ppermute(send, "pix", swap(1))
    parts = []
    for k in range(1, keep.shape[0]):
        parts.append(lax.ppermute(keep[k] + arrived[k], "pix", swap(2 * k)))
    new_traces, again = traces_call(scalars, keep, arrived, parts, gathered)
    near = [again]
    for k in range(1, keep.shape[0]):
        near.append(lax.ppermute(again, "pix", swap(2 * k)))
    far = []
    for piece in near:
        far.append(lax.ppermute(piece, "pix", swap(1)))

    products = []
    for h in range(HALVES):
        products.append(products_call(scalars, near, far, movies, h, count, scatter_places(count), h == 0))
    sums = [line_scatter(blocks, "tm", count) for blocks in products]
    part = pixel_count // HALVES
    gram_mine = sum(array[:, part:] for array in sums[0])
    gram_other = lax.ppermute(gram_mine, "pix", swap(1))
    new_footprints, below = first_final_call(scalars, footprints, foot, sums[0], gram_mine, gram_other)
    new_footprints = second_final_call(footprints, sums[1], below, new_footprints)
    return current, new_footprints, new_traces


def solution(mesh):
    placed = (P("pix", None, "tm"), P("tm", "pix"), P("pix", "tm"))
    return jax.shard_map(
        compute,
        mesh=mesh,
        in_specs=placed,
        out_specs=(P("pix", None, "tm"), P("tm", "pix"), P("pix", "tm")),
        check_vma=False,
    )
```
